32 devices in a mesh: grp: 2 (over x), row: 16 (over z, y, core).
Axes of the slice: x: 2, y: 2, z: 4, core: 2. Of those that a mesh axis runs over, the one named last changes fastest.
Arguments:
- positions: float32 [3, 12288], P(None, ('grp', 'row')), parts along dimension 1, may hold values from -6 to 6
- noise: float32 [3, 12288], P(None, ('grp', 'row')), parts along dimension 1, may hold values from -6 to 6
- atom_single: bfloat16 [12288, 128], P(('grp', 'row')), parts along dimension 0, may hold values from -6 to 6
- atom_token: int32 [12288], P(('grp', 'row')), parts along dimension 0, may hold values from 0 to 511, as said below
- atom_counts: int32 [32], P(('grp', 'row')), parts along dimension 0, may hold values from 192 to 384, as said below
- window_offsets: int32 [384], P(('grp', 'row')), parts along dimension 0, may hold values from -64 to -32
- atom_bias: float32 [4, 12288, 128], P(None, ('grp', 'row')), parts along dimension 1, may hold values from -4 to 302
- token_single: bfloat16 [1024, 768], P(('grp', 'row')), parts along dimension 0, may hold values from -6 to 6
- token_bias: float32 [16, 1024, 512], P(None, ('grp', 'row')), parts along dimension 1, may hold values from -9 to 302
- pair_mask: int32 [1024, 512], P(('grp', 'row')), parts along dimension 0, may hold values from 0 to 1, as said below
- w_coord: float32 [3, 128], replicated, may hold values from -3.5 to 3.5
- w_atom_qkv: bfloat16 [128, 384], replicated, may hold values from -0.5 to 0.5
- w_atom_out: bfloat16 [128, 128], replicated, may hold values from -0.5 to 0.5
- w_agg: bfloat16 [128, 768], replicated, may hold values from -0.5 to 0.5
- w_tok_qkv: bfloat16 [768, 2304], replicated, may hold values from -0.21875 to 0.21875
- w_tok_gate: bfloat16 [768, 768], replicated, may hold values from -0.21875 to 0.21875
- w_tok_out: bfloat16 [768, 768], replicated, may hold values from -0.21875 to 0.21875
- w_back: bfloat16 [768, 128], replicated, may hold values from -0.21875 to 0.21875
- w_pos: bfloat16 [3, 128], replicated, may hold values from -0.5 to 0.5
Outputs:
- denoised: float32 [3, 12288], P(None, ('grp', 'row')), parts along dimension 1
- token_out: bfloat16 [1024, 768], P(('grp', 'row')), parts along dimension 0
The draws below stay inside these ranges and needn't reach their ends.
There are 2 independent parts, one for each index of `grp`. The reference program is written for one: setup_inputs(seed, part) draws one part's arguments, and reference() takes and returns one part's arrays. A program takes and returns all parts, laid end to end along the dimension named above; an argument that names none is the same for every part. Nothing has to cross between parts.
Inputs may be any that keep to these rules, and one draw needn't show every extreme that they name: `atom_token`: slots i * 384 to (i + 1) * 384 - 1 name tokens from i * 32 - 32 // 4 to (i + 1) * 32 + 32 // 4; ids never fall along the slots. `atom_counts`: entry i is the number of live slots at the front of slots i * 384 onward; some entry equals 384. `pair_mask`: each token's own column, and the column of its index xor 1, are 1.
All inputs are finite; a program needn't handle non-finite values.
Results may differ from the reference program's by a relative error of at most 0.0075.
Values may be sent and summed in bfloat16 or wider, within the bound.
A program may use at most 64 MiB of HBM per device.

```python
import jax
import jax.numpy as jnp
from jax import lax

CA = 128
AH = 4
CT = 768
TH = 16
QWIN = 32
KWIN = 128
TOKQ = 32
ACAP = 384
TOKENS = 512
ATOMS = 6144
WINS = 192
N_ROW = 16


def shared_counts(key):
    inner = jax.random.fold_in(key, 11)
    first_key, second_key = jax.random.split(inner)
    counts = jax.random.randint(first_key, (N_ROW,), ACAP // 2, ACAP + 1)
    fullest = jax.random.randint(second_key, (), 0, N_ROW)
    return jnp.where(jnp.arange(N_ROW) == fullest, ACAP, counts).astype(jnp.int32)


def draw_atom_counts(key, part):
    return shared_counts(key)


def draw_atom_token(key, part):
    counts = shared_counts(key)
    inner = jax.random.fold_in(key, 12)
    first_key, second_key, third_key = jax.random.split(inner, 3)
    margin = TOKQ // 4
    jitter = jax.random.randint(first_key, (N_ROW + 1,), -margin, margin + 1)
    bounds = jnp.arange(N_ROW + 1) * TOKQ + jitter
    bounds = bounds.at[0].set(0)
    bounds = bounds.at[N_ROW].set(TOKENS - 1)
    bounds = jnp.clip(bounds, 0, TOKENS - 1)
    lower = bounds[:-1]
    upper = bounds[1:]
    raw_ids = jax.random.randint(second_key, (N_ROW, ACAP), 0, 1 << 20)
    picked = lower[:, None] + raw_ids % (upper - lower + 1)[:, None]
    ordered = jnp.sort(picked, axis=1)
    slot_ids = jnp.arange(ACAP)
    chosen = jnp.minimum(slot_ids[None, :] * ACAP // counts[:, None], ACAP - 1)
    live_ids = jnp.take_along_axis(ordered, chosen, axis=1)
    hole_raw = jax.random.randint(third_key, (N_ROW,), 0, 1 << 20)
    hole = lower + 1 + hole_raw % jnp.maximum(upper - lower - 2, 1)
    live_ids = jnp.where(live_ids == hole[:, None], hole[:, None] + 1, live_ids)
    result = jnp.where(slot_ids[None, :] < counts[:, None], live_ids, upper[:, None])
    return result.reshape(-1).astype(jnp.int32)


def draw_atom_bias(key, part):
    inner = jax.random.fold_in(key, 21)
    first_key = jax.random.fold_in(inner, 0)
    return jnp.clip(jax.random.normal(first_key, (AH, ATOMS, KWIN)), -4.0, 4.0).astype(jnp.float32)


def draw_token_bias(key, part):
    inner = jax.random.fold_in(key, 22)
    first_key = jax.random.fold_in(inner, 0)
    return jnp.clip(3.0 * jax.random.normal(first_key, (TH, TOKENS, TOKENS)), -9.0, 9.0).astype(jnp.float32)


def draw_pair_mask(key, part):
    inner = jax.random.fold_in(key, 31)
    coins = jax.random.randint(inner, (TOKENS, TOKENS), 0, 4) != 0
    row_ids = jnp.arange(TOKENS)[:, None]
    col_ids = jnp.arange(TOKENS)[None, :]
    keep = coins | (col_ids == row_ids) | (col_ids == row_ids ^ 1)
    return keep.astype(jnp.int32)


def plant(array, own_key, smallest, largest):
    index_at = [jax.random.randint(jax.random.fold_in(own_key, axis), (), 0, length) for axis, length in enumerate(array.shape)]
    longest = array.shape.index(max(array.shape))
    beside = index_at[:longest] + [(index_at[longest] + 1) % array.shape[longest]] + index_at[longest + 1:]
    return array.at[tuple(index_at)].set(smallest).at[tuple(beside)].set(largest)


def steps_of(own_key, dims, cuts, least, top_value):
    def one(axis_at, shards_of):
        heights = jax.random.uniform(jax.random.fold_in(jax.random.fold_in(own_key, 6), axis_at), (shards_of,), jnp.float32, least / len(cuts), top_value / len(cuts))
        return jnp.repeat(jnp.exp(heights), dims[axis_at] // shards_of).reshape((-1,) + (1,) * (len(dims) - axis_at - 1))

    factor_of = one(*cuts[0])
    for cut in cuts[1:]:
        factor_of = factor_of * one(*cut)
    return factor_of


def bell_draw(rng, extent, deviation, reach, cuts=(), kind=jnp.bfloat16):
    loudness = steps_of(rng, extent, cuts, -0.22, 0.18) if cuts else 1.0
    values = jax.random.normal(rng, extent, jnp.float32) * deviation * loudness
    return jnp.minimum(jnp.maximum(values, -reach), reach).astype(kind)


def setup_inputs(seed: int = 0, part: int = 0) -> dict:
    seeds = jax.random.split(jax.random.key(seed), 20)
    part_splits = jax.random.split(jax.random.fold_in(seeds[19], part), 20)
    return {
        "positions": bell_draw(part_splits[0], (3, ATOMS), 1.0, 6.0, ((1, 16),), jnp.float32),
        "noise": bell_draw(part_splits[1], (3, ATOMS), 1.0, 6.0, ((1, 16),), jnp.float32),
        "atom_single": bell_draw(part_splits[2], (ATOMS, CA), 1.0, 6.0, ((0, 16),)),
        "atom_token": draw_atom_token(jax.random.fold_in(jax.random.fold_in(seeds[19], part), 71), part),
        "atom_counts": draw_atom_counts(jax.random.fold_in(jax.random.fold_in(seeds[19], part), 71), part),
        "window_offsets": plant(jax.random.randint(part_splits[5], (WINS,), -(KWIN // 2), 1 - QWIN), jax.random.fold_in(part_splits[5], 1), -(KWIN // 2), (1 - QWIN) - 1).astype(jnp.int32),
        "atom_bias": draw_atom_bias(jax.random.fold_in(jax.random.fold_in(seeds[19], part), 71), part),
        "token_single": bell_draw(part_splits[7], (TOKENS, CT), 1.0, 6.0, ((0, 16),)),
        "token_bias": draw_token_bias(jax.random.fold_in(jax.random.fold_in(seeds[19], part), 71), part),
        "pair_mask": draw_pair_mask(jax.random.fold_in(jax.random.fold_in(seeds[19], part), 71), part),
        "w_coord": bell_draw(seeds[10], (3, CA), 3 ** -0.5, 3.5, (), jnp.float32),
        "w_atom_qkv": bell_draw(seeds[11], (CA, 3 * CA), CA ** -0.5, 0.5),
        "w_atom_out": bell_draw(seeds[12], (CA, CA), CA ** -0.5, 0.5),
        "w_agg": bell_draw(seeds[13], (CA, CT), CA ** -0.5, 0.5),
        "w_tok_qkv": bell_draw(seeds[14], (CT, 3 * CT), CT ** -0.5, 0.21875),
        "w_tok_gate": bell_draw(seeds[15], (CT, CT), CT ** -0.5, 0.21875),
        "w_tok_out": bell_draw(seeds[16], (CT, CT), CT ** -0.5, 0.21875),
        "w_back": bell_draw(seeds[17], (CT, CA), CT ** -0.5, 0.21875),
        "w_pos": bell_draw(seeds[18], (3, CA), CA ** -0.5, 0.5),
    }


noise_level = 2.0
input_scale = 1.0 / 5.0 ** 0.5
skip_scale = 1.0 / 5.0
output_scale = 2.0 / 5.0 ** 0.5
masked_score = -1e+30

def normalize(values):
    values = values.astype(jnp.float32)
    center = values - lax.optimization_barrier(jnp.mean(values, axis=-1, keepdims=True))
    spread = lax.optimization_barrier(jnp.mean(center * center, axis=-1, keepdims=True))
    return center * lax.rsqrt(spread + 1e-05)

def reference(positions, noise, atom_single, atom_token, atom_counts, window_offsets, atom_bias, token_single, token_bias, pair_mask, w_coord, w_atom_qkv, w_atom_out, w_agg, w_tok_qkv, w_tok_gate, w_tok_out, w_back, w_pos):
    noisy_coords = positions + noise_level * noise
    atom_start = atom_single.astype(jnp.float32) + lax.dot_general(input_scale * noisy_coords, w_coord, (((0,), (0,)), ((), ())), precision=lax.Precision.HIGHEST, preferred_element_type=jnp.float32)
    slot_ids = jnp.arange(ACAP, dtype=jnp.int32)
    living = (slot_ids[None, :] < atom_counts[:, None]).reshape(-1)
    starts = (jnp.cumsum(atom_counts) - atom_counts).astype(jnp.int32)
    total_atoms = jnp.sum(atom_counts).astype(jnp.int32)
    sequence_index = jnp.where(living, (starts[:, None] + slot_ids[None, :]).reshape(-1), ATOMS).astype(jnp.int32)
    normed = normalize(atom_start).astype(jnp.bfloat16)
    projected = jnp.dot(normed, w_atom_qkv, preferred_element_type=jnp.float32).astype(jnp.bfloat16)
    queries = projected[:, :CA]
    key_vals = projected[:, CA:]
    compact = jnp.zeros((ATOMS, 2 * CA), jnp.bfloat16).at[sequence_index].set(key_vals, mode='drop')
    windows = ATOMS // QWIN
    per_window = ACAP // QWIN
    window_ids = jnp.arange(windows, dtype=jnp.int32)
    window_first = starts[window_ids // per_window] + QWIN * (window_ids % per_window)
    key_index = window_first[:, None] + window_offsets[:, None] + jnp.arange(KWIN, dtype=jnp.int32)[None, :]
    key_usable = (key_index >= 0) & (key_index < total_atoms)
    clipped = jnp.clip(key_index, 0, ATOMS - 1).astype(jnp.int32)
    window_kv = compact[clipped]
    head_width = CA // AH
    query_heads = queries.reshape(windows, QWIN, AH, head_width).astype(jnp.float32)
    key_heads = window_kv[..., :CA].reshape(windows, KWIN, AH, head_width).astype(jnp.float32)
    value_heads = window_kv[..., CA:].reshape(windows, KWIN, AH, head_width).astype(jnp.float32)
    scores = jnp.einsum('wqhd,wkhd->hwqk', query_heads, key_heads) / head_width ** 0.5 + atom_bias.reshape(AH, windows, QWIN, KWIN)
    scores = jnp.where(key_usable[None, :, None, :], scores, masked_score)
    weights = jax.nn.softmax(scores, axis=-1).astype(jnp.bfloat16)
    attended = jnp.einsum('hwqk,wkhd->wqhd', weights.astype(jnp.float32), value_heads).reshape(ATOMS, CA)
    atom_mid = atom_start + jnp.dot(attended.astype(jnp.bfloat16), w_atom_out, preferred_element_type=jnp.float32)
    spread_rows = jnp.maximum(jnp.dot(atom_mid.astype(jnp.bfloat16), w_agg, preferred_element_type=jnp.float32), 0.0).astype(jnp.bfloat16)
    live_rows = jnp.where(living[:, None], spread_rows.astype(jnp.float32), 0.0)
    token_sum = jax.ops.segment_sum(live_rows, atom_token, num_segments=TOKENS)
    token_count = jax.ops.segment_sum(living.astype(jnp.float32), atom_token, num_segments=TOKENS)
    token_in = token_single.astype(jnp.float32) + token_sum / jnp.maximum(token_count, 1.0)[:, None]
    token_norm = normalize(token_in).astype(jnp.bfloat16)
    token_proj = jnp.dot(token_norm, w_tok_qkv, preferred_element_type=jnp.float32).astype(jnp.bfloat16)
    token_head = CT // TH
    head_query = token_proj[:, :CT].reshape(TOKENS, TH, token_head).transpose(1, 0, 2)
    head_key = token_proj[:, CT:2 * CT].reshape(TOKENS, TH, token_head).transpose(1, 0, 2)
    head_value = token_proj[:, 2 * CT:].reshape(TOKENS, TH, token_head).transpose(1, 0, 2)

    def attend(head_items):
        one_query, one_key, one_value, one_bias = head_items
        head_scores = jnp.dot(one_query, one_key.T, preferred_element_type=jnp.float32) / token_head ** 0.5 + one_bias
        head_scores = jnp.where(pair_mask == 1, head_scores, masked_score)
        head_weights = jax.nn.softmax(head_scores, axis=-1).astype(jnp.bfloat16)
        return jnp.dot(head_weights, one_value, preferred_element_type=jnp.float32)
    token_att = lax.map(attend, (head_query, head_key, head_value, token_bias)).transpose(1, 0, 2).reshape(TOKENS, CT)
    gating = jax.nn.sigmoid(jnp.dot(token_norm, w_tok_gate, preferred_element_type=jnp.float32))
    gated = (gating * token_att).astype(jnp.bfloat16)
    token_out = (token_in + jnp.dot(gated, w_tok_out, preferred_element_type=jnp.float32)).astype(jnp.bfloat16)
    back_rows = jnp.dot(token_out, w_back, preferred_element_type=jnp.float32).astype(jnp.bfloat16)
    atom_last = atom_mid + back_rows[atom_token].astype(jnp.float32)
    final_norm = normalize(atom_last).astype(jnp.bfloat16)
    update = lax.dot_general(w_pos, final_norm, (((1,), (1,)), ((), ())), preferred_element_type=jnp.float32)
    denoised = jnp.where(living[None, :], skip_scale * noisy_coords + output_scale * update, 0.0)
    return (denoised, token_out)
```

```python
import jax
import jax.numpy as jnp
from jax import lax
from jax.experimental import pallas as pl
from jax.experimental.pallas import tpu as pltpu
from jax.sharding import PartitionSpec as P

AH = 4
TH = 16
QWIN = 32
KWIN = 128
BEHIND = KWIN // 2
AHEAD = KWIN - QWIN

noise_level = 2.0
input_scale = 1.0 / 5.0**0.5
skip_scale = 1.0 / 5.0
output_scale = 2.0 / 5.0**0.5
masked_score = -1e30

F32 = jnp.float32
BF16 = jnp.bfloat16
PIECES = 2
VMEM_LIMIT = 40 * 1024 * 1024


def normalize(values):
    center = values - jnp.mean(values, axis=-1, keepdims=True)
    spread = jnp.mean(center * center, axis=-1, keepdims=True)
    return center * lax.rsqrt(spread + 1e-05)


def mm(a, b):
    return jnp.dot(a, b, preferred_element_type=F32)


def mm_t(a, b):
    return lax.dot_general(a, b, (((1,), (1,)), ((), ())), preferred_element_type=F32)


def lanes_between(width, low, high):
    lane = lax.broadcasted_iota(jnp.int32, (1, width), 1)
    return ((lane >= low) & (lane < high)).astype(F32)


def kernel(
    n,
    counts_s, offsets_h,
    pos_h, noise_h, single_h, token_h, abias_h, tsingle_h, tbias_h, mask_h,
    wcoord_h, waqkv_h, waout_h, wagg_h, wtqkv_h, wgate_h, wtout_h, wback_h, wpos_h,
    den_ref, tout_ref,
    offsets_s,
    pos, noise, single, token, abias, tsingle, tbias, pmask,
    wcoord, waqkv, waout, wagg, wtqkv, wgate, wtout, wback, wpos,
    columns, hs, tail, head, lo, up, shifted, ext, keys_s, values_s, mid, att_s,
    part_down, part_up, from_low, from_high, u_all, near,
    local_sem, edge_send, edge_recv, line_send, ag_send, ag_recv,
):
    cap, ca = single.shape
    rows, ct = tsingle.shape
    me = lax.axis_index("row")
    last = n - 1
    has_low = me > 0
    has_high = me < last

    pairs = [
        (pos_h, pos), (noise_h, noise), (single_h, single), (wcoord_h, wcoord), (token_h, token),
        (waqkv_h, waqkv), (abias_h, abias), (waout_h, waout), (wagg_h, wagg), (tsingle_h, tsingle),
        (wtqkv_h, wtqkv), (wgate_h, wgate), (mask_h, pmask), (tbias_h, tbias), (wtout_h, wtout),
        (wback_h, wback), (wpos_h, wpos), (offsets_h, offsets_s),
    ]
    copies = {}
    for k, (src, dst) in enumerate(pairs):
        copies[id(dst)] = pltpu.make_async_copy(src, dst, local_sem.at[k])
        copies[id(dst)].start()

    def need(*refs):
        for r in refs:
            copies[id(r)].wait()

    core = lax.rem(me, 2)
    y = lax.rem(me // 2, 2)
    z = me // 4
    depth = n // 4

    def index_of(zz, yy, cc):
        return zz * 4 + yy * 2 + cc

    partner = index_of(z, y, 1 - core)
    across = index_of(z, 1 - y, core)
    line = []
    for d in range(1, depth):
        line.append((z + d < depth, index_of(z + d, y, core), 2 * d))
        line.append((z >= d, index_of(z - d, y, core), 2 * d + 1))

    barrier = pltpu.get_barrier_semaphore()

    def greet(peer):
        pl.semaphore_signal(
            barrier, inc=1, device_id={"row": peer}, device_id_type=pl.DeviceIdType.MESH
        )

    greet(partner)
    greet(across)
    for there, peer, _ in line:
        pl.when(there)(lambda peer=peer: greet(peer))
    far = me - 1 + 2 * core
    has_far = (far >= 0) & (far < n)
    pl.when(has_far)(lambda: greet(far))

    shifted[...] = jnp.zeros_like(shifted)
    columns[...] = jnp.zeros_like(columns)
    near[...] = jnp.zeros_like(near)

    @pl.when(me == 0)
    def _():
        lo[...] = jnp.zeros_like(lo)
        from_low[...] = jnp.zeros_like(from_low)

    @pl.when(me == last)
    def _():
        up[...] = jnp.zeros_like(up)
        from_high[...] = jnp.zeros_like(from_high)

    need(pos, noise, single, wcoord, token)
    live = jnp.clip(counts_s[0], cap // 2, cap)
    noisy = pos[...] + noise_level * noise[...]
    columns[0:3, :] = input_scale * noisy
    relative = token[...].reshape(1, cap) - (me - 1) * rows
    columns[3:4, :] = relative.astype(F32)
    turned = columns[...].T
    wc = wcoord[...]
    atom_start = single[...].astype(F32) + (
        turned[:, 0:1] * wc[0:1, :] + turned[:, 1:2] * wc[1:2, :] + turned[:, 2:3] * wc[2:3, :]
    )
    near_rows = near.shape[0]
    lane_ids = lax.broadcasted_iota(jnp.int32, (cap, near_rows), 1).astype(F32)
    hot_t = (turned[:, 3:4] == lane_ids).astype(F32).astype(BF16)
    normed = normalize(atom_start)
    hs[...] = normed
    mid[...] = atom_start
    head[...] = normed[:AHEAD].astype(BF16)
    tail[...] = hs[pl.ds(live - BEHIND, BEHIND), :].astype(BF16)

    peers = 2 + (depth - 1) + jnp.where(has_far, 1, 0)
    pl.semaphore_wait(barrier, peers)

    def edge(k, src, dst, peer):
        return pltpu.make_async_remote_copy(
            src_ref=src,
            dst_ref=dst,
            send_sem=edge_send.at[k],
            recv_sem=edge_recv.at[k],
            device_id={"row": peer},
            device_id_type=pl.DeviceIdType.MESH,
        )

    def exchange(stage, src_up, dst_up, src_down, dst_down):
        going_up = edge(2 * stage, src_up, dst_up, me + 1)
        going_down = edge(2 * stage + 1, src_down, dst_down, me - 1)
        pl.when(has_high)(going_up.start)
        pl.when(has_low)(going_down.start)

        def receive():
            pl.when(has_low)(going_up.wait_recv)
            pl.when(has_high)(going_down.wait_recv)

        def finish():
            pl.when(has_high)(going_up.wait_send)
            pl.when(has_low)(going_down.wait_send)

        return receive, finish

    receive_rim, finish_rim = exchange(0, tail, lo, head, up)

    need(waqkv)
    queries = mm(normed.astype(BF16), waqkv[:, :ca]).astype(BF16)
    hw = ca // AH
    head_lanes = [lanes_between(ca, h * hw, (h + 1) * hw) for h in range(AH)]
    ext[BEHIND : BEHIND + cap, :] = normed
    need(abias, offsets_s)

    receive_rim()
    ext[:BEHIND, :] = lo[...].astype(F32)
    half = cap // 2
    shifted[half : half + AHEAD, :] = up[...].astype(F32)
    first = BEHIND + half
    count = half + AHEAD
    moved = shifted[pl.ds(cap - live, count), :]
    row_ids = lax.broadcasted_iota(jnp.int32, (count, ca), 0) + first
    ext[first : BEHIND + cap, :] = jnp.where(
        row_ids[:half] < BEHIND + live, ext[first : BEHIND + cap, :], moved[:half]
    )
    ext[BEHIND + cap :, :] = moved[half:]
    kv_rows = mm(ext[...].astype(BF16), waqkv[:, ca:]).astype(BF16).astype(F32)
    keys_s[...] = kv_rows[:, :ca]
    values_s[...] = kv_rows[:, ca:]

    top = jnp.where(has_high, BEHIND + live + AHEAD, BEHIND + live)
    bottom = jnp.where(has_low, 0, BEHIND)
    lane_key = lax.broadcasted_iota(jnp.int32, (1, KWIN), 1)
    for w in range(cap // QWIN):
        at = BEHIND + QWIN * w + offsets_s[w]
        key = keys_s[pl.ds(at, KWIN), :].astype(BF16)
        value = values_s[pl.ds(at, KWIN), :].astype(BF16)
        q = queries[w * QWIN : (w + 1) * QWIN, :]
        wide = jnp.concatenate([q * m.astype(BF16) for m in head_lanes], axis=0)
        score = mm_t(wide, key) * (1.0 / hw**0.5)
        score = score + abias[:, w * QWIN : (w + 1) * QWIN, :].reshape(AH * QWIN, KWIN)
        keys = lane_key + at
        score = jnp.where((keys >= bottom) & (keys < top), score, masked_score)
        e = jnp.exp(score - jnp.max(score, axis=-1, keepdims=True))
        weights = (e / jnp.sum(e, axis=-1, keepdims=True)).astype(BF16)
        out = mm(weights, value)
        total = out[:QWIN] * head_lanes[0]
        for h in range(1, AH):
            total = total + out[h * QWIN : (h + 1) * QWIN] * head_lanes[h]
        att_s[w * QWIN : (w + 1) * QWIN, :] = total.astype(BF16)

    need(waout, wagg)
    atom_mid = mid[...] + mm(att_s[...], waout[...])
    mid[...] = atom_mid
    spread = jnp.maximum(mm(atom_mid.astype(BF16), wagg[...]), 0.0).astype(BF16)
    slot_lane = lax.broadcasted_iota(jnp.int32, (1, cap), 1)
    living = slot_lane < live
    sub_ids = lax.broadcasted_iota(jnp.int32, (3 * rows, cap), 0)
    hot = ((sub_ids == relative) & living).astype(F32)
    counted = jnp.sum(hot, axis=-1, keepdims=True)
    partial = mm(hot.astype(BF16), spread)
    few = jnp.minimum(counted, 256.0)
    lane_c = lax.broadcasted_iota(jnp.int32, (3 * rows, 128), 1)
    count_wide = jnp.where(lane_c < 64, few, counted - few)
    part_down[:, :ct] = partial[:rows].astype(BF16)
    part_down[:, ct:] = count_wide[:rows].astype(BF16)
    part_up[:, :ct] = partial[2 * rows :].astype(BF16)
    part_up[:, ct:] = count_wide[2 * rows :].astype(BF16)
    receive_part, finish_part = exchange(1, part_up, from_low, part_down, from_high)

    need(tsingle, wtqkv, wgate)
    receive_part()
    low = from_low[...].astype(F32)
    high = from_high[...].astype(F32)
    token_sum = partial[rows : 2 * rows] + high[:, :ct] + low[:, :ct]
    token_count = (
        counted[rows : 2 * rows]
        + (high[:, ct : ct + 1] + high[:, ct + 64 : ct + 65])
        + (low[:, ct : ct + 1] + low[:, ct + 64 : ct + 65])
    )
    token_in = tsingle[...].astype(F32) + token_sum / jnp.maximum(token_count, 1.0)
    u = normalize(token_in).astype(BF16)
    u_all[pl.ds(pl.multiple_of(me * rows, rows), rows), :] = u

    part = rows // PIECES

    def block(src, piece, peer, sent):
        view = u_all.at[pl.ds(pl.multiple_of(src * rows + piece * part, part), part), :]
        return pltpu.make_async_remote_copy(
            src_ref=view,
            dst_ref=view,
            send_sem=sent,
            recv_sem=ag_recv.at[src, piece],
            device_id={"row": peer},
            device_id_type=pl.DeviceIdType.MESH,
        )

    def relay(src, piece, over, act):
        if over:
            act(block(src, piece, across, ag_send.at[0, src, piece]))
        act(block(src, piece, partner, ag_send.at[1, src, piece]))

    def own_sends(act):
        for piece in range(PIECES):
            relay(me, piece, True, act)
            for there, peer, way in line:
                pl.when(there)(lambda piece=piece, peer=peer, way=way: act(block(me, piece, peer, line_send.at[way, piece])))

    def start(c):
        c.start()

    def end(c):
        c.wait_send()

    steps = []
    for d in range(1, depth + 1):
        if d < depth:
            steps.append((z >= d, index_of(z - d, y, core), True))
            steps.append((z + d < depth, index_of(z + d, y, core), True))
        if d == 1:
            steps.append((None, across, False))
        else:
            steps.append((z >= d - 1, index_of(z - d + 1, 1 - y, core), False))
            steps.append((z + d - 1 < depth, index_of(z + d - 1, 1 - y, core), False))

    own_sends(start)

    tw = ct // TH
    group = TH // 2
    gw = group * tw
    tquery = mm(u, wtqkv[:, :ct]).astype(BF16)
    through = []
    group_lanes = [lanes_between(gw, h * tw, (h + 1) * tw) for h in range(group)]
    for g in range(2):
        q = tquery[:, g * gw : (g + 1) * gw]
        wide = jnp.concatenate([q * m.astype(BF16) for m in group_lanes], axis=0)
        through.append(mm_t(wide, wtqkv[:, ct + g * gw : ct + (g + 1) * gw]).astype(BF16))
    gate = jax.nn.sigmoid(mm(u, wgate[...]))

    def arrive(src, over):
        for piece in range(PIECES):
            block(src, piece, partner, ag_send.at[1, 0, piece]).wait_recv()
            relay(src, piece, over, start)

    def leave(src, over):
        for piece in range(PIECES):
            relay(src, piece, over, end)

    def each(visit):
        for there, src, over in steps:
            if there is None:
                visit(src, over)
            else:
                pl.when(there)(lambda src=src, over=over: visit(src, over))

    each(arrive)
    for zz in range(depth):
        for yy in range(2):
            for piece in range(PIECES):
                block(index_of(zz, yy, 1 - core), piece, partner, ag_send.at[1, 0, piece]).wait_recv()

    need(pmask, tbias, wtout, wback, wpos)
    features = u_all[...]
    allowed = (pmask[...] == 1)[None]
    pieces = []
    for g in range(2):
        score = mm_t(through[g], features) * (1.0 / tw**0.5)
        score = score.reshape(group, rows, score.shape[-1]) + tbias[g * group : (g + 1) * group]
        score = jnp.where(allowed, score, masked_score)
        e = jnp.exp(score - jnp.max(score, axis=-1, keepdims=True))
        weights = (e / jnp.sum(e, axis=-1, keepdims=True)).astype(BF16)
        mixed = mm(weights.reshape(group * rows, -1), features).astype(BF16)
        out = mm(mixed, wtqkv[:, 2 * ct + g * gw : 2 * ct + (g + 1) * gw])
        total = out[:rows] * group_lanes[0]
        for h in range(1, group):
            total = total + out[h * rows : (h + 1) * rows] * group_lanes[h]
        pieces.append(total)
    gated = (gate * jnp.concatenate(pieces, axis=1)).astype(BF16)
    token_out = (token_in + mm(gated, wtout[...])).astype(BF16)
    tout_ref[...] = token_out
    near[rows : 2 * rows, :] = mm(token_out, wback[...]).astype(BF16)
    own = near.at[rows : 2 * rows]
    receive_back, finish_back = exchange(
        2, own, near.at[0:rows], own, near.at[2 * rows : 3 * rows]
    )
    finish_rim()
    finish_part()
    own_sends(end)
    each(leave)
    receive_back()
    atom_last = mid[...] + mm(hot_t, near[...])
    final = normalize(atom_last).astype(BF16)
    update = mm_t(wpos[...], final)
    den_ref[...] = jnp.where(living, skip_scale * noisy + output_scale * update, 0.0)
    finish_back()


def store(den, tout, den_h, tout_h, sem):
    copies = [pltpu.make_async_copy(den, den_h, sem.at[0]), pltpu.make_async_copy(tout, tout_h, sem.at[1])]
    for c in copies:
        c.start()
    for c in copies:
        c.wait()


def on_device(
    positions, noise, atom_single, atom_token, atom_counts, window_offsets, atom_bias,
    token_single, token_bias, pair_mask, w_coord, w_atom_qkv, w_atom_out, w_agg,
    w_tok_qkv, w_tok_gate, w_tok_out, w_back, w_pos,
):
    n = lax.axis_size("row")
    cap, ca = atom_single.shape
    rows, ct = token_single.shape
    big = (
        positions, noise, atom_single, atom_token, atom_bias, token_single,
        token_bias, pair_mask, w_coord, w_atom_qkv, w_atom_out, w_agg, w_tok_qkv, w_tok_gate,
        w_tok_out, w_back, w_pos,
    )
    near_rows = -(-3 * rows // 128) * 128
    hbm = pl.BlockSpec(memory_space=pltpu.HBM)
    vmem = pl.BlockSpec(memory_space=pltpu.VMEM)
    out_shapes = (((positions.shape[0], cap), F32), ((rows, ct), BF16))
    results = pl.pallas_call(
        lambda *refs: kernel(n, *refs),
        out_shape=tuple(pltpu.VMEM(shape, kind) for shape, kind in out_shapes),
        in_specs=[pl.BlockSpec(memory_space=pltpu.SMEM)] + [hbm] * (1 + len(big)),
        out_specs=(vmem, vmem),
        scratch_shapes=[pltpu.SMEM(window_offsets.shape, jnp.int32)]
        + [pltpu.VMEM(a.shape, a.dtype) for a in big]
        + [
            pltpu.VMEM((128, cap), F32),
            pltpu.VMEM((cap, ca), F32),
            pltpu.VMEM((BEHIND, ca), BF16),
            pltpu.VMEM((AHEAD, ca), BF16),
            pltpu.VMEM((BEHIND, ca), BF16),
            pltpu.VMEM((AHEAD, ca), BF16),
            pltpu.VMEM((cap + AHEAD, ca), F32),
            pltpu.VMEM((BEHIND + cap + AHEAD, ca), F32),
            pltpu.VMEM((BEHIND + cap + AHEAD, ca), F32),
            pltpu.VMEM((BEHIND + cap + AHEAD, ca), F32),
            pltpu.VMEM((cap, ca), F32),
            pltpu.VMEM((cap, ca), BF16),
            pltpu.VMEM((rows, ct + 128), BF16),
            pltpu.VMEM((rows, ct + 128), BF16),
            pltpu.VMEM((rows, ct + 128), BF16),
            pltpu.VMEM((rows, ct + 128), BF16),
            pltpu.VMEM((n * rows, ct), BF16),
            pltpu.VMEM((near_rows, ca), BF16),
            pltpu.SemaphoreType.DMA((1 + len(big),)),
            pltpu.SemaphoreType.DMA((6,)),
            pltpu.SemaphoreType.DMA((6,)),
            pltpu.SemaphoreType.DMA((n // 2, PIECES)),
            pltpu.SemaphoreType.DMA((2, n, PIECES)),
            pltpu.SemaphoreType.DMA((n, PIECES)),
        ],
        compiler_params=pltpu.CompilerParams(collective_id=0, has_side_effects=True, vmem_limit_bytes=VMEM_LIMIT),
    )(atom_counts, *(pltpu.with_memory_space_constraint(a, pltpu.HBM) for a in (window_offsets,) + big))
    results = tuple(pltpu.with_memory_space_constraint(a, pltpu.VMEM) for a in results)
    return pl.pallas_call(
        store,
        out_shape=tuple(jax.ShapeDtypeStruct(shape, kind) for shape, kind in out_shapes),
        in_specs=[vmem, vmem],
        out_specs=(hbm, hbm),
        scratch_shapes=[pltpu.SemaphoreType.DMA((2,))],
    )(*results)


def solution(mesh):
    placed = (
        P(None, ("grp", "row")),
        P(None, ("grp", "row")),
        P(("grp", "row"), None),
        P(("grp", "row")),
        P(("grp", "row")),
        P(("grp", "row")),
        P(None, ("grp", "row"), None),
        P(("grp", "row"), None),
        P(None, ("grp", "row"), None),
        P(("grp", "row"), None),
    ) + (P(),) * 9
    return jax.shard_map(
        on_device,
        mesh=mesh,
        in_specs=placed,
        out_specs=(P(None, ("grp", "row")), P(("grp", "row"), None)),
        check_vma=False,
    )
```

```python
import jax
import jax.numpy as jnp
from jax import lax
from jax.experimental import pallas as pl
from jax.experimental.pallas import tpu as pltpu
from jax.sharding import PartitionSpec as P

AH = 4
TH = 16
QWIN = 32
KWIN = 128
BEHIND = KWIN // 2
AHEAD = KWIN - QWIN

noise_level = 2.0
input_scale = 1.0 / 5.0**0.5
skip_scale = 1.0 / 5.0
output_scale = 2.0 / 5.0**0.5
masked_score = -1e30

F32 = jnp.float32
BF16 = jnp.bfloat16
PIECES = 2
GROUP = 5
VMEM_LIMIT = 40 * 1024 * 1024


def normalize(values):
    center = values - jnp.mean(values, axis=-1, keepdims=True)
    spread = jnp.mean(center * center, axis=-1, keepdims=True)
    return center * lax.rsqrt(spread + 1e-05)


def mm(a, b):
    return jnp.dot(a, b, preferred_element_type=F32)


def mm_t(a, b):
    return lax.dot_general(a, b, (((1,), (1,)), ((), ())), preferred_element_type=F32)


def lanes_between(width, low, high):
    lane = lax.broadcasted_iota(jnp.int32, (1, width), 1)
    return ((lane >= low) & (lane < high)).astype(F32)


def kernel(
    n,
    counts_s, offsets_h,
    pos_h, noise_h, single_h, token_h, abias_h, tsingle_h, tbias_h, mask_h,
    wcoord_h, waqkv_h, waout_h, wagg_h, wtqkv_h, wgate_h, wtout_h, wback_h, wpos_h,
    den_ref, tout_ref,
    offsets_s,
    pos, noise, single, token, abias, tsingle, tbias, pmask,
    wcoord, waqkv, waout, wagg, wtqkv, wgate, wtout, wback, wpos,
    columns, hs, tail, head, lo, up, shifted, ext, keys_s, values_s, mid, att_s,
    part_down, part_up, from_low, from_high, u_all, near,
    local_sem, edge_send, edge_recv, line_send, ag_send, ag_recv,
):
    cap, ca = single.shape
    rows, ct = tsingle.shape
    me = lax.axis_index("row")
    last = n - 1
    has_low = me > 0
    has_high = me < last

    pairs = [
        (pos_h, pos), (noise_h, noise), (single_h, single), (wcoord_h, wcoord), (token_h, token),
        (waqkv_h, waqkv), (abias_h, abias), (waout_h, waout), (wagg_h, wagg), (tsingle_h, tsingle),
        (wtqkv_h, wtqkv), (wgate_h, wgate), (mask_h, pmask), (tbias_h, tbias), (wtout_h, wtout),
        (wback_h, wback), (wpos_h, wpos), (offsets_h, offsets_s),
    ]
    copies = {}
    for k, (src, dst) in enumerate(pairs):
        copies[id(dst)] = pltpu.make_async_copy(src, dst, local_sem.at[k])
        copies[id(dst)].start()

    def need(*refs):
        for r in refs:
            copies[id(r)].wait()

    core = lax.rem(me, 2)
    y = lax.rem(me // 2, 2)
    z = me // 4
    depth = n // 4

    def index_of(zz, yy, cc):
        return zz * 4 + yy * 2 + cc

    partner = index_of(z, y, 1 - core)
    across = index_of(z, 1 - y, core)
    line = []
    for d in range(1, depth):
        line.append((z + d < depth, index_of(z + d, y, core), 2 * d))
        line.append((z >= d, index_of(z - d, y, core), 2 * d + 1))

    barrier = pltpu.get_barrier_semaphore()

    def greet(peer):
        pl.semaphore_signal(
            barrier, inc=1, device_id={"row": peer}, device_id_type=pl.DeviceIdType.MESH
        )

    greet(partner)
    greet(across)
    for there, peer, _ in line:
        pl.when(there)(lambda peer=peer: greet(peer))
    far = me - 1 + 2 * core
    has_far = (far >= 0) & (far < n)
    pl.when(has_far)(lambda: greet(far))

    shifted[...] = jnp.zeros_like(shifted)
    columns[...] = jnp.zeros_like(columns)
    near[...] = jnp.zeros_like(near)

    @pl.when(me == 0)
    def _():
        lo[...] = jnp.zeros_like(lo)
        from_low[...] = jnp.zeros_like(from_low)

    @pl.when(me == last)
    def _():
        up[...] = jnp.zeros_like(up)
        from_high[...] = jnp.zeros_like(from_high)

    need(pos, noise, single, wcoord, token)
    live = jnp.clip(counts_s[0], cap // 2, cap)
    noisy = pos[...] + noise_level * noise[...]
    columns[0:3, :] = input_scale * noisy
    relative = token[...].reshape(1, cap) - (me - 1) * rows
    columns[3:4, :] = relative.astype(F32)
    turned = columns[...].T
    wc = wcoord[...]
    atom_start = single[...].astype(F32) + (
        turned[:, 0:1] * wc[0:1, :] + turned[:, 1:2] * wc[1:2, :] + turned[:, 2:3] * wc[2:3, :]
    )
    near_rows = near.shape[0]
    lane_ids = lax.broadcasted_iota(jnp.int32, (cap, near_rows), 1).astype(F32)
    hot_t = (turned[:, 3:4] == lane_ids).astype(F32).astype(BF16)
    normed = normalize(atom_start)
    hs[...] = normed
    mid[...] = atom_start
    head[...] = normed[:AHEAD].astype(BF16)
    tail[...] = hs[pl.ds(live - BEHIND, BEHIND), :].astype(BF16)

    peers = 2 + (depth - 1) + jnp.where(has_far, 1, 0)
    pl.semaphore_wait(barrier, peers)

    def edge(k, src, dst, peer):
        return pltpu.make_async_remote_copy(
            src_ref=src,
            dst_ref=dst,
            send_sem=edge_send.at[k],
            recv_sem=edge_recv.at[k],
            device_id={"row": peer},
            device_id_type=pl.DeviceIdType.MESH,
        )

    def exchange(stage, src_up, dst_up, src_down, dst_down):
        going_up = edge(2 * stage, src_up, dst_up, me + 1)
        going_down = edge(2 * stage + 1, src_down, dst_down, me - 1)
        pl.when(has_high)(going_up.start)
        pl.when(has_low)(going_down.start)

        def receive():
            pl.when(has_low)(going_up.wait_recv)
            pl.when(has_high)(going_down.wait_recv)

        def finish():
            pl.when(has_high)(going_up.wait_send)
            pl.when(has_low)(going_down.wait_send)

        return receive, finish

    receive_rim, finish_rim = exchange(0, tail, lo, head, up)

    need(waqkv)
    hw = ca // AH
    normed_b = normed.astype(BF16)
    own = mm(normed_b, waqkv[...])
    queries = (own[:, :ca] * (1.0 / hw**0.5)).astype(BF16)
    head_lanes = [lanes_between(ca, h * hw, (h + 1) * hw) for h in range(AH)]
    keys_s[BEHIND : BEHIND + cap, :] = own[:, ca : 2 * ca]
    values_s[BEHIND : BEHIND + cap, :] = own[:, 2 * ca :]
    ext[BEHIND : BEHIND + cap, :] = normed
    need(abias, offsets_s)

    top = jnp.where(has_high, BEHIND + live + AHEAD, BEHIND + live)
    bottom = jnp.where(has_low, 0, BEHIND)
    lane_key = lax.broadcasted_iota(jnp.int32, (1, KWIN), 1)
    ones = jnp.ones((KWIN, ca), BF16)

    def attend(windows):
        at = [BEHIND + QWIN * w + offsets_s[w] for w in windows]
        scores = []
        for w, start in zip(windows, at):
            key = keys_s[pl.ds(start, KWIN), :].astype(BF16)
            q = queries[w * QWIN : (w + 1) * QWIN, :]
            wide = jnp.concatenate([q * m.astype(BF16) for m in head_lanes], axis=0)
            scores.append(mm_t(wide, key))
        exps = []
        for w, start, score in zip(windows, at, scores):
            score = score + abias[:, w * QWIN : (w + 1) * QWIN, :].reshape(AH * QWIN, KWIN)
            keys = lane_key + start
            score = jnp.where((keys >= bottom) & (keys < top), score, masked_score)
            exps.append(jnp.exp(score - jnp.max(score, axis=-1, keepdims=True)).astype(BF16))
        outs = []
        for start, e in zip(at, exps):
            value = values_s[pl.ds(start, KWIN), :].astype(BF16)
            outs.append(mm(e, jnp.concatenate([value, ones], axis=1)))
        for w, out in zip(windows, outs):
            mixed = out[:QWIN] * wide_lanes[0]
            for h in range(1, AH):
                mixed = mixed + out[h * QWIN : (h + 1) * QWIN] * wide_lanes[h]
            att_s[w * QWIN : (w + 1) * QWIN, :] = (mixed[:, :ca] / mixed[:, ca:]).astype(BF16)

    wide_lanes = [jnp.concatenate([m, m], axis=1) for m in head_lanes]
    half = cap // 2
    count = cap // QWIN
    behind_windows = BEHIND // QWIN
    inner = [w for w in range(count) if w >= behind_windows and QWIN * w + AHEAD <= half]
    outer = [w for w in range(count) if w not in inner]
    attend(inner)

    receive_rim()
    ext[:BEHIND, :] = lo[...].astype(F32)
    shifted[half : half + AHEAD, :] = up[...].astype(F32)
    first = BEHIND + half
    span = half + AHEAD
    moved = shifted[pl.ds(cap - live, span), :]
    row_ids = lax.broadcasted_iota(jnp.int32, (span, ca), 0) + first
    ext[first : BEHIND + cap, :] = jnp.where(
        row_ids[:half] < BEHIND + live, ext[first : BEHIND + cap, :], moved[:half]
    )
    ext[BEHIND + cap :, :] = moved[half:]
    low_kv = mm(ext[:BEHIND, :].astype(BF16), waqkv[:, ca:])
    keys_s[:BEHIND, :] = low_kv[:, :ca]
    values_s[:BEHIND, :] = low_kv[:, ca:]
    high_kv = mm(ext[first:, :].astype(BF16), waqkv[:, ca:])
    keys_s[first:, :] = high_kv[:, :ca]
    values_s[first:, :] = high_kv[:, ca:]
    for k in range(0, len(outer), GROUP):
        attend(outer[k : k + GROUP])

    need(waout, wagg)
    atom_mid = mid[...] + mm(att_s[...], waout[...])
    mid[...] = atom_mid
    spread = jnp.maximum(mm(atom_mid.astype(BF16), wagg[...]), 0.0).astype(BF16)
    slot_lane = lax.broadcasted_iota(jnp.int32, (1, cap), 1)
    living = slot_lane < live
    sub_ids = lax.broadcasted_iota(jnp.int32, (3 * rows, cap), 0)
    hot = ((sub_ids == relative) & living).astype(F32)
    counted = jnp.sum(hot, axis=-1, keepdims=True)
    partial = mm(hot.astype(BF16), spread)
    few = jnp.minimum(counted, 256.0)
    lane_c = lax.broadcasted_iota(jnp.int32, (3 * rows, 128), 1)
    count_wide = jnp.where(lane_c < 64, few, counted - few)
    part_down[:, :ct] = partial[:rows].astype(BF16)
    part_down[:, ct:] = count_wide[:rows].astype(BF16)
    part_up[:, :ct] = partial[2 * rows :].astype(BF16)
    part_up[:, ct:] = count_wide[2 * rows :].astype(BF16)
    receive_part, finish_part = exchange(1, part_up, from_low, part_down, from_high)

    need(tsingle, wtqkv, wgate)
    receive_part()
    low = from_low[...].astype(F32)
    high = from_high[...].astype(F32)
    token_sum = partial[rows : 2 * rows] + high[:, :ct] + low[:, :ct]
    token_count = (
        counted[rows : 2 * rows]
        + (high[:, ct : ct + 1] + high[:, ct + 64 : ct + 65])
        + (low[:, ct : ct + 1] + low[:, ct + 64 : ct + 65])
    )
    token_in = tsingle[...].astype(F32) + token_sum / jnp.maximum(token_count, 1.0)
    u = normalize(token_in).astype(BF16)
    u_all[pl.ds(pl.multiple_of(me * rows, rows), rows), :] = u

    part = rows // PIECES

    def block(src, piece, peer, sent):
        view = u_all.at[pl.ds(pl.multiple_of(src * rows + piece * part, part), part), :]
        return pltpu.make_async_remote_copy(
            src_ref=view,
            dst_ref=view,
            send_sem=sent,
            recv_sem=ag_recv.at[src, piece],
            device_id={"row": peer},
            device_id_type=pl.DeviceIdType.MESH,
        )

    def relay(src, piece, over, act):
        if over:
            act(block(src, piece, across, ag_send.at[0, src, piece]))
        act(block(src, piece, partner, ag_send.at[1, src, piece]))

    def own_sends(act):
        for piece in range(PIECES):
            relay(me, piece, True, act)
            for there, peer, way in line:
                pl.when(there)(lambda piece=piece, peer=peer, way=way: act(block(me, piece, peer, line_send.at[way, piece])))

    def start(c):
        c.start()

    def end(c):
        c.wait_send()

    steps = []
    for d in range(1, depth + 1):
        if d < depth:
            steps.append((z >= d, index_of(z - d, y, core), True))
            steps.append((z + d < depth, index_of(z + d, y, core), True))
        if d == 1:
            steps.append((None, across, False))
        else:
            steps.append((z >= d - 1, index_of(z - d + 1, 1 - y, core), False))
            steps.append((z + d - 1 < depth, index_of(z + d - 1, 1 - y, core), False))

    own_sends(start)

    tw = ct // TH
    group = TH // 2
    gw = group * tw
    tquery = mm(u, wtqkv[:, :ct]).astype(BF16)
    through = []
    group_lanes = [lanes_between(gw, h * tw, (h + 1) * tw) for h in range(group)]
    for g in range(2):
        q = tquery[:, g * gw : (g + 1) * gw]
        wide = jnp.concatenate([q * m.astype(BF16) for m in group_lanes], axis=0)
        through.append(mm_t(wide, wtqkv[:, ct + g * gw : ct + (g + 1) * gw]).astype(BF16))
    gate = jax.nn.sigmoid(mm(u, wgate[...]))

    def arrive(src, over):
        for piece in range(PIECES):
            block(src, piece, partner, ag_send.at[1, 0, piece]).wait_recv()
            relay(src, piece, over, start)

    def leave(src, over):
        for piece in range(PIECES):
            relay(src, piece, over, end)

    def each(visit):
        for there, src, over in steps:
            if there is None:
                visit(src, over)
            else:
                pl.when(there)(lambda src=src, over=over: visit(src, over))

    each(arrive)
    for zz in range(depth):
        for yy in range(2):
            for piece in range(PIECES):
                block(index_of(zz, yy, 1 - core), piece, partner, ag_send.at[1, 0, piece]).wait_recv()

    need(pmask, tbias, wtout, wback, wpos)
    features = u_all[...]
    allowed = (pmask[...] == 1)[None]
    pieces = []
    for g in range(2):
        score = mm_t(through[g], features) * (1.0 / tw**0.5)
        score = score.reshape(group, rows, score.shape[-1]) + tbias[g * group : (g + 1) * group]
        score = jnp.where(allowed, score, masked_score)
        e = jnp.exp(score - jnp.max(score, axis=-1, keepdims=True))
        weights = (e / jnp.sum(e, axis=-1, keepdims=True)).astype(BF16)
        mixed = mm(weights.reshape(group * rows, -1), features).astype(BF16)
        out = mm(mixed, wtqkv[:, 2 * ct + g * gw : 2 * ct + (g + 1) * gw])
        total = out[:rows] * group_lanes[0]
        for h in range(1, group):
            total = total + out[h * rows : (h + 1) * rows] * group_lanes[h]
        pieces.append(total)
    gated = (gate * jnp.concatenate(pieces, axis=1)).astype(BF16)
    token_out = (token_in + mm(gated, wtout[...])).astype(BF16)
    tout_ref[...] = token_out
    near[rows : 2 * rows, :] = mm(token_out, wback[...]).astype(BF16)
    own = near.at[rows : 2 * rows]
    receive_back, finish_back = exchange(
        2, own, near.at[0:rows], own, near.at[2 * rows : 3 * rows]
    )
    finish_rim()
    finish_part()
    own_sends(end)
    each(leave)
    receive_back()
    atom_last = mid[...] + mm(hot_t, near[...])
    final = normalize(atom_last).astype(BF16)
    update = mm_t(wpos[...], final)
    den_ref[...] = jnp.where(living, skip_scale * noisy + output_scale * update, 0.0)
    finish_back()


def store(den, tout, den_h, tout_h, sem):
    copies = [pltpu.make_async_copy(den, den_h, sem.at[0]), pltpu.make_async_copy(tout, tout_h, sem.at[1])]
    for c in copies:
        c.start()
    for c in copies:
        c.wait()


def on_device(
    positions, noise, atom_single, atom_token, atom_counts, window_offsets, atom_bias,
    token_single, token_bias, pair_mask, w_coord, w_atom_qkv, w_atom_out, w_agg,
    w_tok_qkv, w_tok_gate, w_tok_out, w_back, w_pos,
):
    n = lax.axis_size("row")
    cap, ca = atom_single.shape
    rows, ct = token_single.shape
    big = (
        positions, noise, atom_single, atom_token, atom_bias, token_single,
        token_bias, pair_mask, w_coord, w_atom_qkv, w_atom_out, w_agg, w_tok_qkv, w_tok_gate,
        w_tok_out, w_back, w_pos,
    )
    near_rows = -(-3 * rows // 128) * 128
    hbm = pl.BlockSpec(memory_space=pltpu.HBM)
    vmem = pl.BlockSpec(memory_space=pltpu.VMEM)
    out_shapes = (((positions.shape[0], cap), F32), ((rows, ct), BF16))
    results = pl.pallas_call(
        lambda *refs: kernel(n, *refs),
        out_shape=tuple(pltpu.VMEM(shape, kind) for shape, kind in out_shapes),
        in_specs=[pl.BlockSpec(memory_space=pltpu.SMEM)] + [hbm] * (1 + len(big)),
        out_specs=(vmem, vmem),
        scratch_shapes=[pltpu.SMEM(window_offsets.shape, jnp.int32)]
        + [pltpu.VMEM(a.shape, a.dtype) for a in big]
        + [
            pltpu.VMEM((128, cap), F32),
            pltpu.VMEM((cap, ca), F32),
            pltpu.VMEM((BEHIND, ca), BF16),
            pltpu.VMEM((AHEAD, ca), BF16),
            pltpu.VMEM((BEHIND, ca), BF16),
            pltpu.VMEM((AHEAD, ca), BF16),
            pltpu.VMEM((cap + AHEAD, ca), F32),
            pltpu.VMEM((BEHIND + cap + AHEAD, ca), F32),
            pltpu.VMEM((BEHIND + cap + AHEAD, ca), F32),
            pltpu.VMEM((BEHIND + cap + AHEAD, ca), F32),
            pltpu.VMEM((cap, ca), F32),
            pltpu.VMEM((cap, ca), BF16),
            pltpu.VMEM((rows, ct + 128), BF16),
            pltpu.VMEM((rows, ct + 128), BF16),
            pltpu.VMEM((rows, ct + 128), BF16),
            pltpu.VMEM((rows, ct + 128), BF16),
            pltpu.VMEM((n * rows, ct), BF16),
            pltpu.VMEM((near_rows, ca), BF16),
            pltpu.SemaphoreType.DMA((1 + len(big),)),
            pltpu.SemaphoreType.DMA((6,)),
            pltpu.SemaphoreType.DMA((6,)),
            pltpu.SemaphoreType.DMA((n // 2, PIECES)),
            pltpu.SemaphoreType.DMA((2, n, PIECES)),
            pltpu.SemaphoreType.DMA((n, PIECES)),
        ],
        compiler_params=pltpu.CompilerParams(collective_id=0, has_side_effects=True, vmem_limit_bytes=VMEM_LIMIT),
    )(atom_counts, *(pltpu.with_memory_space_constraint(a, pltpu.HBM) for a in (window_offsets,) + big))
    results = tuple(pltpu.with_memory_space_constraint(a, pltpu.VMEM) for a in results)
    return pl.pallas_call(
        store,
        out_shape=tuple(jax.ShapeDtypeStruct(shape, kind) for shape, kind in out_shapes),
        in_specs=[vmem, vmem],
        out_specs=(hbm, hbm),
        scratch_shapes=[pltpu.SemaphoreType.DMA((2,))],
    )(*results)


def solution(mesh):
    placed = (
        P(None, ("grp", "row")),
        P(None, ("grp", "row")),
        P(("grp", "row"), None),
        P(("grp", "row")),
        P(("grp", "row")),
        P(("grp", "row")),
        P(None, ("grp", "row"), None),
        P(("grp", "row"), None),
        P(None, ("grp", "row"), None),
        P(("grp", "row"), None),
    ) + (P(),) * 9
    return jax.shard_map(
        on_device,
        mesh=mesh,
        in_specs=placed,
        out_specs=(P(None, ("grp", "row")), P(("grp", "row"), None)),
        check_vma=False,
    )
```

```python
import jax
import jax.numpy as jnp
from jax import lax
from jax.experimental import pallas as pl
from jax.experimental.pallas import tpu as pltpu
from jax.sharding import PartitionSpec as P

AH = 4
TH = 16
QWIN = 32
KWIN = 128
BEHIND = KWIN // 2
AHEAD = KWIN - QWIN

noise_level = 2.0
input_scale = 1.0 / 5.0**0.5
skip_scale = 1.0 / 5.0
output_scale = 2.0 / 5.0**0.5
masked_score = -1e30

F32 = jnp.float32
BF16 = jnp.bfloat16
GROUP = 5
BATCH = 4
VMEM_LIMIT = 40 * 1024 * 1024


def normalize(values):
    center = values - jnp.mean(values, axis=-1, keepdims=True)
    spread = jnp.mean(center * center, axis=-1, keepdims=True)
    return center * lax.rsqrt(spread + 1e-05)


def mm(a, b):
    return jnp.dot(a, b, preferred_element_type=F32)


def mm_t(a, b):
    return lax.dot_general(a, b, (((1,), (1,)), ((), ())), preferred_element_type=F32)


def lanes_between(width, low, high):
    lane = lax.broadcasted_iota(jnp.int32, (1, width), 1)
    return ((lane >= low) & (lane < high)).astype(F32)


def kernel(
    n,
    counts_s, offsets_h,
    pos_h, noise_h, single_h, token_h, abias_h, tsingle_h, tbias_h, mask_h,
    wcoord_h, waqkv_h, waout_h, wagg_h, wtqkv_h, wgate_h, wtout_h, wback_h, wpos_h,
    den_ref, tout_ref,
    offsets_s,
    pos, noise, single, token, abias, tsingle, tbias, pmask,
    wcoord, waqkv, waout, wagg, wtqkv, wgate, wtout, wback, wpos,
    columns, hs, tail, head, lo, up, shifted, ext, keys_s, values_s, mid, att_s,
    part_down, part_up, from_low, from_high, early_all, late_all, u_all, hot_s, near,
    local_sem, edge_send, edge_recv, line_send, across_send, ag_send, ag_recv,
):
    cap, ca = single.shape
    rows, ct = tsingle.shape
    margin = rows // 4
    rim_rows = 2 * margin
    me = lax.axis_index("row")
    last = n - 1
    has_low = me > 0
    has_high = me < last

    pairs = [
        (pos_h, pos), (noise_h, noise), (single_h, single), (wcoord_h, wcoord), (token_h, token),
        (waqkv_h, waqkv), (abias_h, abias), (waout_h, waout), (wagg_h, wagg), (tsingle_h, tsingle),
        (wtqkv_h, wtqkv), (wgate_h, wgate), (mask_h, pmask), (tbias_h, tbias), (wtout_h, wtout),
        (wback_h, wback), (wpos_h, wpos), (offsets_h, offsets_s),
    ]
    copies = {}
    for k, (src, dst) in enumerate(pairs):
        copies[id(dst)] = pltpu.make_async_copy(src, dst, local_sem.at[k])
        copies[id(dst)].start()

    def need(*refs):
        for r in refs:
            copies[id(r)].wait()

    core = lax.rem(me, 2)
    y = lax.rem(me // 2, 2)
    z = me // 4
    depth = n // 4

    def index_of(zz, yy, cc):
        return zz * 4 + yy * 2 + cc

    partner = index_of(z, y, 1 - core)
    across = index_of(z, 1 - y, core)
    line = []
    for d in range(1, depth):
        line.append((z + d < depth, index_of(z + d, y, core), z + d))
        line.append((z >= d, index_of(z - d, y, core), z - d))

    ends = depth - 1
    if ends:
        line.append((z == 0, index_of(z + ends, 1 - y, core), z))
        line.append((z == ends, index_of(z - ends, 1 - y, core), z))

    barrier = pltpu.get_barrier_semaphore()

    def greet(peer):
        pl.semaphore_signal(
            barrier, inc=1, device_id={"row": peer}, device_id_type=pl.DeviceIdType.MESH
        )

    greet(partner)
    greet(across)
    for there, peer, _ in line:
        pl.when(there)(lambda peer=peer: greet(peer))
    far = me - 1 + 2 * core
    has_far = (far >= 0) & (far < n)
    pl.when(has_far)(lambda: greet(far))

    shifted[...] = jnp.zeros_like(shifted)
    columns[...] = jnp.zeros_like(columns)
    near[...] = jnp.zeros_like(near)

    @pl.when(me == 0)
    def _():
        lo[...] = jnp.zeros_like(lo)
        from_low[...] = jnp.zeros_like(from_low)

    @pl.when(me == last)
    def _():
        up[...] = jnp.zeros_like(up)
        from_high[...] = jnp.zeros_like(from_high)

    need(pos, noise, single, wcoord, token)
    live = jnp.clip(counts_s[0], cap // 2, cap)
    noisy = pos[...] + noise_level * noise[...]
    columns[0:3, :] = input_scale * noisy
    relative = token[...].reshape(1, cap) - (me - 1) * rows
    turned = columns[...].T
    wc = wcoord[...]
    atom_start = single[...].astype(F32) + (
        turned[:, 0:1] * wc[0:1, :] + turned[:, 1:2] * wc[1:2, :] + turned[:, 2:3] * wc[2:3, :]
    )
    normed = normalize(atom_start)
    hs[...] = normed
    mid[...] = atom_start
    head[...] = normed[:AHEAD].astype(BF16)
    tail[...] = hs[pl.ds(live - BEHIND, BEHIND), :].astype(BF16)

    at_end = jnp.where((z == 0) | (z == ends), 1, 0) if ends else 0
    peers = 2 + (depth - 1) + jnp.where(has_far, 1, 0) + at_end
    pl.semaphore_wait(barrier, peers)

    def edge(k, src, dst, peer):
        return pltpu.make_async_remote_copy(
            src_ref=src,
            dst_ref=dst,
            send_sem=edge_send.at[k],
            recv_sem=edge_recv.at[k],
            device_id={"row": peer},
            device_id_type=pl.DeviceIdType.MESH,
        )

    def exchange(stage, src_up, dst_up, src_down, dst_down):
        going_up = edge(2 * stage, src_up, dst_up, me + 1)
        going_down = edge(2 * stage + 1, src_down, dst_down, me - 1)
        pl.when(has_high)(going_up.start)
        pl.when(has_low)(going_down.start)

        def receive():
            pl.when(has_low)(going_up.wait_recv)
            pl.when(has_high)(going_down.wait_recv)

        def finish():
            pl.when(has_high)(going_up.wait_send)
            pl.when(has_low)(going_down.wait_send)

        return receive, finish

    receive_rim, finish_rim = exchange(0, tail, lo, head, up)

    need(waqkv)
    hw = ca // AH
    normed_b = normed.astype(BF16)
    own = mm(normed_b, waqkv[...])
    queries = (own[:, :ca] * (1.0 / hw**0.5)).astype(BF16)
    head_lanes = [lanes_between(ca, h * hw, (h + 1) * hw) for h in range(AH)]
    keys_s[BEHIND : BEHIND + cap, :] = own[:, ca : 2 * ca]
    values_s[BEHIND : BEHIND + cap, :] = own[:, 2 * ca :]
    ext[BEHIND : BEHIND + cap, :] = normed
    need(abias, offsets_s)

    top = jnp.where(has_high, BEHIND + live + AHEAD, BEHIND + live)
    bottom = jnp.where(has_low, 0, BEHIND)
    lane_key = lax.broadcasted_iota(jnp.int32, (1, KWIN), 1)
    ones = jnp.ones((KWIN, ca), BF16)

    def attend(windows):
        at = [BEHIND + QWIN * w + offsets_s[w] for w in windows]
        scores = []
        for w, start in zip(windows, at):
            key = keys_s[pl.ds(start, KWIN), :].astype(BF16)
            q = queries[w * QWIN : (w + 1) * QWIN, :]
            wide = jnp.concatenate([q * m.astype(BF16) for m in head_lanes], axis=0)
            scores.append(mm_t(wide, key))
        exps = []
        for w, start, score in zip(windows, at, scores):
            score = score + abias[:, w * QWIN : (w + 1) * QWIN, :].reshape(AH * QWIN, KWIN)
            keys = lane_key + start
            score = jnp.where((keys >= bottom) & (keys < top), score, masked_score)
            exps.append(jnp.exp(score - jnp.max(score, axis=-1, keepdims=True)).astype(BF16))
        outs = []
        for start, e in zip(at, exps):
            value = values_s[pl.ds(start, KWIN), :].astype(BF16)
            outs.append(mm(e, jnp.concatenate([value, ones], axis=1)))
        for w, out in zip(windows, outs):
            mixed = out[:QWIN] * wide_lanes[0]
            for h in range(1, AH):
                mixed = mixed + out[h * QWIN : (h + 1) * QWIN] * wide_lanes[h]
            att_s[w * QWIN : (w + 1) * QWIN, :] = (mixed[:, :ca] / mixed[:, ca:]).astype(BF16)

    wide_lanes = [jnp.concatenate([m, m], axis=1) for m in head_lanes]
    half = cap // 2
    count = cap // QWIN
    behind_windows = BEHIND // QWIN
    inner = [w for w in range(count) if w >= behind_windows and QWIN * w + AHEAD <= half]
    outer = [w for w in range(count) if w not in inner]
    attend(inner)

    receive_rim()
    ext[:BEHIND, :] = lo[...].astype(F32)
    shifted[half : half + AHEAD, :] = up[...].astype(F32)
    first = BEHIND + half
    span = half + AHEAD
    moved = shifted[pl.ds(cap - live, span), :]
    row_ids = lax.broadcasted_iota(jnp.int32, (span, ca), 0) + first
    ext[first : BEHIND + cap, :] = jnp.where(
        row_ids[:half] < BEHIND + live, ext[first : BEHIND + cap, :], moved[:half]
    )
    ext[BEHIND + cap :, :] = moved[half:]
    low_kv = mm(ext[:BEHIND, :].astype(BF16), waqkv[:, ca:])
    keys_s[:BEHIND, :] = low_kv[:, :ca]
    values_s[:BEHIND, :] = low_kv[:, ca:]
    high_kv = mm(ext[first:, :].astype(BF16), waqkv[:, ca:])
    keys_s[first:, :] = high_kv[:, :ca]
    values_s[first:, :] = high_kv[:, ca:]
    for k in range(0, len(outer), GROUP):
        attend(outer[k : k + GROUP])

    need(waout, wagg)
    atom_mid = mid[...] + mm(att_s[...], waout[...])
    mid[...] = atom_mid
    spread = jnp.maximum(mm(atom_mid.astype(BF16), wagg[...]), 0.0).astype(BF16)
    slot_lane = lax.broadcasted_iota(jnp.int32, (1, cap), 1)
    living = slot_lane < live
    sub_ids = lax.broadcasted_iota(jnp.int32, (3 * rows, cap), 0)
    hot = ((sub_ids == relative) & living).astype(F32)
    counted = jnp.sum(hot, axis=-1, keepdims=True)
    hot_s[...] = hot.astype(BF16)
    partial = mm(hot_s[...], spread)
    few = jnp.minimum(counted, 256.0)
    lane_c = lax.broadcasted_iota(jnp.int32, (3 * rows, 128), 1)
    count_wide = jnp.where(lane_c < 64, few, counted - few)
    down = slice(rows - margin, rows)
    ahead = slice(2 * rows, 2 * rows + rim_rows)
    part_down[:, :ct] = partial[down].astype(BF16)
    part_down[:, ct:] = count_wide[down].astype(BF16)
    part_up[:, :ct] = partial[ahead].astype(BF16)
    part_up[:, ct:] = count_wide[ahead].astype(BF16)
    receive_part, finish_part = exchange(1, part_up, from_low, part_down, from_high)

    need(tsingle)
    own_sum = partial[rows : 2 * rows]
    own_count = counted[rows : 2 * rows]
    middle = slice(margin, rows - margin)
    token_mid = tsingle[middle, :].astype(F32) + own_sum[middle] / jnp.maximum(own_count[middle], 1.0)
    early_all[pl.ds(me, 1)] = normalize(token_mid).astype(BF16)[None]

    def block(kind, src, peer, sent):
        view = (early_all, late_all)[kind].at[src]
        return pltpu.make_async_remote_copy(
            src_ref=view,
            dst_ref=view,
            send_sem=sent,
            recv_sem=ag_recv.at[src, kind],
            device_id={"row": peer},
            device_id_type=pl.DeviceIdType.MESH,
        )

    def relay(kind, src, over, act):
        if over:
            act(block(kind, src, across, across_send.at[src // 4, kind]))
        act(block(kind, src, partner, ag_send.at[src // 2, kind]))

    def own_sends(kind, act):
        for there, peer, way in line:
            pl.when(there)(lambda peer=peer, way=way: act(block(kind, me, peer, line_send.at[way, kind])))
        relay(kind, me, True, act)

    def start(c):
        c.start()

    def end(c):
        c.wait_send()

    own_sends(0, start)

    need(wtqkv, wgate)
    receive_part()
    low = from_low[...].astype(F32)
    high = from_high[...].astype(F32)

    def counts_in(sums):
        return sums[:, ct : ct + 1] + sums[:, ct + 64 : ct + 65]

    def edges(own, below, above):
        return jnp.concatenate(
            [own[:rim_rows] + below, own[rim_rows : rows - margin], own[rows - margin :] + above], axis=0
        )

    token_sum = edges(own_sum, low[:, :ct], high[:, :ct])
    token_count = edges(own_count, counts_in(low), counts_in(high))
    token_in = tsingle[...].astype(F32) + token_sum / jnp.maximum(token_count, 1.0)
    u_wide = normalize(token_in)
    u = u_wide.astype(BF16)
    chunks = ct // 128
    odd = [u_wide[margin : margin + 1, 128 * k : 128 * (k + 1)] for k in range(chunks)]
    odd.append(jnp.zeros((rim_rows - chunks, 128), F32))
    late = jnp.concatenate(
        [
            jnp.concatenate([u_wide[rows - margin :], u_wide[:margin]], axis=0),
            jnp.concatenate(odd, axis=0),
        ],
        axis=1,
    )
    late_all[pl.ds(me, 1)] = late.astype(BF16)[None]
    own_sends(1, start)

    direct = []
    crossed = []
    for d in range(1, depth):
        over = d < ends
        direct.append((z >= d, index_of(z - d, y, core), over))
        direct.append((z + d < depth, index_of(z + d, y, core), over))
    crossed.append((None, across, False))
    for d in range(1, depth):
        crossed.append((z >= d, index_of(z - d, 1 - y, core), False))
        crossed.append((z + d < depth, index_of(z + d, 1 - y, core), False))
    steps = direct + crossed

    def arrive(kind, src, over):
        block(kind, src, partner, ag_send.at[0, kind]).wait_recv()
        relay(kind, src, over, start)

    def leave(kind, src, over):
        relay(kind, src, over, end)

    def each(kind, some, visit):
        for there, src, over in some:
            if there is None:
                visit(kind, src, over)
            else:
                pl.when(there)(lambda src=src, over=over: visit(kind, src, over))

    def last_hops(kind):
        for zz in range(depth):
            for yy in range(2):
                block(kind, index_of(zz, yy, 1 - core), partner, ag_send.at[0, kind]).wait_recv()

    each(0, direct[:2], arrive)
    tw = ct // TH
    tquery = (mm(u, wtqkv[:, :ct]) * (1.0 / tw**0.5)).astype(BF16)
    batches = []
    for first_head in range(0, TH, BATCH):
        heads = range(first_head, first_head + BATCH)
        left = first_head * tw // 128 * 128
        right = -(-(first_head + BATCH) * tw // 128) * 128
        lanes = [lanes_between(right - left, h * tw - left, (h + 1) * tw - left) for h in heads]
        q = tquery[:, left:right]
        wide = jnp.concatenate([q * m.astype(BF16) for m in lanes], axis=0)
        through = mm_t(wide, wtqkv[:, ct + left : ct + right]).astype(BF16)
        batches.append((first_head, left, right, lanes, through))
    gate = jax.nn.sigmoid(mm(u, wgate[...]))
    mid_t = mid[...].T
    each(0, direct[2:], arrive)
    each(1, direct, arrive)
    each(0, crossed, arrive)
    each(1, crossed, arrive)
    last_hops(0)
    for src in range(n):
        u_all[src * rows + margin : (src + 1) * rows - margin, :] = early_all[src]
    last_hops(1)
    first_row = lax.broadcasted_iota(jnp.int32, (margin, ct), 0) == 0
    for src in range(n):
        at = src * rows
        u_all[at : at + margin, :] = late_all[src, margin:, :ct]
        u_all[at + rows - margin : at + rows, :] = late_all[src, :margin, :ct]
        extra = late_all[src, :, ct:].astype(F32)
        row = jnp.concatenate([extra[k : k + 1] for k in range(chunks)], axis=1)
        tile = early_all[src, :margin, :].astype(F32)
        u_all[at + margin : at + 2 * margin, :] = jnp.where(first_row, row, tile).astype(BF16)
    need(pmask, tbias, wtout, wback, wpos)
    features = u_all[...]
    allowed = (pmask[...] == 1)[None]
    scores = [mm_t(through, features) for _, _, _, _, through in batches]
    weighted = []
    for (first_head, _, _, _, _), score in zip(batches, scores):
        score = score.reshape(BATCH, rows, score.shape[-1]) + tbias[first_head : first_head + BATCH]
        score = jnp.where(allowed, score, masked_score)
        e = jnp.exp(score - jnp.max(score, axis=-1, keepdims=True))
        weights = (e / jnp.sum(e, axis=-1, keepdims=True)).astype(BF16)
        weighted.append(mm(weights.reshape(BATCH * rows, -1), features).astype(BF16))
    blocks = [None] * chunks
    for (_, left, right, lanes, _), mixed in zip(batches, weighted):
        out = mm(mixed, wtqkv[:, 2 * ct + left : 2 * ct + right])
        total = out[:rows] * lanes[0]
        for h in range(1, BATCH):
            total = total + out[h * rows : (h + 1) * rows] * lanes[h]
        for k in range(left // 128, right // 128):
            part = total[:, 128 * k - left : 128 * (k + 1) - left]
            blocks[k] = part if blocks[k] is None else blocks[k] + part
    gated = (gate * jnp.concatenate(blocks, axis=1)).astype(BF16)
    token_out = (token_in + mm(gated, wtout[...])).astype(BF16)
    tout_ref[...] = token_out
    near[rows : 2 * rows, :] = mm(token_out, wback[...]).astype(BF16)
    upper = near.at[2 * rows - margin : 2 * rows]
    lower = near.at[rows : rows + rim_rows]
    receive_back, finish_back = exchange(
        2, upper, near.at[rows - margin : rows], lower, near.at[2 * rows : 2 * rows + rim_rows]
    )
    finish_rim()
    finish_part()
    for kind in range(2):
        own_sends(kind, end)
        each(kind, steps, leave)
    receive_back()
    back_t = lax.dot_general(near[...], hot_s[...], (((0,), (0,)), ((), ())), preferred_element_type=F32)
    atom_last = mid_t + back_t
    center = atom_last - jnp.mean(atom_last, axis=0, keepdims=True)
    width = jnp.mean(center * center, axis=0, keepdims=True)
    final = (center * lax.rsqrt(width + 1e-05)).astype(BF16)
    update = mm(wpos[...], final)
    den_ref[...] = jnp.where(living, skip_scale * noisy + output_scale * update, 0.0)
    finish_back()


def store(den, tout, den_h, tout_h, sem):
    copies = [pltpu.make_async_copy(den, den_h, sem.at[0]), pltpu.make_async_copy(tout, tout_h, sem.at[1])]
    for c in copies:
        c.start()
    for c in copies:
        c.wait()


def on_device(
    positions, noise, atom_single, atom_token, atom_counts, window_offsets, atom_bias,
    token_single, token_bias, pair_mask, w_coord, w_atom_qkv, w_atom_out, w_agg,
    w_tok_qkv, w_tok_gate, w_tok_out, w_back, w_pos,
):
    n = lax.axis_size("row")
    cap, ca = atom_single.shape
    rows, ct = token_single.shape
    big = (
        positions, noise, atom_single, atom_token, atom_bias, token_single,
        token_bias, pair_mask, w_coord, w_atom_qkv, w_atom_out, w_agg, w_tok_qkv, w_tok_gate,
        w_tok_out, w_back, w_pos,
    )
    margin = rows // 4
    send_up, send_down = (2 * margin, ct + 128), (margin, ct + 128)
    hbm = pl.BlockSpec(memory_space=pltpu.HBM)
    vmem = pl.BlockSpec(memory_space=pltpu.VMEM)
    out_shapes = (((positions.shape[0], cap), F32), ((rows, ct), BF16))
    results = pl.pallas_call(
        lambda *refs: kernel(n, *refs),
        out_shape=tuple(pltpu.VMEM(shape, kind) for shape, kind in out_shapes),
        in_specs=[pl.BlockSpec(memory_space=pltpu.SMEM)] + [hbm] * (1 + len(big)),
        out_specs=(vmem, vmem),
        scratch_shapes=[pltpu.SMEM(window_offsets.shape, jnp.int32)]
        + [pltpu.VMEM(a.shape, a.dtype) for a in big]
        + [
            pltpu.VMEM((128, cap), F32),
            pltpu.VMEM((cap, ca), F32),
            pltpu.VMEM((BEHIND, ca), BF16),
            pltpu.VMEM((AHEAD, ca), BF16),
            pltpu.VMEM((BEHIND, ca), BF16),
            pltpu.VMEM((AHEAD, ca), BF16),
            pltpu.VMEM((cap + AHEAD, ca), F32),
            pltpu.VMEM((BEHIND + cap + AHEAD, ca), F32),
            pltpu.VMEM((BEHIND + cap + AHEAD, ca), F32),
            pltpu.VMEM((BEHIND + cap + AHEAD, ca), F32),
            pltpu.VMEM((cap, ca), F32),
            pltpu.VMEM((cap, ca), BF16),
            pltpu.VMEM(send_down, BF16),
            pltpu.VMEM(send_up, BF16),
            pltpu.VMEM(send_up, BF16),
            pltpu.VMEM(send_down, BF16),
            pltpu.VMEM((n, rows - 2 * margin, ct), BF16),
            pltpu.VMEM((n, 2 * margin, ct + 128), BF16),
            pltpu.VMEM((n * rows, ct), BF16),
            pltpu.VMEM((3 * rows, cap), BF16),
            pltpu.VMEM((3 * rows, ca), BF16),
            pltpu.SemaphoreType.DMA((1 + len(big),)),
            pltpu.SemaphoreType.DMA((6,)),
            pltpu.SemaphoreType.DMA((6,)),
            pltpu.SemaphoreType.DMA((n // 4, 2)),
            pltpu.SemaphoreType.DMA((n // 4, 2)),
            pltpu.SemaphoreType.DMA((n // 2, 2)),
            pltpu.SemaphoreType.DMA((n, 2)),
        ],
        compiler_params=pltpu.CompilerParams(collective_id=0, has_side_effects=True, vmem_limit_bytes=VMEM_LIMIT),
    )(atom_counts, *(pltpu.with_memory_space_constraint(a, pltpu.HBM) for a in (window_offsets,) + big))
    results = tuple(pltpu.with_memory_space_constraint(a, pltpu.VMEM) for a in results)
    return pl.pallas_call(
        store,
        out_shape=tuple(jax.ShapeDtypeStruct(shape, kind) for shape, kind in out_shapes),
        in_specs=[vmem, vmem],
        out_specs=(hbm, hbm),
        scratch_shapes=[pltpu.SemaphoreType.DMA((2,))],
    )(*results)


def solution(mesh):
    placed = (
        P(None, ("grp", "row")),
        P(None, ("grp", "row")),
        P(("grp", "row"), None),
        P(("grp", "row")),
        P(("grp", "row")),
        P(("grp", "row")),
        P(None, ("grp", "row"), None),
        P(("grp", "row"), None),
        P(None, ("grp", "row"), None),
        P(("grp", "row"), None),
    ) + (P(),) * 9
    return jax.shard_map(
        on_device,
        mesh=mesh,
        in_specs=placed,
        out_specs=(P(None, ("grp", "row")), P(("grp", "row"), None)),
        check_vma=False,
    )
```

```python
import jax
import jax.numpy as jnp
from jax import lax
from jax.experimental import pallas as pl
from jax.experimental.pallas import tpu as pltpu
from jax.sharding import PartitionSpec as P

AH = 4
TH = 16
QWIN = 32
KWIN = 128
BEHIND = KWIN // 2
AHEAD = KWIN - QWIN

noise_level = 2.0
input_scale = 1.0 / 5.0**0.5
skip_scale = 1.0 / 5.0
output_scale = 2.0 / 5.0**0.5
masked_score = -1e30

F32 = jnp.float32
BF16 = jnp.bfloat16
GROUP = 5
BATCH = 4
VMEM_LIMIT = 40 * 1024 * 1024


def normalize(values):
    center = values - jnp.mean(values, axis=-1, keepdims=True)
    spread = jnp.mean(center * center, axis=-1, keepdims=True)
    return center * lax.rsqrt(spread + 1e-05)


def mm(a, b):
    return jnp.dot(a, b, preferred_element_type=F32)


def mm_t(a, b):
    return lax.dot_general(a, b, (((1,), (1,)), ((), ())), preferred_element_type=F32)


def lanes_between(width, low, high):
    lane = lax.broadcasted_iota(jnp.int32, (1, width), 1)
    return ((lane >= low) & (lane < high)).astype(F32)


def kernel(
    n,
    counts_s, offsets_h,
    pos_h, noise_h, single_h, token_h, abias_h, tsingle_h, tbias_h, mask_h,
    wcoord_h, waqkv_h, waout_h, wagg_h, wtqkv_h, wgate_h, wtout_h, wback_h, wpos_h,
    den_ref, tout_ref,
    offsets_s,
    pos, noise, single, token, abias, tsingle, tbias, pmask,
    wcoord, waqkv, waout, wagg, wtqkv, wgate, wtout, wback, wpos,
    columns, hs, tail, head, lo, up, shifted, ext, keys_s, values_s, mid, att_s,
    part_down, part_up, from_low, from_high, early_all, late_all, u_half, bias_half, own_out, hot_s, near,
    local_sem, edge_send, edge_recv, line_send, across_send, ag_send, ag_recv,
):
    cap, ca = single.shape
    rows, ct = tsingle.shape
    margin = rows // 4
    rim_rows = 2 * margin
    me = lax.axis_index("row")
    last = n - 1
    has_low = me > 0
    has_high = me < last

    pairs = [
        (pos_h, pos), (noise_h, noise), (single_h, single), (wcoord_h, wcoord), (token_h, token),
        (waqkv_h, waqkv), (abias_h, abias), (waout_h, waout), (wagg_h, wagg), (tsingle_h, tsingle),
        (wtqkv_h, wtqkv), (wgate_h, wgate), (mask_h, pmask), (tbias_h, tbias), (wtout_h, wtout),
        (wback_h, wback), (wpos_h, wpos), (offsets_h, offsets_s),
    ]
    copies = {}
    for k, (src, dst) in enumerate(pairs):
        copies[id(dst)] = pltpu.make_async_copy(src, dst, local_sem.at[k])
        copies[id(dst)].start()

    def need(*refs):
        for r in refs:
            copies[id(r)].wait()

    core = lax.rem(me, 2)
    y = lax.rem(me // 2, 2)
    z = me // 4
    depth = n // 4

    def index_of(zz, yy, cc):
        return zz * 4 + yy * 2 + cc

    partner = index_of(z, y, 1 - core)
    across = index_of(z, 1 - y, core)
    line = []
    for d in range(1, depth):
        line.append((z + d < depth, index_of(z + d, y, core), z + d))
        line.append((z >= d, index_of(z - d, y, core), z - d))

    ends = depth - 1
    if ends:
        line.append((z == 0, index_of(z + ends, 1 - y, core), z))
        line.append((z == ends, index_of(z - ends, 1 - y, core), z))

    barrier = pltpu.get_barrier_semaphore()

    def greet(peer):
        pl.semaphore_signal(
            barrier, inc=1, device_id={"row": peer}, device_id_type=pl.DeviceIdType.MESH
        )

    greet(partner)
    greet(across)
    for there, peer, _ in line:
        pl.when(there)(lambda peer=peer: greet(peer))
    far = me - 1 + 2 * core
    has_far = (far >= 0) & (far < n)
    pl.when(has_far)(lambda: greet(far))

    shifted[...] = jnp.zeros_like(shifted)
    columns[...] = jnp.zeros_like(columns)
    near[...] = jnp.zeros_like(near)

    @pl.when(me == 0)
    def _():
        lo[...] = jnp.zeros_like(lo)
        from_low[...] = jnp.zeros_like(from_low)

    @pl.when(me == last)
    def _():
        up[...] = jnp.zeros_like(up)
        from_high[...] = jnp.zeros_like(from_high)

    need(pos, noise, single, wcoord, token)
    live = jnp.clip(counts_s[0], cap // 2, cap)
    noisy = pos[...] + noise_level * noise[...]
    columns[0:3, :] = input_scale * noisy
    relative = token[...].reshape(1, cap) - (me - 1) * rows
    turned = columns[...].T
    wc = wcoord[...]
    atom_start = single[...].astype(F32) + (
        turned[:, 0:1] * wc[0:1, :] + turned[:, 1:2] * wc[1:2, :] + turned[:, 2:3] * wc[2:3, :]
    )
    normed = normalize(atom_start)
    hs[...] = normed
    mid[...] = atom_start
    head[...] = normed[:AHEAD].astype(BF16)
    tail[...] = hs[pl.ds(live - BEHIND, BEHIND), :].astype(BF16)

    at_end = jnp.where((z == 0) | (z == ends), 1, 0) if ends else 0
    peers = 2 + (depth - 1) + jnp.where(has_far, 1, 0) + at_end
    pl.semaphore_wait(barrier, peers)

    def edge(k, src, dst, peer):
        return pltpu.make_async_remote_copy(
            src_ref=src,
            dst_ref=dst,
            send_sem=edge_send.at[k],
            recv_sem=edge_recv.at[k],
            device_id={"row": peer},
            device_id_type=pl.DeviceIdType.MESH,
        )

    def exchange(stage, src_up, dst_up, src_down, dst_down):
        going_up = edge(2 * stage, src_up, dst_up, me + 1)
        going_down = edge(2 * stage + 1, src_down, dst_down, me - 1)
        pl.when(has_high)(going_up.start)
        pl.when(has_low)(going_down.start)

        def receive():
            pl.when(has_low)(going_up.wait_recv)
            pl.when(has_high)(going_down.wait_recv)

        def finish():
            pl.when(has_high)(going_up.wait_send)
            pl.when(has_low)(going_down.wait_send)

        return receive, finish

    receive_rim, finish_rim = exchange(0, tail, lo, head, up)

    need(waqkv)
    hw = ca // AH
    normed_b = normed.astype(BF16)
    own = mm(normed_b, waqkv[...])
    queries = (own[:, :ca] * (1.0 / hw**0.5)).astype(BF16)
    head_lanes = [lanes_between(ca, h * hw, (h + 1) * hw) for h in range(AH)]
    keys_s[BEHIND : BEHIND + cap, :] = own[:, ca : 2 * ca]
    values_s[BEHIND : BEHIND + cap, :] = own[:, 2 * ca :]
    ext[BEHIND : BEHIND + cap, :] = normed
    need(abias, offsets_s)

    top = jnp.where(has_high, BEHIND + live + AHEAD, BEHIND + live)
    bottom = jnp.where(has_low, 0, BEHIND)
    lane_key = lax.broadcasted_iota(jnp.int32, (1, KWIN), 1)
    ones = jnp.ones((KWIN, ca), BF16)

    def attend(windows):
        at = [BEHIND + QWIN * w + offsets_s[w] for w in windows]
        scores = []
        for w, start in zip(windows, at):
            key = keys_s[pl.ds(start, KWIN), :].astype(BF16)
            q = queries[w * QWIN : (w + 1) * QWIN, :]
            wide = jnp.concatenate([q * m.astype(BF16) for m in head_lanes], axis=0)
            scores.append(mm_t(wide, key))
        exps = []
        for w, start, score in zip(windows, at, scores):
            score = score + abias[:, w * QWIN : (w + 1) * QWIN, :].reshape(AH * QWIN, KWIN)
            keys = lane_key + start
            score = jnp.where((keys >= bottom) & (keys < top), score, masked_score)
            exps.append(jnp.exp(score - jnp.max(score, axis=-1, keepdims=True)).astype(BF16))
        outs = []
        for start, e in zip(at, exps):
            value = values_s[pl.ds(start, KWIN), :].astype(BF16)
            outs.append(mm(e, jnp.concatenate([value, ones], axis=1)))
        for w, out in zip(windows, outs):
            mixed = out[:QWIN] * wide_lanes[0]
            for h in range(1, AH):
                mixed = mixed + out[h * QWIN : (h + 1) * QWIN] * wide_lanes[h]
            att_s[w * QWIN : (w + 1) * QWIN, :] = (mixed[:, :ca] / mixed[:, ca:]).astype(BF16)

    wide_lanes = [jnp.concatenate([m, m], axis=1) for m in head_lanes]
    half = cap // 2
    count = cap // QWIN
    behind_windows = BEHIND // QWIN
    inner = [w for w in range(count) if w >= behind_windows and QWIN * w + AHEAD <= half]
    outer = [w for w in range(count) if w not in inner]
    attend(inner)

    receive_rim()
    ext[:BEHIND, :] = lo[...].astype(F32)
    shifted[half : half + AHEAD, :] = up[...].astype(F32)
    first = BEHIND + half
    span = half + AHEAD
    moved = shifted[pl.ds(cap - live, span), :]
    row_ids = lax.broadcasted_iota(jnp.int32, (span, ca), 0) + first
    ext[first : BEHIND + cap, :] = jnp.where(
        row_ids[:half] < BEHIND + live, ext[first : BEHIND + cap, :], moved[:half]
    )
    ext[BEHIND + cap :, :] = moved[half:]
    low_kv = mm(ext[:BEHIND, :].astype(BF16), waqkv[:, ca:])
    keys_s[:BEHIND, :] = low_kv[:, :ca]
    values_s[:BEHIND, :] = low_kv[:, ca:]
    high_kv = mm(ext[first:, :].astype(BF16), waqkv[:, ca:])
    keys_s[first:, :] = high_kv[:, :ca]
    values_s[first:, :] = high_kv[:, ca:]
    for k in range(0, len(outer), GROUP):
        attend(outer[k : k + GROUP])

    need(waout, wagg)
    atom_mid = mid[...] + mm(att_s[...], waout[...])
    mid[...] = atom_mid
    spread = jnp.maximum(mm(atom_mid.astype(BF16), wagg[...]), 0.0).astype(BF16)
    slot_lane = lax.broadcasted_iota(jnp.int32, (1, cap), 1)
    living = slot_lane < live
    sub_ids = lax.broadcasted_iota(jnp.int32, (3 * rows, cap), 0)
    hot = ((sub_ids == relative) & living).astype(F32)
    counted = jnp.sum(hot, axis=-1, keepdims=True)
    hot_s[...] = hot.astype(BF16)
    partial = mm(hot_s[...], spread)
    few = jnp.minimum(counted, 256.0)
    lane_c = lax.broadcasted_iota(jnp.int32, (3 * rows, 128), 1)
    count_wide = jnp.where(lane_c < 64, few, counted - few)
    down = slice(rows - margin, rows)
    ahead = slice(2 * rows, 2 * rows + rim_rows)
    part_down[:, :ct] = partial[down].astype(BF16)
    part_down[:, ct:] = count_wide[down].astype(BF16)
    part_up[:, :ct] = partial[ahead].astype(BF16)
    part_up[:, ct:] = count_wide[ahead].astype(BF16)
    receive_part, finish_part = exchange(1, part_up, from_low, part_down, from_high)

    need(tsingle)
    own_sum = partial[rows : 2 * rows]
    own_count = counted[rows : 2 * rows]
    middle = slice(margin, rows - margin)
    token_mid = tsingle[middle, :].astype(F32) + own_sum[middle] / jnp.maximum(own_count[middle], 1.0)
    early_all[pl.ds(me, 1)] = normalize(token_mid).astype(BF16)[None]

    def block(kind, src, peer, sent):
        view = (early_all, late_all)[kind].at[src]
        return pltpu.make_async_remote_copy(
            src_ref=view,
            dst_ref=view,
            send_sem=sent,
            recv_sem=ag_recv.at[src, kind],
            device_id={"row": peer},
            device_id_type=pl.DeviceIdType.MESH,
        )

    def relay(kind, src, over, act):
        if over:
            act(block(kind, src, across, across_send.at[src // 4, kind]))
        act(block(kind, src, partner, ag_send.at[src // 2, kind]))

    def own_sends(kind, act):
        for there, peer, way in line:
            pl.when(there)(lambda peer=peer, way=way: act(block(kind, me, peer, line_send.at[way, kind])))
        relay(kind, me, True, act)

    def start(c):
        c.start()

    def end(c):
        c.wait_send()

    own_sends(0, start)

    need(pmask, tbias)
    pair = 2 * rows
    allowed = pmask[...] == 1
    front = lax.broadcasted_iota(jnp.int32, (1, 2 * pair), 1) < pair
    for h in range(TH):
        masked = jnp.where(allowed, tbias[h], masked_score)
        for k in range(depth // 2):
            one = masked[:, 4 * k * pair : (4 * k + 2) * pair]
            two = masked[:, (4 * k + 2) * pair : (4 * k + 4) * pair]
            here = slice(2 * k * pair, (2 * k + 2) * pair)
            bias_half[0, h, :, here] = jnp.where(front, one, pltpu.roll(two, pair, 1))
            bias_half[1, h, :, here] = jnp.where(front, pltpu.roll(one, pair, 1), two)
    mid_t = mid[...].T
    need(wtqkv, wgate)
    receive_part()
    low = from_low[...].astype(F32)
    high = from_high[...].astype(F32)

    def counts_in(sums):
        return sums[:, ct : ct + 1] + sums[:, ct + 64 : ct + 65]

    def edges(own, below, above):
        return jnp.concatenate(
            [own[:rim_rows] + below, own[rim_rows : rows - margin], own[rows - margin :] + above], axis=0
        )

    token_sum = edges(own_sum, low[:, :ct], high[:, :ct])
    token_count = edges(own_count, counts_in(low), counts_in(high))
    token_in = tsingle[...].astype(F32) + token_sum / jnp.maximum(token_count, 1.0)
    u_wide = normalize(token_in)
    u = u_wide.astype(BF16)
    chunks = ct // 128
    odd = [u_wide[margin : margin + 1, 128 * k : 128 * (k + 1)] for k in range(chunks)]
    odd.append(jnp.zeros((rim_rows - chunks, 128), F32))
    late = jnp.concatenate(
        [
            jnp.concatenate([u_wide[rows - margin :], u_wide[:margin]], axis=0),
            jnp.concatenate(odd, axis=0),
        ],
        axis=1,
    )
    late_all[pl.ds(me, 1)] = late.astype(BF16)[None]
    own_sends(1, start)

    direct = []
    crossed = []
    for d in range(1, depth):
        over = d < ends
        direct.append((z >= d, index_of(z - d, y, core), over))
        direct.append((z + d < depth, index_of(z + d, y, core), over))
    crossed.append((None, across, False))
    for d in range(1, depth):
        crossed.append((z >= d, index_of(z - d, 1 - y, core), False))
        crossed.append((z + d < depth, index_of(z + d, 1 - y, core), False))
    steps = direct + crossed

    def arrive(kind, src, over):
        block(kind, src, partner, ag_send.at[0, kind]).wait_recv()
        relay(kind, src, over, start)

    def leave(kind, src, over):
        relay(kind, src, over, end)

    def each(kind, some, visit):
        for there, src, over in some:
            if there is None:
                visit(kind, src, over)
            else:
                pl.when(there)(lambda src=src, over=over: visit(kind, src, over))

    def last_hops(column):
        for zz in range(depth):
            for kind in range(2):
                block(kind, index_of(zz, column, 1 - core), partner, ag_send.at[0, kind]).wait_recv()

    first_row = lax.broadcasted_iota(jnp.int32, (margin, ct), 0) == 0

    def assemble(side, column):
        for zz in range(depth):
            for cc in range(2):
                src = index_of(zz, column, cc)
                at = (2 * zz + cc) * rows
                early_rows = early_all[src]
                late_rows = late_all[src]
                u_half[side, at : at + margin, :] = late_rows[margin:, :ct]
                u_half[side, at + rows - margin : at + rows, :] = late_rows[:margin, :ct]
                extra = late_rows[:, ct:].astype(F32)
                row = jnp.concatenate([extra[k : k + 1] for k in range(chunks)], axis=1)
                tile = early_rows[:margin].astype(F32)
                u_half[side, at + margin : at + 2 * margin, :] = jnp.where(first_row, row, tile).astype(BF16)
                u_half[side, at + 2 * margin : at + rows - margin, :] = early_rows[margin:]

    each(0, direct[:2], arrive)
    tw = ct // TH
    tquery = (mm(u, wtqkv[:, :ct]) * (1.0 / tw**0.5)).astype(BF16)
    batches = []
    for first_head in range(0, TH, BATCH):
        heads = range(first_head, first_head + BATCH)
        left = first_head * tw // 128 * 128
        right = -(-(first_head + BATCH) * tw // 128) * 128
        lanes = [lanes_between(right - left, h * tw - left, (h + 1) * tw - left) for h in heads]
        q = tquery[:, left:right]
        wide = jnp.concatenate([q * m.astype(BF16) for m in lanes], axis=0)
        through = mm_t(wide, wtqkv[:, ct + left : ct + right]).astype(BF16)
        batches.append((first_head, left, right, lanes, through))
    gate = jax.nn.sigmoid(mm(u, wgate[...]))
    each(0, direct[2:], arrive)
    each(1, direct, arrive)
    last_hops(y)
    assemble(0, y)

    def scored(side, column):
        features = u_half[side]
        bias = bias_half[column]
        scores = []
        for first_head, _, _, _, through in batches:
            score = mm_t(through, features)
            scores.append(score + bias[first_head : first_head + BATCH].reshape(score.shape))
        return features, scores

    def valued(features, exps):
        mixed = [mm(e.astype(BF16), features).astype(BF16) for e in exps]
        return [
            mm(m, wtqkv[:, 2 * ct + left : 2 * ct + right]) for m, (_, left, right, _, _) in zip(mixed, batches)
        ]

    features, scores = scored(0, y)
    own_max = [jnp.max(score, axis=-1, keepdims=True) for score in scores]
    exps = [jnp.exp(score - m) for score, m in zip(scores, own_max)]
    own_total = [jnp.sum(e, axis=-1, keepdims=True) for e in exps]
    for k, out in enumerate(valued(features, exps)):
        own_out[k] = out
    each(0, crossed, arrive)
    each(1, crossed, arrive)
    last_hops(1 - y)
    assemble(1, 1 - y)
    need(wtout, wback, wpos)
    features, scores = scored(1, 1 - y)
    all_max = [jnp.maximum(m, jnp.max(score, axis=-1, keepdims=True)) for score, m in zip(scores, own_max)]
    exps = [jnp.exp(score - m) for score, m in zip(scores, all_max)]
    outs = valued(features, exps)
    blocks = [None] * chunks
    for k, (_, left, right, lanes, _) in enumerate(batches):
        scale = jnp.exp(own_max[k] - all_max[k])
        share = 1.0 / (own_total[k] * scale + jnp.sum(exps[k], axis=-1, keepdims=True))
        out = own_out[k] * (scale * share) + outs[k] * share
        total = out[:rows] * lanes[0]
        for h in range(1, BATCH):
            total = total + out[h * rows : (h + 1) * rows] * lanes[h]
        for c in range(left // 128, right // 128):
            part = total[:, 128 * c - left : 128 * (c + 1) - left]
            blocks[c] = part if blocks[c] is None else blocks[c] + part
    gated = (gate * jnp.concatenate(blocks, axis=1)).astype(BF16)
    token_out = (token_in + mm(gated, wtout[...])).astype(BF16)
    tout_ref[...] = token_out
    near[rows : 2 * rows, :] = mm(token_out, wback[...]).astype(BF16)
    upper = near.at[2 * rows - margin : 2 * rows]
    lower = near.at[rows : rows + rim_rows]
    receive_back, finish_back = exchange(
        2, upper, near.at[rows - margin : rows], lower, near.at[2 * rows : 2 * rows + rim_rows]
    )
    finish_rim()
    finish_part()
    for kind in range(2):
        own_sends(kind, end)
        each(kind, steps, leave)
    receive_back()
    back_t = lax.dot_general(near[...], hot_s[...], (((0,), (0,)), ((), ())), preferred_element_type=F32)
    atom_last = mid_t + back_t
    center = atom_last - jnp.mean(atom_last, axis=0, keepdims=True)
    width = jnp.mean(center * center, axis=0, keepdims=True)
    final = (center * lax.rsqrt(width + 1e-05)).astype(BF16)
    update = mm(wpos[...], final)
    den_ref[...] = jnp.where(living, skip_scale * noisy + output_scale * update, 0.0)
    finish_back()


def store(den, tout, den_h, tout_h, sem):
    copies = [pltpu.make_async_copy(den, den_h, sem.at[0]), pltpu.make_async_copy(tout, tout_h, sem.at[1])]
    for c in copies:
        c.start()
    for c in copies:
        c.wait()


def on_device(
    positions, noise, atom_single, atom_token, atom_counts, window_offsets, atom_bias,
    token_single, token_bias, pair_mask, w_coord, w_atom_qkv, w_atom_out, w_agg,
    w_tok_qkv, w_tok_gate, w_tok_out, w_back, w_pos,
):
    n = lax.axis_size("row")
    cap, ca = atom_single.shape
    rows, ct = token_single.shape
    big = (
        positions, noise, atom_single, atom_token, atom_bias, token_single,
        token_bias, pair_mask, w_coord, w_atom_qkv, w_atom_out, w_agg, w_tok_qkv, w_tok_gate,
        w_tok_out, w_back, w_pos,
    )
    margin = rows // 4
    send_up, send_down = (2 * margin, ct + 128), (margin, ct + 128)
    hbm = pl.BlockSpec(memory_space=pltpu.HBM)
    vmem = pl.BlockSpec(memory_space=pltpu.VMEM)
    out_shapes = (((positions.shape[0], cap), F32), ((rows, ct), BF16))
    results = pl.pallas_call(
        lambda *refs: kernel(n, *refs),
        out_shape=tuple(pltpu.VMEM(shape, kind) for shape, kind in out_shapes),
        in_specs=[pl.BlockSpec(memory_space=pltpu.SMEM)] + [hbm] * (1 + len(big)),
        out_specs=(vmem, vmem),
        scratch_shapes=[pltpu.SMEM(window_offsets.shape, jnp.int32)]
        + [pltpu.VMEM(a.shape, a.dtype) for a in big]
        + [
            pltpu.VMEM((128, cap), F32),
            pltpu.VMEM((cap, ca), F32),
            pltpu.VMEM((BEHIND, ca), BF16),
            pltpu.VMEM((AHEAD, ca), BF16),
            pltpu.VMEM((BEHIND, ca), BF16),
            pltpu.VMEM((AHEAD, ca), BF16),
            pltpu.VMEM((cap + AHEAD, ca), F32),
            pltpu.VMEM((BEHIND + cap + AHEAD, ca), F32),
            pltpu.VMEM((BEHIND + cap + AHEAD, ca), F32),
            pltpu.VMEM((BEHIND + cap + AHEAD, ca), F32),
            pltpu.VMEM((cap, ca), F32),
            pltpu.VMEM((cap, ca), BF16),
            pltpu.VMEM(send_down, BF16),
            pltpu.VMEM(send_up, BF16),
            pltpu.VMEM(send_up, BF16),
            pltpu.VMEM(send_down, BF16),
            pltpu.VMEM((n, rows - 2 * margin, ct), BF16),
            pltpu.VMEM((n, 2 * margin, ct + 128), BF16),
            pltpu.VMEM((2, n * rows // 2, ct), BF16),
            pltpu.VMEM((2, TH, rows, n * rows // 2), F32),
            pltpu.VMEM((TH // BATCH, BATCH * rows, 256), F32),
            pltpu.VMEM((3 * rows, cap), BF16),
            pltpu.VMEM((3 * rows, ca), BF16),
            pltpu.SemaphoreType.DMA((1 + len(big),)),
            pltpu.SemaphoreType.DMA((6,)),
            pltpu.SemaphoreType.DMA((6,)),
            pltpu.SemaphoreType.DMA((n // 4, 2)),
            pltpu.SemaphoreType.DMA((n // 4, 2)),
            pltpu.SemaphoreType.DMA((n // 2, 2)),
            pltpu.SemaphoreType.DMA((n, 2)),
        ],
        compiler_params=pltpu.CompilerParams(collective_id=0, has_side_effects=True, vmem_limit_bytes=VMEM_LIMIT),
    )(atom_counts, *(pltpu.with_memory_space_constraint(a, pltpu.HBM) for a in (window_offsets,) + big))
    results = tuple(pltpu.with_memory_space_constraint(a, pltpu.VMEM) for a in results)
    return pl.pallas_call(
        store,
        out_shape=tuple(jax.ShapeDtypeStruct(shape, kind) for shape, kind in out_shapes),
        in_specs=[vmem, vmem],
        out_specs=(hbm, hbm),
        scratch_shapes=[pltpu.SemaphoreType.DMA((2,))],
    )(*results)


def solution(mesh):
    placed = (
        P(None, ("grp", "row")),
        P(None, ("grp", "row")),
        P(("grp", "row"), None),
        P(("grp", "row")),
        P(("grp", "row")),
        P(("grp", "row")),
        P(None, ("grp", "row"), None),
        P(("grp", "row"), None),
        P(None, ("grp", "row"), None),
        P(("grp", "row"), None),
    ) + (P(),) * 9
    return jax.shard_map(
        on_device,
        mesh=mesh,
        in_specs=placed,
        out_specs=(P(None, ("grp", "row")), P(("grp", "row"), None)),
        check_vma=False,
    )
```

```python
import jax
import jax.numpy as jnp
from jax import lax
from jax.experimental import pallas as pl
from jax.experimental.pallas import tpu as pltpu
from jax.sharding import PartitionSpec as P

AH = 4
TH = 16
QWIN = 32
KWIN = 128
BEHIND = KWIN // 2
AHEAD = KWIN - QWIN

noise_level = 2.0
input_scale = 1.0 / 5.0**0.5
skip_scale = 1.0 / 5.0
output_scale = 2.0 / 5.0**0.5
masked_score = -1e30

F32 = jnp.float32
BF16 = jnp.bfloat16
GROUP = 4
BATCH = 4
VMEM_LIMIT = 40 * 1024 * 1024


def normalize(values):
    center = values - jnp.mean(values, axis=-1, keepdims=True)
    spread = jnp.mean(center * center, axis=-1, keepdims=True)
    return center * lax.rsqrt(spread + 1e-05)


def mm(a, b):
    return jnp.dot(a, b, preferred_element_type=F32)


def mm_t(a, b):
    return lax.dot_general(a, b, (((1,), (1,)), ((), ())), preferred_element_type=F32)


def lanes_between(width, low, high):
    lane = lax.broadcasted_iota(jnp.int32, (1, width), 1)
    return ((lane >= low) & (lane < high)).astype(F32)


def kernel(
    n,
    counts_s, offsets_h,
    pos_h, noise_h, single_h, token_h, abias_h, tsingle_h, tbias_h, mask_h,
    wcoord_h, waqkv_h, waout_h, wagg_h, wtqkv_h, wgate_h, wtout_h, wback_h, wpos_h,
    den_ref, tout_ref,
    offsets_s,
    pos, noise, single, token, abias, tsingle, tbias, pmask,
    wcoord, waqkv, waout, wagg, wtqkv, wgate, wtout, wback, wpos,
    columns, hs, tail, head, lo, up, shifted, queries, keys_s, values_s, mid, att_s,
    part_down, part_up, from_low, from_high, early_all, late_all, u_half, bias_half, hot_s, near,
    local_sem, edge_recv, line_recv, cross_early, cross_late, pair_recv, ready,
):
    cap, ca = single.shape
    rows, ct = tsingle.shape
    margin = rows // 4
    rim_rows = 2 * margin
    me = lax.axis_index("row")
    last = n - 1
    has_low = me > 0
    has_high = me < last

    pairs = [
        (pos_h, pos), (noise_h, noise), (single_h, single), (wcoord_h, wcoord), (token_h, token),
        (waqkv_h, waqkv), (abias_h, abias), (waout_h, waout), (wagg_h, wagg), (tsingle_h, tsingle),
        (wtqkv_h, wtqkv), (wgate_h, wgate), (mask_h, pmask), (tbias_h, tbias), (wtout_h, wtout),
        (wback_h, wback), (wpos_h, wpos), (offsets_h, offsets_s),
    ]
    copies = {}
    for k, (src, dst) in enumerate(pairs):
        copies[id(dst)] = pltpu.make_async_copy(src, dst, local_sem.at[k])
        copies[id(dst)].start()

    def need(*refs):
        for r in refs:
            copies[id(r)].wait()

    core = lax.rem(me, 2)
    y = lax.rem(me // 2, 2)
    z = me // 4
    depth = n // 4

    def index_of(zz, yy, cc):
        return zz * 4 + yy * 2 + cc

    partner = index_of(z, y, 1 - core)
    across = index_of(z, 1 - y, core)
    line = []
    for d in range(1, depth):
        line.append((z + d < depth, index_of(z + d, y, core), False))
        line.append((z >= d, index_of(z - d, y, core), False))

    ends = depth - 1
    if ends:
        line.append((z == 0, index_of(z + ends, 1 - y, core), True))
        line.append((z == ends, index_of(z - ends, 1 - y, core), True))

    barrier = pltpu.get_barrier_semaphore()

    def greet(peer):
        pl.semaphore_signal(
            barrier, inc=1, device_id={"row": peer}, device_id_type=pl.DeviceIdType.MESH
        )

    greet(partner)
    greet(across)
    beside = [(z >= 1, index_of(z - 1, y, core)), (z + 1 < depth, index_of(z + 1, y, core))]
    for there, peer in beside:
        pl.when(there)(lambda peer=peer: greet(peer))
    far = me - 1 + 2 * core
    has_far = (far >= 0) & (far < n)
    pl.when(has_far)(lambda: greet(far))

    shifted[...] = jnp.zeros_like(shifted)
    columns[...] = jnp.zeros_like(columns)
    near[...] = jnp.zeros_like(near)

    @pl.when(me == 0)
    def _():
        lo[...] = jnp.zeros_like(lo)
        from_low[...] = jnp.zeros_like(from_low)

    @pl.when(me == last)
    def _():
        up[...] = jnp.zeros_like(up)
        from_high[...] = jnp.zeros_like(from_high)

    need(pos, noise, single, wcoord, token)
    live = jnp.clip(counts_s[0], cap // 2, cap)
    noisy = pos[...] + noise_level * noise[...]
    columns[0:3, :] = input_scale * noisy
    relative = token[...].reshape(1, cap) - (me - 1) * rows
    turned = columns[...].T
    wc = wcoord[...]
    atom_start = single[...].astype(F32) + (
        turned[:, 0:1] * wc[0:1, :] + turned[:, 1:2] * wc[1:2, :] + turned[:, 2:3] * wc[2:3, :]
    )
    normed = normalize(atom_start)
    hs[...] = normed
    mid[...] = atom_start
    head[...] = normed[:AHEAD].astype(BF16)
    tail[...] = hs[pl.ds(live - BEHIND, BEHIND), :].astype(BF16)

    links = jnp.where(z >= 1, 1, 0) + jnp.where(z + 1 < depth, 1, 0) + 1
    peers = 1 + links + jnp.where(has_far, 1, 0)
    pl.semaphore_wait(barrier, peers)

    def edge(stage, way, src, dst, peer):
        return pltpu.make_async_remote_copy(
            src_ref=src,
            dst_ref=dst,
            send_sem=local_sem.at[2 + way],
            recv_sem=edge_recv.at[2 * (stage % 2) + way],
            device_id={"row": peer},
            device_id_type=pl.DeviceIdType.MESH,
        )

    def exchange(stage, src_up, dst_up, src_down, dst_down):
        going_up = edge(stage, 0, src_up, dst_up, me + 1)
        going_down = edge(stage, 1, src_down, dst_down, me - 1)
        pl.when(has_high)(going_up.start)
        pl.when(has_low)(going_down.start)

        def receive_low():
            pl.when(has_low)(going_up.wait_recv)

        def receive_high():
            pl.when(has_high)(going_down.wait_recv)

        def finish():
            pl.when(has_high)(going_up.wait_send)
            pl.when(has_low)(going_down.wait_send)

        return receive_low, receive_high, finish

    rim_low, rim_high, finish_rim = exchange(0, tail, lo, head, up)

    def tell(step):
        def one(peer):
            pl.semaphore_signal(
                ready.at[step], inc=1, device_id={"row": peer}, device_id_type=pl.DeviceIdType.MESH
            )

        one(across)
        for there, peer in beside:
            pl.when(there)(lambda peer=peer: one(peer))

    def hear(step):
        pl.semaphore_wait(ready.at[step], links)

    rounds = depth - 1
    if rounds:
        tell(0)
    need(waqkv)
    hw = ca // AH
    normed_b = normed.astype(BF16)
    own = mm(normed_b, waqkv[...])
    queries[...] = (own[:, :ca] * (1.0 / hw**0.5)).astype(BF16)
    head_lanes = [lanes_between(ca, h * hw, (h + 1) * hw) for h in range(AH)]
    keys_s[BEHIND : BEHIND + cap, :] = own[:, ca : 2 * ca]
    values_s[BEHIND : BEHIND + cap, :] = own[:, 2 * ca :]
    need(abias, offsets_s, waout, wagg)

    top = jnp.where(has_high, BEHIND + live + AHEAD, BEHIND + live)
    bottom = jnp.where(has_low, 0, BEHIND)
    lane_key = lax.broadcasted_iota(jnp.int32, (1, KWIN), 1)
    ones = jnp.ones((KWIN, ca), BF16)

    def attend(windows):
        at = [BEHIND + QWIN * w + offsets_s[w] for w in windows]
        scores = []
        for w, start in zip(windows, at):
            key = keys_s[pl.ds(start, KWIN), :].astype(BF16)
            q = queries[w * QWIN : (w + 1) * QWIN, :]
            wide = jnp.concatenate([q * m.astype(BF16) for m in head_lanes], axis=0)
            scores.append(mm_t(wide, key))
        exps = []
        for w, start, score in zip(windows, at, scores):
            score = score + abias[:, w * QWIN : (w + 1) * QWIN, :].reshape(AH * QWIN, KWIN)
            keys = lane_key + start
            score = jnp.where((keys >= bottom) & (keys < top), score, masked_score)
            exps.append(jnp.exp(score - jnp.max(score, axis=-1, keepdims=True)).astype(BF16))
        outs = []
        for start, e in zip(at, exps):
            value = values_s[pl.ds(start, KWIN), :].astype(BF16)
            outs.append(mm(e, jnp.concatenate([value, ones], axis=1)))
        for w, out in zip(windows, outs):
            mixed = out[:QWIN] * wide_lanes[0]
            for h in range(1, AH):
                mixed = mixed + out[h * QWIN : (h + 1) * QWIN] * wide_lanes[h]
            att_s[w * QWIN : (w + 1) * QWIN, :] = (mixed[:, :ca] / mixed[:, ca:]).astype(BF16)

    wide_lanes = [jnp.concatenate([m, m], axis=1) for m in head_lanes]
    half = cap // 2
    count = cap // QWIN
    behind_windows = BEHIND // QWIN
    inner = [w for w in range(count) if w >= behind_windows and QWIN * w + AHEAD <= half]
    below = range(behind_windows)
    above = range(inner[-1] + 1, count)
    first = BEHIND + half
    span = half + AHEAD
    attend(inner)
    if rounds > 1:
        hear(0)
        tell(1)

    def with_low():
        rim_low()
        low_kv = mm(lo[...], waqkv[:, ca:])
        keys_s[:BEHIND, :] = low_kv[:, :ca]
        values_s[:BEHIND, :] = low_kv[:, ca:]
        attend(below)

    def with_high():
        rim_high()
        shifted[half : half + AHEAD, :] = up[...].astype(F32)
        moved = shifted[pl.ds(cap - live, span), :]
        row_ids = lax.broadcasted_iota(jnp.int32, (half, ca), 0) + first
        merged = jnp.where(row_ids < BEHIND + live, hs[half:cap, :], moved[:half])
        high_rows = jnp.concatenate([merged, moved[half:]], axis=0).astype(BF16)
        high_kv = mm(high_rows, waqkv[:, ca:])
        keys_s[first:, :] = high_kv[:, :ca]
        values_s[first:, :] = high_kv[:, ca:]
        for k in range(0, len(above), GROUP):
            attend(above[k : k + GROUP])

    pl.when(core == 0)(with_high)
    if rounds > 2:
        hear(1)
        tell(2)
    with_low()
    pl.when(core == 1)(with_high)
    finish_rim()
    atom_mid = mid[...] + mm(att_s[...], waout[...])
    mid[...] = atom_mid
    spread = jnp.maximum(mm(atom_mid.astype(BF16), wagg[...]), 0.0).astype(BF16)
    slot_lane = lax.broadcasted_iota(jnp.int32, (1, cap), 1)
    living = slot_lane < live
    sub_ids = lax.broadcasted_iota(jnp.int32, (3 * rows, cap), 0)
    hot = ((sub_ids == relative) & living).astype(F32)
    counted = jnp.sum(hot, axis=-1, keepdims=True)
    hot_s[...] = hot.astype(BF16)
    partial = mm(hot_s[...], spread)
    few = jnp.minimum(counted, 256.0)
    lane_c = lax.broadcasted_iota(jnp.int32, (3 * rows, 128), 1)
    count_wide = jnp.where(lane_c < 64, few, counted - few)
    down = slice(rows - margin, rows)
    ahead = slice(2 * rows, 2 * rows + rim_rows)
    part_down[:, :ct] = partial[down].astype(BF16)
    part_down[:, ct:] = count_wide[down].astype(BF16)
    part_up[:, :ct] = partial[ahead].astype(BF16)
    part_up[:, ct:] = count_wide[ahead].astype(BF16)
    part_low, part_high, finish_part = exchange(1, part_up, from_low, part_down, from_high)

    need(tsingle)
    own_sum = partial[rows : 2 * rows]
    own_count = counted[rows : 2 * rows]
    middle = slice(margin, rows - margin)
    token_mid = tsingle[middle, :].astype(F32) + own_sum[middle] / jnp.maximum(own_count[middle], 1.0)
    early_all[pl.ds(me, 1)] = normalize(token_mid).astype(BF16)[None]

    messages = (early_all, late_all)

    def block(kind, src, peer, arrived, count=None):
        view = messages[kind].at[src if count is None else pl.ds(0, count)]
        return pltpu.make_async_remote_copy(
            src_ref=view,
            dst_ref=view,
            send_sem=local_sem.at[kind],
            recv_sem=arrived,
            device_id={"row": peer},
            device_id_type=pl.DeviceIdType.MESH,
        )

    def crossing(kind, zz):
        return cross_late.at[zz] if kind else cross_early.at[0]

    def relay(kind, src, over):
        if over:
            block(kind, src, across, crossing(kind, src // 4)).start()
        block(kind, src, partner, pair_recv.at[0, kind]).start()

    def own_sends(kind):
        for there, peer, diagonal in (line if kind == 0 else line[2:-2] + line[-2:] + line[:2]):
            arrived = crossing(kind, z) if diagonal else line_recv.at[z, kind]
            pl.when(there)(lambda peer=peer, arrived=arrived: block(kind, me, peer, arrived).start())
        relay(kind, me, True)

    for step in range(min(rounds - 1, 2), rounds):
        hear(step)
        if step + 1 < rounds:
            tell(step + 1)
    own_sends(0)

    need(pmask, tbias)
    pair = 2 * rows
    allowed = pmask[...] == 1
    front = lax.broadcasted_iota(jnp.int32, (1, 2 * pair), 1) < pair
    for h in range(TH):
        masked = jnp.where(allowed, tbias[h], masked_score)
        for k in range(depth // 2):
            one = masked[:, 4 * k * pair : (4 * k + 2) * pair]
            two = masked[:, (4 * k + 2) * pair : (4 * k + 4) * pair]
            here = slice(2 * k * pair, (2 * k + 2) * pair)
            bias_half[0, h, :, here] = jnp.where(front, one, pltpu.roll(two, pair, 1))
            bias_half[1, h, :, here] = jnp.where(front, pltpu.roll(one, pair, 1), two)
    mid_t = mid[...].T
    need(wtqkv, wgate, wtout, wback, wpos)
    joint = mm(wtout[...], wback[...]).astype(BF16)
    part_low()
    part_high()
    low = from_low[...].astype(F32)
    high = from_high[...].astype(F32)

    def counts_in(sums):
        return sums[:, ct : ct + 1] + sums[:, ct + 64 : ct + 65]

    def edges(own, below, above):
        return jnp.concatenate(
            [own[:rim_rows] + below, own[rim_rows : rows - margin], own[rows - margin :] + above], axis=0
        )

    token_sum = edges(own_sum, low[:, :ct], high[:, :ct])
    token_count = edges(own_count, counts_in(low), counts_in(high))
    token_in = tsingle[...].astype(F32) + token_sum / jnp.maximum(token_count, 1.0)
    u_wide = normalize(token_in)
    u = u_wide.astype(BF16)
    chunks = ct // 128
    odd = [u_wide[margin : margin + 1, 128 * k : 128 * (k + 1)] for k in range(chunks)]
    odd.append(jnp.zeros((rim_rows - chunks, 128), F32))
    late = jnp.concatenate(
        [
            jnp.concatenate([u_wide[rows - margin :], u_wide[:margin]], axis=0),
            jnp.concatenate(odd, axis=0),
        ],
        axis=1,
    )
    late_all[pl.ds(me, 1)] = late.astype(BF16)[None]
    own_sends(1)

    direct = []
    for d in range(1, depth):
        direct.append((z >= d, z - d, d < ends))
        direct.append((z + d < depth, z + d, d < ends))

    def arrive(kind, some):
        for there, zz, over in some:
            src = index_of(zz, y, core)

            @pl.when(there)
            def _(src=src, zz=zz, over=over):
                block(kind, src, partner, line_recv.at[zz, kind]).wait_recv()
                relay(kind, src, over)

    def crossed_late(there, zz):
        src = index_of(zz, 1 - y, core)

        @pl.when(there)
        def _():
            block(1, src, partner, cross_late.at[zz]).wait_recv()
            block(1, src, partner, pair_recv.at[1, 1]).start()

    def crossed_early():
        block(0, 0, across, cross_early.at[0], depth).wait_recv()
        for zz in range(depth):
            block(0, index_of(zz, 1 - y, core), partner, pair_recv.at[1, 0]).start()

    def last_hops(side):
        for kind in range(2):
            block(kind, 0, partner, pair_recv.at[side, kind], depth).wait_recv()

    first_row = lax.broadcasted_iota(jnp.int32, (margin, ct), 0) == 0

    def assemble(side, column):
        for zz in range(depth):
            for cc in range(2):
                src = index_of(zz, column, cc)
                at = (2 * zz + cc) * rows
                early_rows = early_all[src]
                late_rows = late_all[src]
                u_half[side, at : at + margin, :] = late_rows[margin:, :ct]
                u_half[side, at + rows - margin : at + rows, :] = late_rows[:margin, :ct]
                extra = late_rows[:, ct:].astype(F32)
                row = jnp.concatenate([extra[k : k + 1] for k in range(chunks)], axis=1)
                tile = early_rows[:margin].astype(F32)
                u_half[side, at + margin : at + 2 * margin, :] = jnp.where(first_row, row, tile).astype(BF16)
                u_half[side, at + 2 * margin : at + rows - margin, :] = early_rows[margin:]

    arrive(0, direct[:2])
    tw = ct // TH
    tquery = (mm(u, wtqkv[:, :ct]) * (1.0 / tw**0.5)).astype(BF16)
    batches = []
    for first_head in range(0, TH, BATCH):
        heads = range(first_head, first_head + BATCH)
        left = first_head * tw // 128 * 128
        right = -(-(first_head + BATCH) * tw // 128) * 128
        lanes = [lanes_between(right - left, h * tw - left, (h + 1) * tw - left) for h in heads]
        q = tquery[:, left:right]
        wide = jnp.concatenate([q * m.astype(BF16) for m in lanes], axis=0)
        through = mm_t(wide, wtqkv[:, ct + left : ct + right]).astype(BF16)
        batches.append((first_head, left, right, lanes, through))
    gate = jax.nn.sigmoid(mm(u, wgate[...]))
    back_in = mm(token_in.astype(BF16), wback[...])
    arrive(0, direct[2:])
    arrive(1, direct)
    crossed_early()
    crossed_late(True, z)
    last_hops(0)
    assemble(0, y)

    def scored(features, column, some):
        bias = bias_half[column]
        scores = []
        for first_head, _, _, _, through in some:
            score = mm_t(through, features)
            scores.append(score + bias[first_head : first_head + BATCH].reshape(score.shape))
        return scores

    def valued(e, features, left, right):
        mixed = mm(e.astype(BF16), features).astype(BF16)
        return mm(mixed, wtqkv[:, 2 * ct + left : 2 * ct + right])

    features = u_half[0]
    own_max = []
    own_total = []
    own_out = []
    parts = len(batches) // 2
    for k in range(0, len(batches), parts):
        some = batches[k : k + parts]
        scores = scored(features, y, some)
        for (_, left, right, _, _), score in zip(some, scores):
            largest = jnp.max(score, axis=-1, keepdims=True)
            e = jnp.exp(score - largest)
            own_max.append(largest)
            own_total.append(jnp.sum(e, axis=-1, keepdims=True))
            own_out.append(valued(e, features, left, right))
        for d in range(1, depth):
            if (k == 0) == (d == 1):
                crossed_late(z >= d, z - d)
                crossed_late(z + d < depth, z + d)
    last_hops(1)
    assemble(1, 1 - y)
    features = u_half[1]
    scores = scored(features, 1 - y, batches)
    all_max = [jnp.maximum(m, jnp.max(score, axis=-1, keepdims=True)) for score, m in zip(scores, own_max)]
    exps = [jnp.exp(score - m) for score, m in zip(scores, all_max)]
    outs = [valued(e, features, left, right) for e, (_, left, right, _, _) in zip(exps, batches)]
    blocks = [None] * chunks
    for k, (_, left, right, lanes, _) in enumerate(batches):
        scale = jnp.exp(own_max[k] - all_max[k])
        share = 1.0 / (own_total[k] * scale + jnp.sum(exps[k], axis=-1, keepdims=True))
        out = own_out[k] * (scale * share) + outs[k] * share
        total = out[:rows] * lanes[0]
        for h in range(1, BATCH):
            total = total + out[h * rows : (h + 1) * rows] * lanes[h]
        for c in range(left // 128, right // 128):
            part = total[:, 128 * c - left : 128 * (c + 1) - left]
            blocks[c] = part if blocks[c] is None else blocks[c] + part
    gated = (gate * jnp.concatenate(blocks, axis=1)).astype(BF16)
    near[rows : 2 * rows, :] = (back_in + mm(gated, joint)).astype(BF16)
    upper = near.at[2 * rows - margin : 2 * rows]
    lower = near.at[rows : rows + rim_rows]
    finish_part()
    back_low, back_high, finish_back = exchange(
        2, upper, near.at[rows - margin : rows], lower, near.at[2 * rows : 2 * rows + rim_rows]
    )
    tout_ref[...] = (token_in + mm(gated, wtout[...])).astype(BF16)
    for kind in range(2):
        block(kind, 0, partner, pair_recv.at[0, kind], n - 1).wait_send()
    back_low()
    back_high()
    back_t = lax.dot_general(near[...], hot_s[...], (((0,), (0,)), ((), ())), preferred_element_type=F32)
    atom_last = mid_t + back_t
    center = atom_last - jnp.mean(atom_last, axis=0, keepdims=True)
    width = jnp.mean(center * center, axis=0, keepdims=True)
    final = (center * lax.rsqrt(width + 1e-05)).astype(BF16)
    update = mm(wpos[...], final)
    den_ref[...] = jnp.where(living, skip_scale * noisy + output_scale * update, 0.0)
    finish_back()


def store(den, tout, den_h, tout_h, sem):
    copies = [pltpu.make_async_copy(den, den_h, sem.at[0]), pltpu.make_async_copy(tout, tout_h, sem.at[1])]
    for c in copies:
        c.start()
    for c in copies:
        c.wait()


def on_device(
    positions, noise, atom_single, atom_token, atom_counts, window_offsets, atom_bias,
    token_single, token_bias, pair_mask, w_coord, w_atom_qkv, w_atom_out, w_agg,
    w_tok_qkv, w_tok_gate, w_tok_out, w_back, w_pos,
):
    n = lax.axis_size("row")
    cap, ca = atom_single.shape
    rows, ct = token_single.shape
    big = (
        positions, noise, atom_single, atom_token, atom_bias, token_single,
        token_bias, pair_mask, w_coord, w_atom_qkv, w_atom_out, w_agg, w_tok_qkv, w_tok_gate,
        w_tok_out, w_back, w_pos,
    )
    margin = rows // 4
    send_up, send_down = (2 * margin, ct + 128), (margin, ct + 128)
    hbm = pl.BlockSpec(memory_space=pltpu.HBM)
    vmem = pl.BlockSpec(memory_space=pltpu.VMEM)
    out_shapes = (((positions.shape[0], cap), F32), ((rows, ct), BF16))
    results = pl.pallas_call(
        lambda *refs: kernel(n, *refs),
        out_shape=tuple(pltpu.VMEM(shape, kind) for shape, kind in out_shapes),
        in_specs=[pl.BlockSpec(memory_space=pltpu.SMEM)] + [hbm] * (1 + len(big)),
        out_specs=(vmem, vmem),
        scratch_shapes=[pltpu.SMEM(window_offsets.shape, jnp.int32)]
        + [pltpu.VMEM(a.shape, a.dtype) for a in big]
        + [
            pltpu.VMEM((128, cap), F32),
            pltpu.VMEM((cap, ca), F32),
            pltpu.VMEM((BEHIND, ca), BF16),
            pltpu.VMEM((AHEAD, ca), BF16),
            pltpu.VMEM((BEHIND, ca), BF16),
            pltpu.VMEM((AHEAD, ca), BF16),
            pltpu.VMEM((cap + AHEAD, ca), F32),
            pltpu.VMEM((cap, ca), BF16),
            pltpu.VMEM((BEHIND + cap + AHEAD, ca), F32),
            pltpu.VMEM((BEHIND + cap + AHEAD, ca), F32),
            pltpu.VMEM((cap, ca), F32),
            pltpu.VMEM((cap, ca), BF16),
            pltpu.VMEM(send_down, BF16),
            pltpu.VMEM(send_up, BF16),
            pltpu.VMEM(send_up, BF16),
            pltpu.VMEM(send_down, BF16),
            pltpu.VMEM((n, rows - 2 * margin, ct), BF16),
            pltpu.VMEM((n, 2 * margin, ct + 128), BF16),
            pltpu.VMEM((2, n * rows // 2, ct), BF16),
            pltpu.VMEM((2, TH, rows, n * rows // 2), F32),
            pltpu.VMEM((3 * rows, cap), BF16),
            pltpu.VMEM((3 * rows, ca), BF16),
            pltpu.SemaphoreType.DMA((1 + len(big),)),
            pltpu.SemaphoreType.DMA((4,)),
            pltpu.SemaphoreType.DMA((n // 4, 2)),
            pltpu.SemaphoreType.DMA((1,)),
            pltpu.SemaphoreType.DMA((n // 4,)),
            pltpu.SemaphoreType.DMA((2, 2)),
            pltpu.SemaphoreType.REGULAR((max(n // 4 - 1, 1),)),
        ],
        compiler_params=pltpu.CompilerParams(collective_id=0, has_side_effects=True, vmem_limit_bytes=VMEM_LIMIT),
    )(atom_counts, *(pltpu.with_memory_space_constraint(a, pltpu.HBM) for a in (window_offsets,) + big))
    results = tuple(pltpu.with_memory_space_constraint(a, pltpu.VMEM) for a in results)
    return pl.pallas_call(
        store,
        out_shape=tuple(jax.ShapeDtypeStruct(shape, kind) for shape, kind in out_shapes),
        in_specs=[vmem, vmem],
        out_specs=(hbm, hbm),
        scratch_shapes=[pltpu.SemaphoreType.DMA((2,))],
    )(*results)


def solution(mesh):
    placed = (
        P(None, ("grp", "row")),
        P(None, ("grp", "row")),
        P(("grp", "row"), None),
        P(("grp", "row")),
        P(("grp", "row")),
        P(("grp", "row")),
        P(None, ("grp", "row"), None),
        P(("grp", "row"), None),
        P(None, ("grp", "row"), None),
        P(("grp", "row"), None),
    ) + (P(),) * 9
    return jax.shard_map(
        on_device,
        mesh=mesh,
        in_specs=placed,
        out_specs=(P(None, ("grp", "row")), P(("grp", "row"), None)),
        check_vma=False,
    )
```

```python
import jax
import jax.numpy as jnp
from jax import lax
from jax.experimental import pallas as pl
from jax.experimental.pallas import tpu as pltpu
from jax.sharding import PartitionSpec as P

AH = 4
TH = 16
QWIN = 32
KWIN = 128
BEHIND = KWIN // 2
AHEAD = KWIN - QWIN

noise_level = 2.0
input_scale = 1.0 / 5.0**0.5
skip_scale = 1.0 / 5.0
output_scale = 2.0 / 5.0**0.5
masked_score = -1e30

F32 = jnp.float32
BF16 = jnp.bfloat16
GROUP = 4
BATCH = 4
VMEM_LIMIT = 40 * 1024 * 1024


def normalize(values):
    center = values - jnp.mean(values, axis=-1, keepdims=True)
    spread = jnp.mean(center * center, axis=-1, keepdims=True)
    return center * lax.rsqrt(spread + 1e-05)


def mm(a, b):
    return jnp.dot(a, b, preferred_element_type=F32)


def mm_t(a, b):
    return lax.dot_general(a, b, (((1,), (1,)), ((), ())), preferred_element_type=F32)


def lanes_between(width, low, high):
    lane = lax.broadcasted_iota(jnp.int32, (1, width), 1)
    return ((lane >= low) & (lane < high)).astype(F32)


def kernel(
    n,
    counts_s, offsets_h,
    pos_h, noise_h, single_h, token_h, abias_h, tsingle_h, tbias_h, mask_h,
    wcoord_h, waqkv_h, waout_h, wagg_h, wtqkv_h, wgate_h, wtout_h, wback_h, wpos_h,
    den_ref, tout_ref,
    offsets_s,
    pos, noise, single, token, abias, tsingle, tbias, pmask,
    wcoord, waqkv, waout, wagg, wtqkv, wgate, wtout, wback, wpos,
    columns, hs, tail, head, lo, up, shifted, queries, keys_s, values_s, mid, att_s,
    part_down, part_up, from_low, from_high, early_all, late_all, u_half, bias_half, hot_s, near,
    local_sem, edge_recv, line_recv, cross_early, cross_late, pair_recv, ready,
):
    cap, ca = single.shape
    rows, ct = tsingle.shape
    margin = rows // 4
    rim_rows = 2 * margin
    me = lax.axis_index("row")
    last = n - 1
    has_low = me > 0
    has_high = me < last

    pairs = [
        (pos_h, pos), (noise_h, noise), (single_h, single), (wcoord_h, wcoord), (token_h, token),
        (waqkv_h, waqkv), (abias_h, abias), (waout_h, waout), (wagg_h, wagg), (tsingle_h, tsingle),
        (wtqkv_h, wtqkv), (wgate_h, wgate), (mask_h, pmask), (tbias_h, tbias), (wtout_h, wtout),
        (wback_h, wback), (wpos_h, wpos), (offsets_h, offsets_s),
    ]
    copies = {}
    for k, (src, dst) in enumerate(pairs):
        copies[id(dst)] = pltpu.make_async_copy(src, dst, local_sem.at[k])
        copies[id(dst)].start()

    def need(*refs):
        for r in refs:
            copies[id(r)].wait()

    core = lax.rem(me, 2)
    y = lax.rem(me // 2, 2)
    z = me // 4
    depth = n // 4

    def index_of(zz, yy, cc):
        return zz * 4 + yy * 2 + cc

    partner = index_of(z, y, 1 - core)
    across = index_of(z, 1 - y, core)
    line = []
    for d in range(1, depth):
        line.append((z + d < depth, index_of(z + d, y, core), False))
        line.append((z >= d, index_of(z - d, y, core), False))

    ends = depth - 1
    if ends:
        line.append((z == 0, index_of(z + ends, 1 - y, core), True))
        line.append((z == ends, index_of(z - ends, 1 - y, core), True))

    barrier = pltpu.get_barrier_semaphore()

    def greet(peer):
        pl.semaphore_signal(
            barrier, inc=1, device_id={"row": peer}, device_id_type=pl.DeviceIdType.MESH
        )

    greet(partner)
    greet(across)
    beside = [(z >= 1, index_of(z - 1, y, core)), (z + 1 < depth, index_of(z + 1, y, core))]
    for there, peer in beside:
        pl.when(there)(lambda peer=peer: greet(peer))
    far = me - 1 + 2 * core
    has_far = (far >= 0) & (far < n)
    pl.when(has_far)(lambda: greet(far))

    shifted[...] = jnp.zeros_like(shifted)
    columns[...] = jnp.zeros_like(columns)
    near[...] = jnp.zeros_like(near)

    @pl.when(me == 0)
    def _():
        lo[...] = jnp.zeros_like(lo)
        from_low[...] = jnp.zeros_like(from_low)

    @pl.when(me == last)
    def _():
        up[...] = jnp.zeros_like(up)
        from_high[...] = jnp.zeros_like(from_high)

    need(pos, noise, single, wcoord, token)
    live = jnp.clip(counts_s[0], cap // 2, cap)
    noisy = pos[...] + noise_level * noise[...]
    columns[0:3, :] = input_scale * noisy
    relative = token[...].reshape(1, cap) - (me - 1) * rows
    turned = columns[...].T
    wc = wcoord[...]
    atom_start = single[...].astype(F32) + (
        turned[:, 0:1] * wc[0:1, :] + turned[:, 1:2] * wc[1:2, :] + turned[:, 2:3] * wc[2:3, :]
    )
    normed = normalize(atom_start)
    hs[...] = normed
    mid[...] = atom_start
    head[...] = normed[:AHEAD].astype(BF16)
    tail[...] = hs[pl.ds(live - BEHIND, BEHIND), :].astype(BF16)

    links = jnp.where(z >= 1, 1, 0) + jnp.where(z + 1 < depth, 1, 0) + 1
    peers = 1 + links + jnp.where(has_far, 1, 0)
    pl.semaphore_wait(barrier, peers)

    def edge(stage, way, src, dst, peer):
        return pltpu.make_async_remote_copy(
            src_ref=src,
            dst_ref=dst,
            send_sem=local_sem.at[2 + way],
            recv_sem=edge_recv.at[2 * (stage % 2) + way],
            device_id={"row": peer},
            device_id_type=pl.DeviceIdType.MESH,
        )

    def exchange(stage, src_up, dst_up, src_down, dst_down):
        going_up = edge(stage, 0, src_up, dst_up, me + 1)
        going_down = edge(stage, 1, src_down, dst_down, me - 1)
        pl.when(has_high)(going_up.start)
        pl.when(has_low)(going_down.start)

        def receive_low():
            pl.when(has_low)(going_up.wait_recv)

        def receive_high():
            pl.when(has_high)(going_down.wait_recv)

        def finish():
            pl.when(has_high)(going_up.wait_send)
            pl.when(has_low)(going_down.wait_send)

        return receive_low, receive_high, finish

    rim_low, rim_high, finish_rim = exchange(0, tail, lo, head, up)

    def tell(step):
        def one(peer):
            pl.semaphore_signal(
                ready.at[step], inc=1, device_id={"row": peer}, device_id_type=pl.DeviceIdType.MESH
            )

        one(across)
        for there, peer in beside:
            pl.when(there)(lambda peer=peer: one(peer))

    def hear(step):
        pl.semaphore_wait(ready.at[step], links)

    rounds = depth - 1
    if rounds:
        tell(0)
    need(waqkv)
    hw = ca // AH
    normed_b = normed.astype(BF16)
    own = mm(normed_b, waqkv[...])
    queries[...] = (own[:, :ca] * (1.0 / hw**0.5)).astype(BF16)
    head_lanes = [lanes_between(ca, h * hw, (h + 1) * hw) for h in range(AH)]
    keys_s[BEHIND : BEHIND + cap, :] = own[:, ca : 2 * ca]
    values_s[BEHIND : BEHIND + cap, :] = own[:, 2 * ca :]
    need(abias, offsets_s, waout, wagg)

    top = jnp.where(has_high, BEHIND + live + AHEAD, BEHIND + live)
    bottom = jnp.where(has_low, 0, BEHIND)
    lane_key = lax.broadcasted_iota(jnp.int32, (1, KWIN), 1)
    ones = jnp.ones((KWIN, ca), BF16)

    def attend(windows):
        at = [BEHIND + QWIN * w + offsets_s[w] for w in windows]
        scores = []
        for w, start in zip(windows, at):
            key = keys_s[pl.ds(start, KWIN), :].astype(BF16)
            q = queries[w * QWIN : (w + 1) * QWIN, :]
            wide = jnp.concatenate([q * m.astype(BF16) for m in head_lanes], axis=0)
            scores.append(mm_t(wide, key))
        exps = []
        for w, start, score in zip(windows, at, scores):
            score = score + abias[:, w * QWIN : (w + 1) * QWIN, :].reshape(AH * QWIN, KWIN)
            keys = lane_key + start
            score = jnp.where((keys >= bottom) & (keys < top), score, masked_score)
            exps.append(jnp.exp(score - jnp.max(score, axis=-1, keepdims=True)).astype(BF16))
        outs = []
        for start, e in zip(at, exps):
            value = values_s[pl.ds(start, KWIN), :].astype(BF16)
            outs.append(mm(e, jnp.concatenate([value, ones], axis=1)))
        for w, out in zip(windows, outs):
            mixed = out[:QWIN] * wide_lanes[0]
            for h in range(1, AH):
                mixed = mixed + out[h * QWIN : (h + 1) * QWIN] * wide_lanes[h]
            att_s[w * QWIN : (w + 1) * QWIN, :] = (mixed[:, :ca] / mixed[:, ca:]).astype(BF16)

    wide_lanes = [jnp.concatenate([m, m], axis=1) for m in head_lanes]
    half = cap // 2
    count = cap // QWIN
    behind_windows = BEHIND // QWIN
    inner = [w for w in range(count) if w >= behind_windows and QWIN * w + AHEAD <= half]
    below = range(behind_windows)
    above = range(inner[-1] + 1, count)
    first = BEHIND + half
    span = half + AHEAD
    attend(inner)
    if rounds > 1:
        hear(0)
        tell(1)

    def with_low():
        rim_low()
        low_kv = mm(lo[...], waqkv[:, ca:])
        keys_s[:BEHIND, :] = low_kv[:, :ca]
        values_s[:BEHIND, :] = low_kv[:, ca:]
        attend(below)

    def with_high():
        rim_high()
        shifted[half : half + AHEAD, :] = up[...].astype(F32)
        moved = shifted[pl.ds(cap - live, span), :]
        row_ids = lax.broadcasted_iota(jnp.int32, (half, ca), 0) + first
        merged = jnp.where(row_ids < BEHIND + live, hs[half:cap, :], moved[:half])
        high_rows = jnp.concatenate([merged, moved[half:]], axis=0).astype(BF16)
        high_kv = mm(high_rows, waqkv[:, ca:])
        keys_s[first:, :] = high_kv[:, :ca]
        values_s[first:, :] = high_kv[:, ca:]
        for k in range(0, len(above), GROUP):
            attend(above[k : k + GROUP])

    pl.when(core == 0)(with_high)
    if rounds > 2:
        hear(1)
        tell(2)
    with_low()
    pl.when(core == 1)(with_high)
    finish_rim()
    atom_mid = mid[...] + mm(att_s[...], waout[...])
    mid[...] = atom_mid
    spread = jnp.maximum(mm(atom_mid.astype(BF16), wagg[...]), 0.0).astype(BF16)
    slot_lane = lax.broadcasted_iota(jnp.int32, (1, cap), 1)
    living = slot_lane < live
    sub_ids = lax.broadcasted_iota(jnp.int32, (3 * rows, cap), 0)
    hot = ((sub_ids == relative) & living).astype(F32)
    counted = jnp.sum(hot, axis=-1, keepdims=True)
    hot_s[...] = hot.astype(BF16)
    partial = mm(hot_s[...], spread)
    few = jnp.minimum(counted, 256.0)
    lane_c = lax.broadcasted_iota(jnp.int32, (3 * rows, 128), 1)
    count_wide = jnp.where(lane_c < 64, few, counted - few)
    down = slice(rows - margin, rows)
    ahead = slice(2 * rows, 2 * rows + rim_rows)
    part_down[:, :ct] = partial[down].astype(BF16)
    part_down[:, ct:] = count_wide[down].astype(BF16)
    part_up[:, :ct] = partial[ahead].astype(BF16)
    part_up[:, ct:] = count_wide[ahead].astype(BF16)
    part_low, part_high, finish_part = exchange(1, part_up, from_low, part_down, from_high)

    need(tsingle)
    own_sum = partial[rows : 2 * rows]
    own_count = counted[rows : 2 * rows]
    middle = slice(margin, rows - margin)
    token_mid = tsingle[middle, :].astype(F32) + own_sum[middle] / jnp.maximum(own_count[middle], 1.0)
    early_all[pl.ds(me, 1)] = normalize(token_mid).astype(BF16)[None]

    messages = (early_all, late_all)

    def block(kind, src, peer, arrived, count=None):
        view = messages[kind].at[src if count is None else pl.ds(0, count)]
        return pltpu.make_async_remote_copy(
            src_ref=view,
            dst_ref=view,
            send_sem=local_sem.at[kind],
            recv_sem=arrived,
            device_id={"row": peer},
            device_id_type=pl.DeviceIdType.MESH,
        )

    def crossing(kind, zz):
        return cross_late.at[zz] if kind else cross_early.at[0]

    def relay(kind, src, over):
        if over:
            block(kind, src, across, crossing(kind, src // 4)).start()
        block(kind, src, partner, pair_recv.at[0, kind]).start()

    def own_sends(kind):
        for there, peer, diagonal in (line[:-2] if kind == 0 else line[2:-2] + line[-2:] + line[:2]):
            arrived = crossing(kind, z) if diagonal else line_recv.at[z, kind]
            pl.when(there)(lambda peer=peer, arrived=arrived: block(kind, me, peer, arrived).start())
        relay(kind, me, True)

    for step in range(min(rounds - 1, 2), rounds):
        hear(step)
        if step + 1 < rounds:
            tell(step + 1)
    own_sends(0)

    need(pmask, tbias)
    pair = 2 * rows
    allowed = pmask[...] == 1
    front = lax.broadcasted_iota(jnp.int32, (1, 2 * pair), 1) < pair
    for h in range(TH):
        masked = jnp.where(allowed, tbias[h], masked_score)
        for k in range(depth // 2):
            one = masked[:, 4 * k * pair : (4 * k + 2) * pair]
            two = masked[:, (4 * k + 2) * pair : (4 * k + 4) * pair]
            here = slice(2 * k * pair, (2 * k + 2) * pair)
            bias_half[0, h, :, here] = jnp.where(front, one, pltpu.roll(two, pair, 1))
            bias_half[1, h, :, here] = jnp.where(front, pltpu.roll(one, pair, 1), two)
    mid_t = mid[...].T
    need(wtqkv, wgate, wtout, wback, wpos)
    joint = mm(wtout[...], wback[...]).astype(BF16)
    part_low()
    part_high()
    low = from_low[...].astype(F32)
    high = from_high[...].astype(F32)

    def counts_in(sums):
        return sums[:, ct : ct + 1] + sums[:, ct + 64 : ct + 65]

    def edges(own, below, above):
        return jnp.concatenate(
            [own[:rim_rows] + below, own[rim_rows : rows - margin], own[rows - margin :] + above], axis=0
        )

    token_sum = edges(own_sum, low[:, :ct], high[:, :ct])
    token_count = edges(own_count, counts_in(low), counts_in(high))
    token_in = tsingle[...].astype(F32) + token_sum / jnp.maximum(token_count, 1.0)
    u_wide = normalize(token_in)
    u = u_wide.astype(BF16)
    chunks = ct // 128
    odd = [u_wide[margin : margin + 1, 128 * k : 128 * (k + 1)] for k in range(chunks)]
    odd.append(jnp.zeros((rim_rows - chunks, 128), F32))
    late = jnp.concatenate(
        [
            jnp.concatenate([u_wide[rows - margin :], u_wide[:margin]], axis=0),
            jnp.concatenate(odd, axis=0),
        ],
        axis=1,
    )
    late_all[pl.ds(me, 1)] = late.astype(BF16)[None]
    own_sends(1)

    direct = []
    for d in range(1, depth):
        direct.append((z >= d, z - d, d < ends))
        direct.append((z + d < depth, z + d, d < ends))

    def arrive(kind, some):
        for there, zz, over in some:
            src = index_of(zz, y, core)

            @pl.when(there)
            def _(src=src, zz=zz, over=over):
                block(kind, src, partner, line_recv.at[zz, kind]).wait_recv()
                relay(kind, src, over or kind == 0)

    def crossed_late(there, zz):
        src = index_of(zz, 1 - y, core)

        @pl.when(there)
        def _():
            block(1, src, partner, cross_late.at[zz]).wait_recv()
            block(1, src, partner, pair_recv.at[1, 1]).start()

    def crossed_early():
        block(0, 0, across, cross_early.at[0], depth).wait_recv()
        for zz in range(depth):
            block(0, index_of(zz, 1 - y, core), partner, pair_recv.at[1, 0]).start()

    def last_hops(side):
        for kind in range(2):
            block(kind, 0, partner, pair_recv.at[side, kind], depth).wait_recv()

    first_row = lax.broadcasted_iota(jnp.int32, (margin, ct), 0) == 0

    def assemble(side, column):
        for zz in range(depth):
            for cc in range(2):
                src = index_of(zz, column, cc)
                at = (2 * zz + cc) * rows
                early_rows = early_all[src]
                late_rows = late_all[src]
                u_half[side, at : at + margin, :] = late_rows[margin:, :ct]
                u_half[side, at + rows - margin : at + rows, :] = late_rows[:margin, :ct]
                extra = late_rows[:, ct:].astype(F32)
                row = jnp.concatenate([extra[k : k + 1] for k in range(chunks)], axis=1)
                tile = early_rows[:margin].astype(F32)
                u_half[side, at + margin : at + 2 * margin, :] = jnp.where(first_row, row, tile).astype(BF16)
                u_half[side, at + 2 * margin : at + rows - margin, :] = early_rows[margin:]

    arrive(0, direct[:2])
    tw = ct // TH
    tquery = (mm(u, wtqkv[:, :ct]) * (1.0 / tw**0.5)).astype(BF16)
    batches = []
    for first_head in range(0, TH, BATCH):
        heads = range(first_head, first_head + BATCH)
        left = first_head * tw // 128 * 128
        right = -(-(first_head + BATCH) * tw // 128) * 128
        lanes = [lanes_between(right - left, h * tw - left, (h + 1) * tw - left) for h in heads]
        q = tquery[:, left:right]
        wide = jnp.concatenate([q * m.astype(BF16) for m in lanes], axis=0)
        through = mm_t(wide, wtqkv[:, ct + left : ct + right]).astype(BF16)
        batches.append((first_head, left, right, lanes, through))
    gate = jax.nn.sigmoid(mm(u, wgate[...]))
    back_in = mm(token_in.astype(BF16), wback[...])
    arrive(0, direct[2:])
    arrive(1, direct)
    crossed_late(True, z)
    last_hops(0)
    assemble(0, y)

    def scored(features, column, some):
        bias = bias_half[column]
        scores = []
        for first_head, _, _, _, through in some:
            score = mm_t(through, features)
            scores.append(score + bias[first_head : first_head + BATCH].reshape(score.shape))
        return scores

    def valued(e, features, left, right):
        mixed = mm(e.astype(BF16), features).astype(BF16)
        return mm(mixed, wtqkv[:, 2 * ct + left : 2 * ct + right])

    features = u_half[0]
    own_max = []
    own_total = []
    own_out = []
    scores = scored(features, y, batches)
    for score in scores:
        own_max.append(jnp.max(score, axis=-1, keepdims=True))
    exps = [jnp.exp(score - m) for score, m in zip(scores, own_max)]
    for (_, left, right, _, _), e in zip(batches, exps):
        own_total.append(jnp.sum(e, axis=-1, keepdims=True))
        own_out.append(valued(e, features, left, right))
    crossed_early()
    for d in range(1, depth):
        crossed_late(z >= d, z - d)
        crossed_late(z + d < depth, z + d)
    last_hops(1)
    assemble(1, 1 - y)
    features = u_half[1]
    scores = scored(features, 1 - y, batches)
    all_max = [jnp.maximum(m, jnp.max(score, axis=-1, keepdims=True)) for score, m in zip(scores, own_max)]
    exps = [jnp.exp(score - m) for score, m in zip(scores, all_max)]
    outs = [valued(e, features, left, right) for e, (_, left, right, _, _) in zip(exps, batches)]
    blocks = [None] * chunks
    for k, (_, left, right, lanes, _) in enumerate(batches):
        scale = jnp.exp(own_max[k] - all_max[k])
        share = 1.0 / (own_total[k] * scale + jnp.sum(exps[k], axis=-1, keepdims=True))
        out = own_out[k] * (scale * share) + outs[k] * share
        total = out[:rows] * lanes[0]
        for h in range(1, BATCH):
            total = total + out[h * rows : (h + 1) * rows] * lanes[h]
        for c in range(left // 128, right // 128):
            part = total[:, 128 * c - left : 128 * (c + 1) - left]
            blocks[c] = part if blocks[c] is None else blocks[c] + part
    gated = (gate * jnp.concatenate(blocks, axis=1)).astype(BF16)
    near[rows : 2 * rows, :] = (back_in + mm(gated, joint)).astype(BF16)
    upper = near.at[2 * rows - margin : 2 * rows]
    lower = near.at[rows : rows + rim_rows]
    finish_part()
    back_low, back_high, finish_back = exchange(
        2, upper, near.at[rows - margin : rows], lower, near.at[2 * rows : 2 * rows + rim_rows]
    )
    tout_ref[...] = (token_in + mm(gated, wtout[...])).astype(BF16)
    for kind in range(2):
        block(kind, 0, partner, pair_recv.at[0, kind], n - 1).wait_send()
    back_low()
    back_high()
    back_t = lax.dot_general(near[...], hot_s[...], (((0,), (0,)), ((), ())), preferred_element_type=F32)
    atom_last = mid_t + back_t
    center = atom_last - jnp.mean(atom_last, axis=0, keepdims=True)
    width = jnp.mean(center * center, axis=0, keepdims=True)
    final = (center * lax.rsqrt(width + 1e-05)).astype(BF16)
    update = mm(wpos[...], final)
    den_ref[...] = jnp.where(living, skip_scale * noisy + output_scale * update, 0.0)
    finish_back()


def store(den, tout, den_h, tout_h, sem):
    copies = [pltpu.make_async_copy(den, den_h, sem.at[0]), pltpu.make_async_copy(tout, tout_h, sem.at[1])]
    for c in copies:
        c.start()
    for c in copies:
        c.wait()


def on_device(
    positions, noise, atom_single, atom_token, atom_counts, window_offsets, atom_bias,
    token_single, token_bias, pair_mask, w_coord, w_atom_qkv, w_atom_out, w_agg,
    w_tok_qkv, w_tok_gate, w_tok_out, w_back, w_pos,
):
    n = lax.axis_size("row")
    cap, ca = atom_single.shape
    rows, ct = token_single.shape
    big = (
        positions, noise, atom_single, atom_token, atom_bias, token_single,
        token_bias, pair_mask, w_coord, w_atom_qkv, w_atom_out, w_agg, w_tok_qkv, w_tok_gate,
        w_tok_out, w_back, w_pos,
    )
    margin = rows // 4
    send_up, send_down = (2 * margin, ct + 128), (margin, ct + 128)
    hbm = pl.BlockSpec(memory_space=pltpu.HBM)
    vmem = pl.BlockSpec(memory_space=pltpu.VMEM)
    out_shapes = (((positions.shape[0], cap), F32), ((rows, ct), BF16))
    results = pl.pallas_call(
        lambda *refs: kernel(n, *refs),
        out_shape=tuple(pltpu.VMEM(shape, kind) for shape, kind in out_shapes),
        in_specs=[pl.BlockSpec(memory_space=pltpu.SMEM)] + [hbm] * (1 + len(big)),
        out_specs=(vmem, vmem),
        scratch_shapes=[pltpu.SMEM(window_offsets.shape, jnp.int32)]
        + [pltpu.VMEM(a.shape, a.dtype) for a in big]
        + [
            pltpu.VMEM((128, cap), F32),
            pltpu.VMEM((cap, ca), F32),
            pltpu.VMEM((BEHIND, ca), BF16),
            pltpu.VMEM((AHEAD, ca), BF16),
            pltpu.VMEM((BEHIND, ca), BF16),
            pltpu.VMEM((AHEAD, ca), BF16),
            pltpu.VMEM((cap + AHEAD, ca), F32),
            pltpu.VMEM((cap, ca), BF16),
            pltpu.VMEM((BEHIND + cap + AHEAD, ca), F32),
            pltpu.VMEM((BEHIND + cap + AHEAD, ca), F32),
            pltpu.VMEM((cap, ca), F32),
            pltpu.VMEM((cap, ca), BF16),
            pltpu.VMEM(send_down, BF16),
            pltpu.VMEM(send_up, BF16),
            pltpu.VMEM(send_up, BF16),
            pltpu.VMEM(send_down, BF16),
            pltpu.VMEM((n, rows - 2 * margin, ct), BF16),
            pltpu.VMEM((n, 2 * margin, ct + 128), BF16),
            pltpu.VMEM((2, n * rows // 2, ct), BF16),
            pltpu.VMEM((2, TH, rows, n * rows // 2), F32),
            pltpu.VMEM((3 * rows, cap), BF16),
            pltpu.VMEM((3 * rows, ca), BF16),
            pltpu.SemaphoreType.DMA((1 + len(big),)),
            pltpu.SemaphoreType.DMA((4,)),
            pltpu.SemaphoreType.DMA((n // 4, 2)),
            pltpu.SemaphoreType.DMA((1,)),
            pltpu.SemaphoreType.DMA((n // 4,)),
            pltpu.SemaphoreType.DMA((2, 2)),
            pltpu.SemaphoreType.REGULAR((max(n // 4 - 1, 1),)),
        ],
        compiler_params=pltpu.CompilerParams(collective_id=0, has_side_effects=True, vmem_limit_bytes=VMEM_LIMIT),
    )(atom_counts, *(pltpu.with_memory_space_constraint(a, pltpu.HBM) for a in (window_offsets,) + big))
    results = tuple(pltpu.with_memory_space_constraint(a, pltpu.VMEM) for a in results)
    return pl.pallas_call(
        store,
        out_shape=tuple(jax.ShapeDtypeStruct(shape, kind) for shape, kind in out_shapes),
        in_specs=[vmem, vmem],
        out_specs=(hbm, hbm),
        scratch_shapes=[pltpu.SemaphoreType.DMA((2,))],
    )(*results)


def solution(mesh):
    placed = (
        P(None, ("grp", "row")),
        P(None, ("grp", "row")),
        P(("grp", "row"), None),
        P(("grp", "row")),
        P(("grp", "row")),
        P(("grp", "row")),
        P(None, ("grp", "row"), None),
        P(("grp", "row"), None),
        P(None, ("grp", "row"), None),
        P(("grp", "row"), None),
    ) + (P(),) * 9
    return jax.shard_map(
        on_device,
        mesh=mesh,
        in_specs=placed,
        out_specs=(P(None, ("grp", "row")), P(("grp", "row"), None)),
        check_vma=False,
    )
```

```python
import jax
import jax.numpy as jnp
from jax import lax
from jax.experimental import pallas as pl
from jax.experimental.pallas import tpu as pltpu
from jax.sharding import PartitionSpec as P

AH = 4
TH = 16
QWIN = 32
KWIN = 128
BEHIND = KWIN // 2
AHEAD = KWIN - QWIN

noise_level = 2.0
input_scale = 1.0 / 5.0**0.5
skip_scale = 1.0 / 5.0
output_scale = 2.0 / 5.0**0.5
masked_score = -1e30

F32 = jnp.float32
BF16 = jnp.bfloat16
GROUP = 8
BATCH = 4
VMEM_LIMIT = 40 * 1024 * 1024


def normalize(values):
    center = values - jnp.mean(values, axis=-1, keepdims=True)
    spread = jnp.mean(center * center, axis=-1, keepdims=True)
    return center * lax.rsqrt(spread + 1e-05)


def mm(a, b):
    return jnp.dot(a, b, preferred_element_type=F32)


def mm_t(a, b):
    return lax.dot_general(a, b, (((1,), (1,)), ((), ())), preferred_element_type=F32)


def lanes_between(width, low, high):
    lane = lax.broadcasted_iota(jnp.int32, (1, width), 1)
    return ((lane >= low) & (lane < high)).astype(F32)


def kernel(
    n,
    counts_s, offsets_h,
    pos_h, noise_h, single_h, token_h, abias_h, tsingle_h, tbias_h, mask_h,
    wcoord_h, waqkv_h, waout_h, wagg_h, wtqkv_h, wgate_h, wtout_h, wback_h, wpos_h,
    den_ref, tout_ref,
    offsets_s,
    pos, noise, single, token, abias, tsingle, tbias, pmask,
    wcoord, waqkv, waout, wagg, wtqkv, wgate, wtout, wback, wpos,
    columns, hs, tail, head, lo, up, shifted, queries, keys_s, values_s, mid, att_s,
    part_down, part_up, from_low, from_high, early_all, late_all, u_half, bias_half, hot_s, near,
    local_sem, edge_recv, line_recv, cross_early, cross_late, pair_recv, ready,
):
    cap, ca = single.shape
    rows, ct = tsingle.shape
    margin = rows // 4
    rim_rows = 2 * margin
    me = lax.axis_index("row")
    last = n - 1
    has_low = me > 0
    has_high = me < last

    pairs = [
        (pos_h, pos), (noise_h, noise), (single_h, single), (wcoord_h, wcoord), (token_h, token),
        (waqkv_h, waqkv), (abias_h, abias), (waout_h, waout), (wagg_h, wagg), (tsingle_h, tsingle),
        (wtqkv_h, wtqkv), (wgate_h, wgate), (mask_h, pmask), (tbias_h, tbias), (wtout_h, wtout),
        (wback_h, wback), (wpos_h, wpos), (offsets_h, offsets_s),
    ]
    copies = {}
    for k, (src, dst) in enumerate(pairs):
        copies[id(dst)] = pltpu.make_async_copy(src, dst, local_sem.at[k])
        copies[id(dst)].start()

    def need(*refs):
        for r in refs:
            copies[id(r)].wait()

    core = lax.rem(me, 2)
    y = lax.rem(me // 2, 2)
    z = me // 4
    depth = n // 4

    def index_of(zz, yy, cc):
        return zz * 4 + yy * 2 + cc

    partner = index_of(z, y, 1 - core)
    across = index_of(z, 1 - y, core)
    line = []
    for d in range(1, depth):
        line.append((z + d < depth, index_of(z + d, y, core)))
        line.append((z >= d, index_of(z - d, y, core)))


    barrier = pltpu.get_barrier_semaphore()

    def greet(peer):
        pl.semaphore_signal(
            barrier, inc=1, device_id={"row": peer}, device_id_type=pl.DeviceIdType.MESH
        )

    greet(partner)
    greet(across)
    beside = [(z >= 1, index_of(z - 1, y, core)), (z + 1 < depth, index_of(z + 1, y, core))]
    for there, peer in beside:
        pl.when(there)(lambda peer=peer: greet(peer))
    far = me - 1 + 2 * core
    has_far = (far >= 0) & (far < n)
    pl.when(has_far)(lambda: greet(far))

    shifted[...] = jnp.zeros_like(shifted)
    columns[...] = jnp.zeros_like(columns)
    near[...] = jnp.zeros_like(near)

    @pl.when(me == 0)
    def _():
        lo[...] = jnp.zeros_like(lo)
        from_low[...] = jnp.zeros_like(from_low)

    @pl.when(me == last)
    def _():
        up[...] = jnp.zeros_like(up)
        from_high[...] = jnp.zeros_like(from_high)

    need(pos, noise, single, wcoord, token)
    live = jnp.clip(counts_s[0], cap // 2, cap)
    noisy = pos[...] + noise_level * noise[...]
    columns[0:3, :] = input_scale * noisy
    relative = token[...].reshape(1, cap) - (me - 1) * rows
    turned = columns[...].T
    wc = wcoord[...]
    atom_start = single[...].astype(F32) + (
        turned[:, 0:1] * wc[0:1, :] + turned[:, 1:2] * wc[1:2, :] + turned[:, 2:3] * wc[2:3, :]
    )
    normed = normalize(atom_start)
    hs[...] = normed
    mid[...] = atom_start
    head[...] = normed[:AHEAD].astype(BF16)
    tail[...] = hs[pl.ds(live - BEHIND, BEHIND), :].astype(BF16)

    links = jnp.where(z >= 1, 1, 0) + jnp.where(z + 1 < depth, 1, 0) + 1
    peers = 1 + links + jnp.where(has_far, 1, 0)
    pl.semaphore_wait(barrier, peers)

    def edge(stage, way, src, dst, peer):
        return pltpu.make_async_remote_copy(
            src_ref=src,
            dst_ref=dst,
            send_sem=local_sem.at[2 + way],
            recv_sem=edge_recv.at[2 * (stage % 2) + way],
            device_id={"row": peer},
            device_id_type=pl.DeviceIdType.MESH,
        )

    def exchange(stage, src_up, dst_up, src_down, dst_down):
        going_up = edge(stage, 0, src_up, dst_up, me + 1)
        going_down = edge(stage, 1, src_down, dst_down, me - 1)
        pl.when(has_high)(going_up.start)
        pl.when(has_low)(going_down.start)

        def receive_low():
            pl.when(has_low)(going_up.wait_recv)

        def receive_high():
            pl.when(has_high)(going_down.wait_recv)

        def finish():
            pl.when(has_high)(going_up.wait_send)
            pl.when(has_low)(going_down.wait_send)

        return receive_low, receive_high, finish

    rim_low, rim_high, finish_rim = exchange(0, tail, lo, head, up)

    def tell(step):
        def one(peer):
            pl.semaphore_signal(
                ready.at[step], inc=1, device_id={"row": peer}, device_id_type=pl.DeviceIdType.MESH
            )

        one(across)
        for there, peer in beside:
            pl.when(there)(lambda peer=peer: one(peer))

    def hear(step):
        pl.semaphore_wait(ready.at[step], links)

    rounds = max(depth - 2, 0)
    if rounds:
        tell(0)
    need(waqkv)
    hw = ca // AH
    normed_b = normed.astype(BF16)
    own = mm(normed_b, waqkv[...])
    queries[...] = (own[:, :ca] * (1.0 / hw**0.5)).astype(BF16)
    head_lanes = [lanes_between(ca, h * hw, (h + 1) * hw) for h in range(AH)]
    keys_s[BEHIND : BEHIND + cap, :] = own[:, ca : 2 * ca]
    values_s[BEHIND : BEHIND + cap, :] = own[:, 2 * ca :]
    need(abias, offsets_s, waout, wagg)

    top = jnp.where(has_high, BEHIND + live + AHEAD, BEHIND + live)
    bottom = jnp.where(has_low, 0, BEHIND)
    lane_key = lax.broadcasted_iota(jnp.int32, (1, KWIN), 1)
    ones = jnp.ones((KWIN, ca), BF16)

    def attend(windows):
        at = [BEHIND + QWIN * w + offsets_s[w] for w in windows]
        scores = []
        for w, start in zip(windows, at):
            key = keys_s[pl.ds(start, KWIN), :].astype(BF16)
            q = queries[w * QWIN : (w + 1) * QWIN, :]
            wide = jnp.concatenate([q * m.astype(BF16) for m in head_lanes], axis=0)
            scores.append(mm_t(wide, key))
        exps = []
        for w, start, score in zip(windows, at, scores):
            score = score + abias[:, w * QWIN : (w + 1) * QWIN, :].reshape(AH * QWIN, KWIN)
            keys = lane_key + start
            score = jnp.where((keys >= bottom) & (keys < top), score, masked_score)
            exps.append(jnp.exp(score - jnp.max(score, axis=-1, keepdims=True)).astype(BF16))
        outs = []
        for start, e in zip(at, exps):
            value = values_s[pl.ds(start, KWIN), :].astype(BF16)
            outs.append(mm(e, jnp.concatenate([value, ones], axis=1)))
        for w, out in zip(windows, outs):
            mixed = out[:QWIN] * wide_lanes[0]
            for h in range(1, AH):
                mixed = mixed + out[h * QWIN : (h + 1) * QWIN] * wide_lanes[h]
            att_s[w * QWIN : (w + 1) * QWIN, :] = (mixed[:, :ca] / mixed[:, ca:]).astype(BF16)

    wide_lanes = [jnp.concatenate([m, m], axis=1) for m in head_lanes]
    half = cap // 2
    count = cap // QWIN
    behind_windows = BEHIND // QWIN
    inner = [w for w in range(count) if w >= behind_windows and QWIN * w + AHEAD <= half]
    below = range(behind_windows)
    above = range(inner[-1] + 1, count)
    first = BEHIND + half
    span = half + AHEAD
    attend(inner)
    if rounds > 1:
        hear(0)
        tell(1)

    def with_low():
        rim_low()
        low_kv = mm(lo[...], waqkv[:, ca:])
        keys_s[:BEHIND, :] = low_kv[:, :ca]
        values_s[:BEHIND, :] = low_kv[:, ca:]
        attend(below)

    def with_high():
        rim_high()
        shifted[half : half + AHEAD, :] = up[...].astype(F32)
        moved = shifted[pl.ds(cap - live, span), :]
        row_ids = lax.broadcasted_iota(jnp.int32, (half, ca), 0) + first
        merged = jnp.where(row_ids < BEHIND + live, hs[half:cap, :], moved[:half])
        high_rows = jnp.concatenate([merged, moved[half:]], axis=0).astype(BF16)
        high_kv = mm(high_rows, waqkv[:, ca:])
        keys_s[first:, :] = high_kv[:, :ca]
        values_s[first:, :] = high_kv[:, ca:]
        for k in range(0, len(above), GROUP):
            attend(above[k : k + GROUP])

    pl.when(core == 0)(with_high)
    if rounds > 2:
        hear(1)
        tell(2)
    with_low()
    pl.when(core == 1)(with_high)
    finish_rim()
    atom_mid = mid[...] + mm(att_s[...], waout[...])
    mid[...] = atom_mid
    spread = jnp.maximum(mm(atom_mid.astype(BF16), wagg[...]), 0.0).astype(BF16)
    slot_lane = lax.broadcasted_iota(jnp.int32, (1, cap), 1)
    living = slot_lane < live
    sub_ids = lax.broadcasted_iota(jnp.int32, (3 * rows, cap), 0)
    hot = ((sub_ids == relative) & living).astype(F32)
    counted = jnp.sum(hot, axis=-1, keepdims=True)
    hot_s[...] = hot.astype(BF16)
    partial = mm(hot_s[...], spread)
    few = jnp.minimum(counted, 256.0)
    lane_c = lax.broadcasted_iota(jnp.int32, (3 * rows, 128), 1)
    count_wide = jnp.where(lane_c < 64, few, counted - few)
    down = slice(rows - margin, rows)
    ahead = slice(2 * rows, 2 * rows + rim_rows)
    part_down[:, :ct] = partial[down].astype(BF16)
    part_down[:, ct:] = count_wide[down].astype(BF16)
    part_up[:, :ct] = partial[ahead].astype(BF16)
    part_up[:, ct:] = count_wide[ahead].astype(BF16)
    part_low, part_high, finish_part = exchange(1, part_up, from_low, part_down, from_high)

    need(tsingle)
    own_sum = partial[rows : 2 * rows]
    own_count = counted[rows : 2 * rows]
    middle = slice(margin, rows - margin)
    token_mid = tsingle[middle, :].astype(F32) + own_sum[middle] / jnp.maximum(own_count[middle], 1.0)
    early_all[pl.ds(me, 1)] = normalize(token_mid).astype(BF16)[None]

    messages = (early_all, late_all)

    def block(kind, src, peer, arrived, count=None):
        view = messages[kind].at[src if count is None else pl.ds(0, count)]
        return pltpu.make_async_remote_copy(
            src_ref=view,
            dst_ref=view,
            send_sem=local_sem.at[kind],
            recv_sem=arrived,
            device_id={"row": peer},
            device_id_type=pl.DeviceIdType.MESH,
        )

    def relay(kind, src):
        block(kind, src, across, cross_late.at[src // 4] if kind else cross_early.at[0]).start()
        block(kind, src, partner, pair_recv.at[0, kind]).start()

    def own_sends(kind):
        for there, peer in line[::-1] if kind else line:
            pl.when(there)(lambda peer=peer: block(kind, me, peer, line_recv.at[z, kind]).start())
        relay(kind, me)

    for step in range(max(min(rounds - 1, 2), 0), rounds):
        hear(step)
        if step + 1 < rounds:
            tell(step + 1)
    own_sends(0)

    need(pmask, tbias)
    pair = 2 * rows
    allowed = pmask[...] == 1
    front = lax.broadcasted_iota(jnp.int32, (1, 2 * pair), 1) < pair
    for h in range(TH):
        masked = jnp.where(allowed, tbias[h], masked_score)
        for k in range(depth // 2):
            one = masked[:, 4 * k * pair : (4 * k + 2) * pair]
            two = masked[:, (4 * k + 2) * pair : (4 * k + 4) * pair]
            here = slice(2 * k * pair, (2 * k + 2) * pair)
            bias_half[0, h, :, here] = jnp.where(front, one, pltpu.roll(two, pair, 1))
            bias_half[1, h, :, here] = jnp.where(front, pltpu.roll(one, pair, 1), two)
    mid_t = mid[...].T
    need(wtqkv, wgate, wtout, wback, wpos)
    joint = mm(wtout[...], wback[...]).astype(BF16)
    part_low()
    part_high()
    low = from_low[...].astype(F32)
    high = from_high[...].astype(F32)

    def counts_in(sums):
        return sums[:, ct : ct + 1] + sums[:, ct + 64 : ct + 65]

    def edges(own, below, above):
        return jnp.concatenate(
            [own[:rim_rows] + below, own[rim_rows : rows - margin], own[rows - margin :] + above], axis=0
        )

    token_sum = edges(own_sum, low[:, :ct], high[:, :ct])
    token_count = edges(own_count, counts_in(low), counts_in(high))
    token_in = tsingle[...].astype(F32) + token_sum / jnp.maximum(token_count, 1.0)
    u_wide = normalize(token_in)
    u = u_wide.astype(BF16)
    chunks = ct // 128
    odd = [u_wide[margin : margin + 1, 128 * k : 128 * (k + 1)] for k in range(chunks)]
    odd.append(jnp.zeros((rim_rows - chunks, 128), F32))
    late = jnp.concatenate(
        [
            jnp.concatenate([u_wide[rows - margin :], u_wide[:margin]], axis=0),
            jnp.concatenate(odd, axis=0),
        ],
        axis=1,
    )
    late_all[pl.ds(me, 1)] = late.astype(BF16)[None]
    own_sends(1)

    direct = []
    for d in range(1, depth):
        direct.append((z >= d, z - d))
        direct.append((z + d < depth, z + d))

    def arrive(kind, some):
        for there, zz in some:
            src = index_of(zz, y, core)

            @pl.when(there)
            def _(src=src, zz=zz):
                block(kind, src, partner, line_recv.at[zz, kind]).wait_recv()
                relay(kind, src)

    def crossed_late(there, zz):
        src = index_of(zz, 1 - y, core)

        @pl.when(there)
        def _():
            block(1, src, partner, cross_late.at[zz]).wait_recv()
            block(1, src, partner, pair_recv.at[1, 1]).start()

    def crossed_early():
        block(0, 0, across, cross_early.at[0], depth).wait_recv()
        for zz in range(depth):
            block(0, index_of(zz, 1 - y, core), partner, pair_recv.at[1, 0]).start()

    def last_hops(side):
        for kind in range(2):
            block(kind, 0, partner, pair_recv.at[side, kind], depth).wait_recv()

    first_row = lax.broadcasted_iota(jnp.int32, (margin, ct), 0) == 0

    def assemble(side, column):
        for zz in range(depth):
            for cc in range(2):
                src = index_of(zz, column, cc)
                at = (2 * zz + cc) * rows
                early_rows = early_all[src]
                late_rows = late_all[src]
                u_half[side, at : at + margin, :] = late_rows[margin:, :ct]
                u_half[side, at + rows - margin : at + rows, :] = late_rows[:margin, :ct]
                extra = late_rows[:, ct:].astype(F32)
                row = jnp.concatenate([extra[k : k + 1] for k in range(chunks)], axis=1)
                tile = early_rows[:margin].astype(F32)
                u_half[side, at + margin : at + 2 * margin, :] = jnp.where(first_row, row, tile).astype(BF16)
                u_half[side, at + 2 * margin : at + rows - margin, :] = early_rows[margin:]

    arrive(0, direct[:2])
    tw = ct // TH
    tquery = (mm(u, wtqkv[:, :ct]) * (1.0 / tw**0.5)).astype(BF16)
    batches = []
    for first_head in range(0, TH, BATCH):
        heads = range(first_head, first_head + BATCH)
        left = first_head * tw // 128 * 128
        right = -(-(first_head + BATCH) * tw // 128) * 128
        lanes = [lanes_between(right - left, h * tw - left, (h + 1) * tw - left) for h in heads]
        q = tquery[:, left:right]
        wide = jnp.concatenate([q * m.astype(BF16) for m in lanes], axis=0)
        through = mm_t(wide, wtqkv[:, ct + left : ct + right]).astype(BF16)
        batches.append((first_head, left, right, lanes, through))
    gate = jax.nn.sigmoid(mm(u, wgate[...]))
    back_in = mm(token_in.astype(BF16), wback[...])
    arrive(0, direct[2:])
    arrive(1, direct)
    crossed_late(True, z)
    last_hops(0)
    assemble(0, y)

    def scored(features, column, some):
        bias = bias_half[column]
        scores = []
        for first_head, _, _, _, through in some:
            score = mm_t(through, features)
            scores.append(score + bias[first_head : first_head + BATCH].reshape(score.shape))
        return scores

    def valued(e, features, left, right):
        mixed = mm(e.astype(BF16), features).astype(BF16)
        return mm(mixed, wtqkv[:, 2 * ct + left : 2 * ct + right])

    features = u_half[0]
    own_max = []
    own_total = []
    own_out = []
    scores = scored(features, y, batches)
    for score in scores:
        own_max.append(jnp.max(score, axis=-1, keepdims=True))
    exps = [jnp.exp(score - m) for score, m in zip(scores, own_max)]
    for (_, left, right, _, _), e in zip(batches, exps):
        own_total.append(jnp.sum(e, axis=-1, keepdims=True))
        own_out.append(valued(e, features, left, right))
    crossed_early()
    for d in range(1, depth):
        crossed_late(z >= d, z - d)
        crossed_late(z + d < depth, z + d)
    last_hops(1)
    assemble(1, 1 - y)
    features = u_half[1]
    scores = scored(features, 1 - y, batches)
    all_max = [jnp.maximum(m, jnp.max(score, axis=-1, keepdims=True)) for score, m in zip(scores, own_max)]
    exps = [jnp.exp(score - m) for score, m in zip(scores, all_max)]
    outs = [valued(e, features, left, right) for e, (_, left, right, _, _) in zip(exps, batches)]
    blocks = [None] * chunks
    for k, (_, left, right, lanes, _) in enumerate(batches):
        scale = jnp.exp(own_max[k] - all_max[k])
        share = 1.0 / (own_total[k] * scale + jnp.sum(exps[k], axis=-1, keepdims=True))
        out = own_out[k] * (scale * share) + outs[k] * share
        total = out[:rows] * lanes[0]
        for h in range(1, BATCH):
            total = total + out[h * rows : (h + 1) * rows] * lanes[h]
        for c in range(left // 128, right // 128):
            part = total[:, 128 * c - left : 128 * (c + 1) - left]
            blocks[c] = part if blocks[c] is None else blocks[c] + part
    gated = (gate * jnp.concatenate(blocks, axis=1)).astype(BF16)
    near[rows : 2 * rows, :] = (back_in + mm(gated, joint)).astype(BF16)
    upper = near.at[2 * rows - margin : 2 * rows]
    lower = near.at[rows : rows + rim_rows]
    finish_part()
    back_low, back_high, finish_back = exchange(
        2, upper, near.at[rows - margin : rows], lower, near.at[2 * rows : 2 * rows + rim_rows]
    )
    tout_ref[...] = (token_in + mm(gated, wtout[...])).astype(BF16)
    for kind in range(2):
        block(kind, 0, partner, pair_recv.at[0, kind], n - 1).wait_send()
    back_low()
    back_high()
    back_t = lax.dot_general(near[...], hot_s[...], (((0,), (0,)), ((), ())), preferred_element_type=F32)
    atom_last = mid_t + back_t
    center = atom_last - jnp.mean(atom_last, axis=0, keepdims=True)
    width = jnp.mean(center * center, axis=0, keepdims=True)
    final = (center * lax.rsqrt(width + 1e-05)).astype(BF16)
    update = mm(wpos[...], final)
    den_ref[...] = jnp.where(living, skip_scale * noisy + output_scale * update, 0.0)
    finish_back()


def store(den, tout, den_h, tout_h, sem):
    copies = [pltpu.make_async_copy(den, den_h, sem.at[0]), pltpu.make_async_copy(tout, tout_h, sem.at[1])]
    for c in copies:
        c.start()
    for c in copies:
        c.wait()


def on_device(
    positions, noise, atom_single, atom_token, atom_counts, window_offsets, atom_bias,
    token_single, token_bias, pair_mask, w_coord, w_atom_qkv, w_atom_out, w_agg,
    w_tok_qkv, w_tok_gate, w_tok_out, w_back, w_pos,
):
    n = lax.axis_size("row")
    cap, ca = atom_single.shape
    rows, ct = token_single.shape
    big = (
        positions, noise, atom_single, atom_token, atom_bias, token_single,
        token_bias, pair_mask, w_coord, w_atom_qkv, w_atom_out, w_agg, w_tok_qkv, w_tok_gate,
        w_tok_out, w_back, w_pos,
    )
    margin = rows // 4
    send_up, send_down = (2 * margin, ct + 128), (margin, ct + 128)
    hbm = pl.BlockSpec(memory_space=pltpu.HBM)
    vmem = pl.BlockSpec(memory_space=pltpu.VMEM)
    out_shapes = (((positions.shape[0], cap), F32), ((rows, ct), BF16))
    results = pl.pallas_call(
        lambda *refs: kernel(n, *refs),
        out_shape=tuple(pltpu.VMEM(shape, kind) for shape, kind in out_shapes),
        in_specs=[pl.BlockSpec(memory_space=pltpu.SMEM)] + [hbm] * (1 + len(big)),
        out_specs=(vmem, vmem),
        scratch_shapes=[pltpu.SMEM(window_offsets.shape, jnp.int32)]
        + [pltpu.VMEM(a.shape, a.dtype) for a in big]
        + [
            pltpu.VMEM((128, cap), F32),
            pltpu.VMEM((cap, ca), F32),
            pltpu.VMEM((BEHIND, ca), BF16),
            pltpu.VMEM((AHEAD, ca), BF16),
            pltpu.VMEM((BEHIND, ca), BF16),
            pltpu.VMEM((AHEAD, ca), BF16),
            pltpu.VMEM((cap + AHEAD, ca), F32),
            pltpu.VMEM((cap, ca), BF16),
            pltpu.VMEM((BEHIND + cap + AHEAD, ca), F32),
            pltpu.VMEM((BEHIND + cap + AHEAD, ca), F32),
            pltpu.VMEM((cap, ca), F32),
            pltpu.VMEM((cap, ca), BF16),
            pltpu.VMEM(send_down, BF16),
            pltpu.VMEM(send_up, BF16),
            pltpu.VMEM(send_up, BF16),
            pltpu.VMEM(send_down, BF16),
            pltpu.VMEM((n, rows - 2 * margin, ct), BF16),
            pltpu.VMEM((n, 2 * margin, ct + 128), BF16),
            pltpu.VMEM((2, n * rows // 2, ct), BF16),
            pltpu.VMEM((2, TH, rows, n * rows // 2), F32),
            pltpu.VMEM((3 * rows, cap), BF16),
            pltpu.VMEM((3 * rows, ca), BF16),
            pltpu.SemaphoreType.DMA((1 + len(big),)),
            pltpu.SemaphoreType.DMA((4,)),
            pltpu.SemaphoreType.DMA((n // 4, 2)),
            pltpu.SemaphoreType.DMA((1,)),
            pltpu.SemaphoreType.DMA((n // 4,)),
            pltpu.SemaphoreType.DMA((2, 2)),
            pltpu.SemaphoreType.REGULAR((max(n // 4 - 2, 1),)),
        ],
        compiler_params=pltpu.CompilerParams(collective_id=0, has_side_effects=True, vmem_limit_bytes=VMEM_LIMIT),
    )(atom_counts, *(pltpu.with_memory_space_constraint(a, pltpu.HBM) for a in (window_offsets,) + big))
    results = tuple(pltpu.with_memory_space_constraint(a, pltpu.VMEM) for a in results)
    return pl.pallas_call(
        store,
        out_shape=tuple(jax.ShapeDtypeStruct(shape, kind) for shape, kind in out_shapes),
        in_specs=[vmem, vmem],
        out_specs=(hbm, hbm),
        scratch_shapes=[pltpu.SemaphoreType.DMA((2,))],
    )(*results)


def solution(mesh):
    placed = (
        P(None, ("grp", "row")),
        P(None, ("grp", "row")),
        P(("grp", "row"), None),
        P(("grp", "row")),
        P(("grp", "row")),
        P(("grp", "row")),
        P(None, ("grp", "row"), None),
        P(("grp", "row"), None),
        P(None, ("grp", "row"), None),
        P(("grp", "row"), None),
    ) + (P(),) * 9
    return jax.shard_map(
        on_device,
        mesh=mesh,
        in_specs=placed,
        out_specs=(P(None, ("grp", "row")), P(("grp", "row"), None)),
        check_vma=False,
    )
```

```python
import jax
import jax.numpy as jnp
from jax import lax
from jax.experimental import pallas as pl
from jax.experimental.pallas import tpu as pltpu
from jax.sharding import PartitionSpec as P

AH = 4
TH = 16
QWIN = 32
KWIN = 128
BEHIND = KWIN // 2
AHEAD = KWIN - QWIN

noise_level = 2.0
input_scale = 1.0 / 5.0**0.5
skip_scale = 1.0 / 5.0
output_scale = 2.0 / 5.0**0.5
masked_score = -1e30

F32 = jnp.float32
BF16 = jnp.bfloat16
GROUP = 8
BATCH = 4
VMEM_LIMIT = 40 * 1024 * 1024


def normalize(values):
    center = values - jnp.mean(values, axis=-1, keepdims=True)
    spread = jnp.mean(center * center, axis=-1, keepdims=True)
    return center * lax.rsqrt(spread + 1e-05)


def mm(a, b):
    return jnp.dot(a, b, preferred_element_type=F32)


def mm_t(a, b):
    return lax.dot_general(a, b, (((1,), (1,)), ((), ())), preferred_element_type=F32)


def lanes_between(width, low, high):
    lane = lax.broadcasted_iota(jnp.int32, (1, width), 1)
    return ((lane >= low) & (lane < high)).astype(F32)


def kernel(
    n,
    counts_s, offsets_h,
    pos_h, noise_h, single_h, token_h, abias_h, tsingle_h, tbias_h, mask_h,
    wcoord_h, waqkv_h, waout_h, wagg_h, wtqkv_h, wgate_h, wtout_h, wback_h, wpos_h,
    den_ref, tout_ref,
    offsets_s,
    pos, noise, single, token, abias, tsingle, tbias, pmask,
    wcoord, waqkv, waout, wagg, wtqkv, wgate, wtout, wback, wpos,
    columns, hs, tail, head, lo, up, shifted, queries, keys_s, values_s, mid, att_s,
    part_down, part_up, from_low, from_high, early_all, late_all, u_half, bias_half, hot_s, near,
    local_sem, edge_recv, line_recv, cross_early, cross_late, pair_recv, ready,
):
    cap, ca = single.shape
    rows, ct = tsingle.shape
    margin = rows // 4
    rim_rows = 2 * margin
    me = lax.axis_index("row")
    last = n - 1
    has_low = me > 0
    has_high = me < last

    pairs = [
        (pos_h, pos), (noise_h, noise), (single_h, single), (wcoord_h, wcoord), (token_h, token),
        (waqkv_h, waqkv), (abias_h, abias), (waout_h, waout), (wagg_h, wagg), (tsingle_h, tsingle),
        (wtqkv_h, wtqkv), (wgate_h, wgate), (mask_h, pmask), (tbias_h, tbias), (wtout_h, wtout),
        (wback_h, wback), (wpos_h, wpos), (offsets_h, offsets_s),
    ]
    copies = {}
    for k, (src, dst) in enumerate(pairs):
        copies[id(dst)] = pltpu.make_async_copy(src, dst, local_sem.at[k])
        copies[id(dst)].start()

    def need(*refs):
        for r in refs:
            copies[id(r)].wait()

    core = lax.rem(me, 2)
    y = lax.rem(me // 2, 2)
    z = me // 4
    depth = n // 4

    def index_of(zz, yy, cc):
        return zz * 4 + yy * 2 + cc

    partner = index_of(z, y, 1 - core)
    across = index_of(z, 1 - y, core)
    line = []
    for d in range(1, depth):
        line.append((z + d < depth, index_of(z + d, y, core)))
        line.append((z >= d, index_of(z - d, y, core)))


    barrier = pltpu.get_barrier_semaphore()

    def greet(peer):
        pl.semaphore_signal(
            barrier, inc=1, device_id={"row": peer}, device_id_type=pl.DeviceIdType.MESH
        )

    greet(partner)
    greet(across)
    beside = [(z >= 1, index_of(z - 1, y, core)), (z + 1 < depth, index_of(z + 1, y, core))]
    for there, peer in beside:
        pl.when(there)(lambda peer=peer: greet(peer))
    far = me - 1 + 2 * core
    has_far = (far >= 0) & (far < n)
    pl.when(has_far)(lambda: greet(far))

    shifted[...] = jnp.zeros_like(shifted)
    columns[...] = jnp.zeros_like(columns)
    near[...] = jnp.zeros_like(near)

    @pl.when(me == 0)
    def _():
        lo[...] = jnp.zeros_like(lo)
        from_low[...] = jnp.zeros_like(from_low)

    @pl.when(me == last)
    def _():
        up[...] = jnp.zeros_like(up)
        from_high[...] = jnp.zeros_like(from_high)

    need(pos, noise, single, wcoord, token)
    live = jnp.clip(counts_s[0], cap // 2, cap)
    noisy = pos[...] + noise_level * noise[...]
    columns[0:3, :] = input_scale * noisy
    relative = token[...].reshape(1, cap) - (me - 1) * rows
    turned = columns[...].T
    wc = wcoord[...]
    atom_start = single[...].astype(F32) + (
        turned[:, 0:1] * wc[0:1, :] + turned[:, 1:2] * wc[1:2, :] + turned[:, 2:3] * wc[2:3, :]
    )
    normed = normalize(atom_start)
    hs[...] = normed
    mid[...] = atom_start
    head[...] = normed[:AHEAD].astype(BF16)
    tail[...] = hs[pl.ds(live - BEHIND, BEHIND), :].astype(BF16)

    links = jnp.where(z >= 1, 1, 0) + jnp.where(z + 1 < depth, 1, 0) + 1
    peers = 1 + links + jnp.where(has_far, 1, 0)
    pl.semaphore_wait(barrier, peers)

    def edge(stage, way, src, dst, peer):
        return pltpu.make_async_remote_copy(
            src_ref=src,
            dst_ref=dst,
            send_sem=local_sem.at[2 + way],
            recv_sem=edge_recv.at[2 * (stage % 2) + way],
            device_id={"row": peer},
            device_id_type=pl.DeviceIdType.MESH,
        )

    def exchange(stage, src_up, dst_up, src_down, dst_down):
        going_up = edge(stage, 0, src_up, dst_up, me + 1)
        going_down = edge(stage, 1, src_down, dst_down, me - 1)
        pl.when(has_high)(going_up.start)
        pl.when(has_low)(going_down.start)

        def receive_low():
            pl.when(has_low)(going_up.wait_recv)

        def receive_high():
            pl.when(has_high)(going_down.wait_recv)

        def finish():
            pl.when(has_high)(going_up.wait_send)
            pl.when(has_low)(going_down.wait_send)

        return receive_low, receive_high, finish

    rim_low, rim_high, finish_rim = exchange(0, tail, lo, head, up)

    def tell(step):
        def one(peer):
            pl.semaphore_signal(
                ready.at[step], inc=1, device_id={"row": peer}, device_id_type=pl.DeviceIdType.MESH
            )

        one(across)
        for there, peer in beside:
            pl.when(there)(lambda peer=peer: one(peer))

    def hear(step):
        pl.semaphore_wait(ready.at[step], links)

    rounds = max(depth - 2, 0)
    if rounds:
        tell(0)
    need(waqkv)
    hw = ca // AH
    normed_b = normed.astype(BF16)
    own = mm(normed_b, waqkv[...])
    queries[...] = (own[:, :ca] * (1.0 / hw**0.5)).astype(BF16)
    head_lanes = [lanes_between(ca, h * hw, (h + 1) * hw) for h in range(AH)]
    keys_s[BEHIND : BEHIND + cap, :] = own[:, ca : 2 * ca]
    values_s[BEHIND : BEHIND + cap, :] = own[:, 2 * ca :]
    need(abias, offsets_s, waout, wagg)

    top = jnp.where(has_high, BEHIND + live + AHEAD, BEHIND + live)
    bottom = jnp.where(has_low, 0, BEHIND)
    lane_key = lax.broadcasted_iota(jnp.int32, (1, KWIN), 1)
    ones = jnp.ones((KWIN, ca), BF16)

    def attend(windows):
        at = [BEHIND + QWIN * w + offsets_s[w] for w in windows]
        scores = []
        for w, start in zip(windows, at):
            key = keys_s[pl.ds(start, KWIN), :].astype(BF16)
            q = queries[w * QWIN : (w + 1) * QWIN, :]
            wide = jnp.concatenate([q * m.astype(BF16) for m in head_lanes], axis=0)
            scores.append(mm_t(wide, key))
        exps = []
        for w, start, score in zip(windows, at, scores):
            score = score + abias[:, w * QWIN : (w + 1) * QWIN, :].reshape(AH * QWIN, KWIN)
            keys = lane_key + start
            score = jnp.where((keys >= bottom) & (keys < top), score, masked_score)
            exps.append(jnp.exp(score - jnp.max(score, axis=-1, keepdims=True)).astype(BF16))
        outs = []
        for start, e in zip(at, exps):
            value = values_s[pl.ds(start, KWIN), :].astype(BF16)
            outs.append(mm(e, jnp.concatenate([value, ones], axis=1)))
        for w, out in zip(windows, outs):
            mixed = out[:QWIN] * wide_lanes[0]
            for h in range(1, AH):
                mixed = mixed + out[h * QWIN : (h + 1) * QWIN] * wide_lanes[h]
            att_s[w * QWIN : (w + 1) * QWIN, :] = (mixed[:, :ca] / mixed[:, ca:]).astype(BF16)

    wide_lanes = [jnp.concatenate([m, m], axis=1) for m in head_lanes]
    half = cap // 2
    count = cap // QWIN
    behind_windows = BEHIND // QWIN
    inner = [w for w in range(count) if w >= behind_windows and QWIN * w + AHEAD <= half]
    below = range(behind_windows)
    above = range(inner[-1] + 1, count)
    first = BEHIND + half
    span = half + AHEAD
    slot_lane = lax.broadcasted_iota(jnp.int32, (1, cap), 1)
    living = slot_lane < live
    sub_ids = lax.broadcasted_iota(jnp.int32, (3 * rows, cap), 0)
    hot = ((sub_ids == relative) & living).astype(F32)
    counted = jnp.sum(hot, axis=-1, keepdims=True)
    hot_s[...] = hot.astype(BF16)
    few = jnp.minimum(counted, 256.0)
    lane_c = lax.broadcasted_iota(jnp.int32, (3 * rows, 128), 1)
    count_wide = jnp.where(lane_c < 64, few, counted - few)
    down = slice(rows - margin, rows)
    ahead = slice(2 * rows, 2 * rows + rim_rows)
    part_down[:, ct:] = count_wide[down].astype(BF16)
    part_up[:, ct:] = count_wide[ahead].astype(BF16)
    attend(inner)
    if rounds > 1:
        hear(0)
        tell(1)

    def with_low():
        rim_low()
        low_kv = mm(lo[...], waqkv[:, ca:])
        keys_s[:BEHIND, :] = low_kv[:, :ca]
        values_s[:BEHIND, :] = low_kv[:, ca:]
        attend(below)

    def with_high():
        rim_high()
        shifted[half : half + AHEAD, :] = up[...].astype(F32)
        moved = shifted[pl.ds(cap - live, span), :]
        row_ids = lax.broadcasted_iota(jnp.int32, (half, ca), 0) + first
        merged = jnp.where(row_ids < BEHIND + live, hs[half:cap, :], moved[:half])
        high_rows = jnp.concatenate([merged, moved[half:]], axis=0).astype(BF16)
        high_kv = mm(high_rows, waqkv[:, ca:])
        keys_s[first:, :] = high_kv[:, :ca]
        values_s[first:, :] = high_kv[:, ca:]
        for k in range(0, len(above), GROUP):
            attend(above[k : k + GROUP])

    pl.when(core == 0)(with_high)
    if rounds > 2:
        hear(1)
        tell(2)
    with_low()
    pl.when(core == 1)(with_high)
    finish_rim()
    atom_mid = mid[...] + mm(att_s[...], waout[...])
    mid[...] = atom_mid
    spread = jnp.maximum(mm(atom_mid.astype(BF16), wagg[...]), 0.0).astype(BF16)
    partial = mm(hot_s[...], spread)
    part_down[:, :ct] = partial[down].astype(BF16)
    part_up[:, :ct] = partial[ahead].astype(BF16)
    part_low, part_high, finish_part = exchange(1, part_up, from_low, part_down, from_high)

    need(tsingle)
    own_sum = partial[rows : 2 * rows]
    own_count = counted[rows : 2 * rows]
    middle = slice(margin, rows - margin)
    token_mid = tsingle[middle, :].astype(F32) + own_sum[middle] / jnp.maximum(own_count[middle], 1.0)
    early_all[pl.ds(me, 1)] = normalize(token_mid).astype(BF16)[None]

    messages = (early_all, late_all)

    def block(kind, src, peer, arrived, count=None):
        view = messages[kind].at[src if count is None else pl.ds(0, count)]
        return pltpu.make_async_remote_copy(
            src_ref=view,
            dst_ref=view,
            send_sem=local_sem.at[kind],
            recv_sem=arrived,
            device_id={"row": peer},
            device_id_type=pl.DeviceIdType.MESH,
        )

    def relay(kind, src):
        block(kind, src, across, cross_late.at[src // 4] if kind else cross_early.at[0]).start()
        block(kind, src, partner, pair_recv.at[0, kind]).start()

    def own_sends(kind):
        for there, peer in line[::-1] if kind else line:
            pl.when(there)(lambda peer=peer: block(kind, me, peer, line_recv.at[z, kind]).start())
        relay(kind, me)

    for step in range(max(min(rounds - 1, 2), 0), rounds):
        hear(step)
        if step + 1 < rounds:
            tell(step + 1)
    own_sends(0)

    need(pmask, tbias)
    pair = 2 * rows
    allowed = pmask[...] == 1
    front = lax.broadcasted_iota(jnp.int32, (1, 2 * pair), 1) < pair
    for h in range(TH):
        masked = jnp.where(allowed, tbias[h], masked_score)
        for k in range(depth // 2):
            one = masked[:, 4 * k * pair : (4 * k + 2) * pair]
            two = masked[:, (4 * k + 2) * pair : (4 * k + 4) * pair]
            here = slice(2 * k * pair, (2 * k + 2) * pair)
            bias_half[0, h, :, here] = jnp.where(front, one, pltpu.roll(two, pair, 1))
            bias_half[1, h, :, here] = jnp.where(front, pltpu.roll(one, pair, 1), two)
    mid_t = mid[...].T
    need(wtqkv, wgate, wtout, wback, wpos)
    joint = mm(wtout[...], wback[...]).astype(BF16)
    part_low()
    part_high()
    low = from_low[...].astype(F32)
    high = from_high[...].astype(F32)

    def counts_in(sums):
        return sums[:, ct : ct + 1] + sums[:, ct + 64 : ct + 65]

    def edges(own, below, above):
        return jnp.concatenate(
            [own[:rim_rows] + below, own[rim_rows : rows - margin], own[rows - margin :] + above], axis=0
        )

    token_sum = edges(own_sum, low[:, :ct], high[:, :ct])
    token_count = edges(own_count, counts_in(low), counts_in(high))
    token_in = tsingle[...].astype(F32) + token_sum / jnp.maximum(token_count, 1.0)
    u_wide = normalize(token_in)
    u = u_wide.astype(BF16)
    chunks = ct // 128
    odd = [u_wide[margin : margin + 1, 128 * k : 128 * (k + 1)] for k in range(chunks)]
    odd.append(jnp.zeros((rim_rows - chunks, 128), F32))
    late = jnp.concatenate(
        [
            jnp.concatenate([u_wide[rows - margin :], u_wide[:margin]], axis=0),
            jnp.concatenate(odd, axis=0),
        ],
        axis=1,
    )
    late_all[pl.ds(me, 1)] = late.astype(BF16)[None]
    own_sends(1)

    direct = []
    for d in range(1, depth):
        direct.append((z >= d, z - d))
        direct.append((z + d < depth, z + d))

    def arrive(kind, some):
        for there, zz in some:
            src = index_of(zz, y, core)

            @pl.when(there)
            def _(src=src, zz=zz):
                block(kind, src, partner, line_recv.at[zz, kind]).wait_recv()
                relay(kind, src)

    def crossed_late(there, zz):
        src = index_of(zz, 1 - y, core)

        @pl.when(there)
        def _():
            block(1, src, partner, cross_late.at[zz]).wait_recv()
            block(1, src, partner, pair_recv.at[1, 1]).start()

    def crossed_early():
        block(0, 0, across, cross_early.at[0], depth).wait_recv()
        for zz in range(depth):
            block(0, index_of(zz, 1 - y, core), partner, pair_recv.at[1, 0]).start()

    def last_hops(side):
        for kind in range(2):
            block(kind, 0, partner, pair_recv.at[side, kind], depth).wait_recv()

    first_row = lax.broadcasted_iota(jnp.int32, (margin, ct), 0) == 0

    def assemble(side, column):
        for zz in range(depth):
            for cc in range(2):
                src = index_of(zz, column, cc)
                at = (2 * zz + cc) * rows
                early_rows = early_all[src]
                late_rows = late_all[src]
                u_half[side, at : at + margin, :] = late_rows[margin:, :ct]
                u_half[side, at + rows - margin : at + rows, :] = late_rows[:margin, :ct]
                extra = late_rows[:, ct:].astype(F32)
                row = jnp.concatenate([extra[k : k + 1] for k in range(chunks)], axis=1)
                tile = early_rows[:margin].astype(F32)
                u_half[side, at + margin : at + 2 * margin, :] = jnp.where(first_row, row, tile).astype(BF16)
                u_half[side, at + 2 * margin : at + rows - margin, :] = early_rows[margin:]

    arrive(0, direct[:2])
    tw = ct // TH
    tquery = (mm(u, wtqkv[:, :ct]) * (1.0 / tw**0.5)).astype(BF16)
    batches = []
    for first_head in range(0, TH, BATCH):
        heads = range(first_head, first_head + BATCH)
        left = first_head * tw // 128 * 128
        right = -(-(first_head + BATCH) * tw // 128) * 128
        lanes = [lanes_between(right - left, h * tw - left, (h + 1) * tw - left) for h in heads]
        q = tquery[:, left:right]
        wide = jnp.concatenate([q * m.astype(BF16) for m in lanes], axis=0)
        through = mm_t(wide, wtqkv[:, ct + left : ct + right]).astype(BF16)
        batches.append((first_head, left, right, lanes, through))
    gate = jax.nn.sigmoid(mm(u, wgate[...]))
    back_in = mm(token_in.astype(BF16), wback[...])
    arrive(0, direct[2:])
    arrive(1, direct)
    crossed_late(True, z)
    last_hops(0)
    assemble(0, y)

    def scored(features, column, some):
        bias = bias_half[column]
        scores = []
        for first_head, _, _, _, through in some:
            score = mm_t(through, features)
            scores.append(score + bias[first_head : first_head + BATCH].reshape(score.shape))
        return scores

    def valued(e, features, left, right):
        mixed = mm(e.astype(BF16), features).astype(BF16)
        return mm(mixed, wtqkv[:, 2 * ct + left : 2 * ct + right])

    features = u_half[0]
    own_max = []
    own_total = []
    own_out = []
    scores = scored(features, y, batches)
    for score in scores:
        own_max.append(jnp.max(score, axis=-1, keepdims=True))
    exps = [jnp.exp(score - m) for score, m in zip(scores, own_max)]
    for (_, left, right, _, _), e in zip(batches, exps):
        own_total.append(jnp.sum(e, axis=-1, keepdims=True))
        own_out.append(valued(e, features, left, right))
    for d in range(1, depth):
        crossed_late(z >= d, z - d)
        crossed_late(z + d < depth, z + d)
    crossed_early()
    last_hops(1)
    assemble(1, 1 - y)
    features = u_half[1]
    scores = scored(features, 1 - y, batches)
    all_max = [jnp.maximum(m, jnp.max(score, axis=-1, keepdims=True)) for score, m in zip(scores, own_max)]
    exps = [jnp.exp(score - m) for score, m in zip(scores, all_max)]
    outs = [valued(e, features, left, right) for e, (_, left, right, _, _) in zip(exps, batches)]
    blocks = [None] * chunks
    for k, (_, left, right, lanes, _) in enumerate(batches):
        scale = jnp.exp(own_max[k] - all_max[k])
        share = 1.0 / (own_total[k] * scale + jnp.sum(exps[k], axis=-1, keepdims=True))
        out = own_out[k] * (scale * share) + outs[k] * share
        total = out[:rows] * lanes[0]
        for h in range(1, BATCH):
            total = total + out[h * rows : (h + 1) * rows] * lanes[h]
        for c in range(left // 128, right // 128):
            part = total[:, 128 * c - left : 128 * (c + 1) - left]
            blocks[c] = part if blocks[c] is None else blocks[c] + part
    gated = (gate * jnp.concatenate(blocks, axis=1)).astype(BF16)
    near[rows : 2 * rows, :] = (back_in + mm(gated, joint)).astype(BF16)
    upper = near.at[2 * rows - margin : 2 * rows]
    lower = near.at[rows : rows + rim_rows]
    finish_part()
    back_low, back_high, finish_back = exchange(
        2, upper, near.at[rows - margin : rows], lower, near.at[2 * rows : 2 * rows + rim_rows]
    )
    tout_ref[...] = (token_in + mm(gated, wtout[...])).astype(BF16)
    for kind in range(2):
        block(kind, 0, partner, pair_recv.at[0, kind], n - 1).wait_send()
    back_low()
    back_high()
    back_t = lax.dot_general(near[...], hot_s[...], (((0,), (0,)), ((), ())), preferred_element_type=F32)
    atom_last = mid_t + back_t
    center = atom_last - jnp.mean(atom_last, axis=0, keepdims=True)
    width = jnp.mean(center * center, axis=0, keepdims=True)
    final = (center * lax.rsqrt(width + 1e-05)).astype(BF16)
    update = mm(wpos[...], final)
    den_ref[...] = jnp.where(living, skip_scale * noisy + output_scale * update, 0.0)
    finish_back()


def store(den, tout, den_h, tout_h, sem):
    copies = [pltpu.make_async_copy(den, den_h, sem.at[0]), pltpu.make_async_copy(tout, tout_h, sem.at[1])]
    for c in copies:
        c.start()
    for c in copies:
        c.wait()


def on_device(
    positions, noise, atom_single, atom_token, atom_counts, window_offsets, atom_bias,
    token_single, token_bias, pair_mask, w_coord, w_atom_qkv, w_atom_out, w_agg,
    w_tok_qkv, w_tok_gate, w_tok_out, w_back, w_pos,
):
    n = lax.axis_size("row")
    cap, ca = atom_single.shape
    rows, ct = token_single.shape
    big = (
        positions, noise, atom_single, atom_token, atom_bias, token_single,
        token_bias, pair_mask, w_coord, w_atom_qkv, w_atom_out, w_agg, w_tok_qkv, w_tok_gate,
        w_tok_out, w_back, w_pos,
    )
    margin = rows // 4
    send_up, send_down = (2 * margin, ct + 128), (margin, ct + 128)
    hbm = pl.BlockSpec(memory_space=pltpu.HBM)
    vmem = pl.BlockSpec(memory_space=pltpu.VMEM)
    out_shapes = (((positions.shape[0], cap), F32), ((rows, ct), BF16))
    results = pl.pallas_call(
        lambda *refs: kernel(n, *refs),
        out_shape=tuple(pltpu.VMEM(shape, kind) for shape, kind in out_shapes),
        in_specs=[pl.BlockSpec(memory_space=pltpu.SMEM)] + [hbm] * (1 + len(big)),
        out_specs=(vmem, vmem),
        scratch_shapes=[pltpu.SMEM(window_offsets.shape, jnp.int32)]
        + [pltpu.VMEM(a.shape, a.dtype) for a in big]
        + [
            pltpu.VMEM((128, cap), F32),
            pltpu.VMEM((cap, ca), F32),
            pltpu.VMEM((BEHIND, ca), BF16),
            pltpu.VMEM((AHEAD, ca), BF16),
            pltpu.VMEM((BEHIND, ca), BF16),
            pltpu.VMEM((AHEAD, ca), BF16),
            pltpu.VMEM((cap + AHEAD, ca), F32),
            pltpu.VMEM((cap, ca), BF16),
            pltpu.VMEM((BEHIND + cap + AHEAD, ca), F32),
            pltpu.VMEM((BEHIND + cap + AHEAD, ca), F32),
            pltpu.VMEM((cap, ca), F32),
            pltpu.VMEM((cap, ca), BF16),
            pltpu.VMEM(send_down, BF16),
            pltpu.VMEM(send_up, BF16),
            pltpu.VMEM(send_up, BF16),
            pltpu.VMEM(send_down, BF16),
            pltpu.VMEM((n, rows - 2 * margin, ct), BF16),
            pltpu.VMEM((n, 2 * margin, ct + 128), BF16),
            pltpu.VMEM((2, n * rows // 2, ct), BF16),
            pltpu.VMEM((2, TH, rows, n * rows // 2), F32),
            pltpu.VMEM((3 * rows, cap), BF16),
            pltpu.VMEM((3 * rows, ca), BF16),
            pltpu.SemaphoreType.DMA((1 + len(big),)),
            pltpu.SemaphoreType.DMA((4,)),
            pltpu.SemaphoreType.DMA((n // 4, 2)),
            pltpu.SemaphoreType.DMA((1,)),
            pltpu.SemaphoreType.DMA((n // 4,)),
            pltpu.SemaphoreType.DMA((2, 2)),
            pltpu.SemaphoreType.REGULAR((max(n // 4 - 2, 1),)),
        ],
        compiler_params=pltpu.CompilerParams(collective_id=0, has_side_effects=True, vmem_limit_bytes=VMEM_LIMIT),
    )(atom_counts, *(pltpu.with_memory_space_constraint(a, pltpu.HBM) for a in (window_offsets,) + big))
    results = tuple(pltpu.with_memory_space_constraint(a, pltpu.VMEM) for a in results)
    return pl.pallas_call(
        store,
        out_shape=tuple(jax.ShapeDtypeStruct(shape, kind) for shape, kind in out_shapes),
        in_specs=[vmem, vmem],
        out_specs=(hbm, hbm),
        scratch_shapes=[pltpu.SemaphoreType.DMA((2,))],
    )(*results)


def solution(mesh):
    placed = (
        P(None, ("grp", "row")),
        P(None, ("grp", "row")),
        P(("grp", "row"), None),
        P(("grp", "row")),
        P(("grp", "row")),
        P(("grp", "row")),
        P(None, ("grp", "row"), None),
        P(("grp", "row"), None),
        P(None, ("grp", "row"), None),
        P(("grp", "row"), None),
    ) + (P(),) * 9
    return jax.shard_map(
        on_device,
        mesh=mesh,
        in_specs=placed,
        out_specs=(P(None, ("grp", "row")), P(("grp", "row"), None)),
        check_vma=False,
    )
```

```python
import jax
import jax.numpy as jnp
from jax import lax
from jax.experimental import pallas as pl
from jax.experimental.pallas import tpu as pltpu
from jax.sharding import PartitionSpec as P

AH = 4
TH = 16
QWIN = 32
KWIN = 128
BEHIND = KWIN // 2
AHEAD = KWIN - QWIN

noise_level = 2.0
input_scale = 1.0 / 5.0**0.5
skip_scale = 1.0 / 5.0
output_scale = 2.0 / 5.0**0.5
masked_score = -1e30

F32 = jnp.float32
BF16 = jnp.bfloat16
GROUP = 8
BATCH = 4
VMEM_LIMIT = 40 * 1024 * 1024


def normalize(values):
    center = values - jnp.mean(values, axis=-1, keepdims=True)
    spread = jnp.mean(center * center, axis=-1, keepdims=True)
    return center * lax.rsqrt(spread + 1e-05)


def mm(a, b):
    return jnp.dot(a, b, preferred_element_type=F32)


def mm_t(a, b):
    return lax.dot_general(a, b, (((1,), (1,)), ((), ())), preferred_element_type=F32)


def lanes_between(width, low, high):
    lane = lax.broadcasted_iota(jnp.int32, (1, width), 1)
    return ((lane >= low) & (lane < high)).astype(F32)


def kernel(
    n,
    counts_s, offsets_h,
    pos_h, noise_h, single_h, token_h, abias_h, tsingle_h, tbias_h, mask_h,
    wcoord_h, waqkv_h, waout_h, wagg_h, wtqkv_h, wgate_h, wtout_h, wback_h, wpos_h,
    den_ref, tout_ref,
    offsets_s,
    pos, noise, single, token, abias, tsingle, tbias, pmask,
    wcoord, atom_w, token_w, wpos,
    columns, hs, tail, head, lo, up, shifted, queries, keys_s, values_s, mid, att_s,
    part_down, part_up, from_low, from_high, early_all, late_all, u_half, bias_half, hot_s, near,
    local_sem, edge_recv, line_recv, cross_early, cross_late, pair_recv, ready,
):
    cap, ca = single.shape
    rows, ct = tsingle.shape
    margin = rows // 4
    rim_rows = 2 * margin
    me = lax.axis_index("row")
    last = n - 1
    has_low = me > 0
    has_high = me < last

    ends_at = (3 * ca, 4 * ca, 4 * ca + ct)
    waqkv, waout, wagg = (atom_w.at[:, a:b] for a, b in zip((0,) + ends_at, ends_at))
    ends_at = (3 * ct, 4 * ct, 5 * ct, 5 * ct + ca)
    wtqkv, wgate, wtout, wback = (token_w.at[:, a:b] for a, b in zip((0,) + ends_at, ends_at))
    joined = [
        (atom_w, [(waqkv_h, waqkv), (waout_h, waout), (wagg_h, wagg)]),
        (token_w, [(wtqkv_h, wtqkv), (wgate_h, wgate), (wtout_h, wtout), (wback_h, wback)]),
    ]
    pairs = [
        (pos_h, pos), (noise_h, noise), (single_h, single), (wcoord_h, wcoord), (token_h, token),
        (abias_h, abias), (tsingle_h, tsingle),
        (mask_h, pmask), (tbias_h, tbias),
        (wpos_h, wpos), (offsets_h, offsets_s),
    ]
    copies = {}
    order = [(k, dst, [(src, dst)]) for k, (src, dst) in enumerate(pairs)]
    group = [(len(pairs) + k, whole, parts) for k, (whole, parts) in enumerate(joined)]
    for k, whole, parts in order[:5] + group[:1] + order[5:7] + group[1:] + order[7:]:
        for src, dst in parts:
            pltpu.make_async_copy(src, dst, local_sem.at[k]).start()
        copies[id(whole)] = pltpu.make_async_copy(whole, whole, local_sem.at[k])

    def need(*refs):
        for r in refs:
            copies[id(r)].wait()

    core = lax.rem(me, 2)
    y = lax.rem(me // 2, 2)
    z = me // 4
    depth = n // 4

    def index_of(zz, yy, cc):
        return zz * 4 + yy * 2 + cc

    partner = index_of(z, y, 1 - core)
    across = index_of(z, 1 - y, core)
    line = []
    for d in range(1, depth):
        line.append((z + d < depth, index_of(z + d, y, core)))
        line.append((z >= d, index_of(z - d, y, core)))


    barrier = pltpu.get_barrier_semaphore()

    def greet(peer):
        pl.semaphore_signal(
            barrier, inc=1, device_id={"row": peer}, device_id_type=pl.DeviceIdType.MESH
        )

    greet(partner)
    greet(across)
    beside = [(z >= 1, index_of(z - 1, y, core)), (z + 1 < depth, index_of(z + 1, y, core))]
    for there, peer in beside:
        pl.when(there)(lambda peer=peer: greet(peer))
    far = me - 1 + 2 * core
    has_far = (far >= 0) & (far < n)
    pl.when(has_far)(lambda: greet(far))

    shifted[...] = jnp.zeros_like(shifted)
    columns[...] = jnp.zeros_like(columns)
    near[...] = jnp.zeros_like(near)

    @pl.when(me == 0)
    def _():
        lo[...] = jnp.zeros_like(lo)
        from_low[...] = jnp.zeros_like(from_low)

    @pl.when(me == last)
    def _():
        up[...] = jnp.zeros_like(up)
        from_high[...] = jnp.zeros_like(from_high)

    need(pos, noise, single, wcoord, token)
    live = jnp.clip(counts_s[0], cap // 2, cap)
    noisy = pos[...] + noise_level * noise[...]
    columns[0:3, :] = input_scale * noisy
    relative = token[...].reshape(1, cap) - (me - 1) * rows
    turned = columns[...].T
    wc = wcoord[...]
    atom_start = single[...].astype(F32) + (
        turned[:, 0:1] * wc[0:1, :] + turned[:, 1:2] * wc[1:2, :] + turned[:, 2:3] * wc[2:3, :]
    )
    normed = normalize(atom_start)
    hs[...] = normed
    mid[...] = atom_start
    head[...] = normed[:AHEAD].astype(BF16)
    tail[...] = hs[pl.ds(live - BEHIND, BEHIND), :].astype(BF16)

    links = jnp.where(z >= 1, 1, 0) + jnp.where(z + 1 < depth, 1, 0) + 1
    peers = 1 + links + jnp.where(has_far, 1, 0)
    pl.semaphore_wait(barrier, peers)

    def edge(stage, way, src, dst, peer):
        return pltpu.make_async_remote_copy(
            src_ref=src,
            dst_ref=dst,
            send_sem=local_sem.at[2 + way],
            recv_sem=edge_recv.at[2 * (stage % 2) + way],
            device_id={"row": peer},
            device_id_type=pl.DeviceIdType.MESH,
        )

    def exchange(stage, src_up, dst_up, src_down, dst_down):
        going_up = edge(stage, 0, src_up, dst_up, me + 1)
        going_down = edge(stage, 1, src_down, dst_down, me - 1)
        pl.when(has_high)(going_up.start)
        pl.when(has_low)(going_down.start)

        def receive_low():
            pl.when(has_low)(going_up.wait_recv)

        def receive_high():
            pl.when(has_high)(going_down.wait_recv)

        def finish():
            pl.when(has_high)(going_up.wait_send)
            pl.when(has_low)(going_down.wait_send)

        return receive_low, receive_high, finish

    rim_low, rim_high, finish_rim = exchange(0, tail, lo, head, up)

    def tell(step):
        def one(peer):
            pl.semaphore_signal(
                ready.at[step], inc=1, device_id={"row": peer}, device_id_type=pl.DeviceIdType.MESH
            )

        one(across)
        for there, peer in beside:
            pl.when(there)(lambda peer=peer: one(peer))

    def hear(step):
        pl.semaphore_wait(ready.at[step], links)

    rounds = max(depth - 2, 0)
    if rounds:
        tell(0)
    need(atom_w)
    hw = ca // AH
    normed_b = normed.astype(BF16)
    own = mm(normed_b, waqkv[...])
    queries[...] = (own[:, :ca] * (1.0 / hw**0.5)).astype(BF16)
    head_lanes = [lanes_between(ca, h * hw, (h + 1) * hw) for h in range(AH)]
    keys_s[BEHIND : BEHIND + cap, :] = own[:, ca : 2 * ca]
    values_s[BEHIND : BEHIND + cap, :] = own[:, 2 * ca :]
    need(abias, offsets_s)

    top = jnp.where(has_high, BEHIND + live + AHEAD, BEHIND + live)
    bottom = jnp.where(has_low, 0, BEHIND)
    lane_key = lax.broadcasted_iota(jnp.int32, (1, KWIN), 1)
    ones = jnp.ones((KWIN, ca), BF16)

    def attend(windows):
        at = [BEHIND + QWIN * w + offsets_s[w] for w in windows]
        scores = []
        for w, start in zip(windows, at):
            key = keys_s[pl.ds(start, KWIN), :].astype(BF16)
            q = queries[w * QWIN : (w + 1) * QWIN, :]
            wide = jnp.concatenate([q * m.astype(BF16) for m in head_lanes], axis=0)
            scores.append(mm_t(wide, key))
        exps = []
        for w, start, score in zip(windows, at, scores):
            score = score + abias[:, w * QWIN : (w + 1) * QWIN, :].reshape(AH * QWIN, KWIN)
            keys = lane_key + start
            score = jnp.where((keys >= bottom) & (keys < top), score, masked_score)
            exps.append(jnp.exp(score - jnp.max(score, axis=-1, keepdims=True)).astype(BF16))
        outs = []
        for start, e in zip(at, exps):
            value = values_s[pl.ds(start, KWIN), :].astype(BF16)
            outs.append(mm(e, jnp.concatenate([value, ones], axis=1)))
        for w, out in zip(windows, outs):
            mixed = out[:QWIN] * wide_lanes[0]
            for h in range(1, AH):
                mixed = mixed + out[h * QWIN : (h + 1) * QWIN] * wide_lanes[h]
            att_s[w * QWIN : (w + 1) * QWIN, :] = (mixed[:, :ca] / mixed[:, ca:]).astype(BF16)

    wide_lanes = [jnp.concatenate([m, m], axis=1) for m in head_lanes]
    half = cap // 2
    count = cap // QWIN
    behind_windows = BEHIND // QWIN
    inner = [w for w in range(count) if w >= behind_windows and QWIN * w + AHEAD <= half]
    below = range(behind_windows)
    above = range(inner[-1] + 1, count)
    first = BEHIND + half
    span = half + AHEAD
    slot_lane = lax.broadcasted_iota(jnp.int32, (1, cap), 1)
    living = slot_lane < live
    sub_ids = lax.broadcasted_iota(jnp.int32, (3 * rows, cap), 0)
    hot = ((sub_ids == relative) & living).astype(F32)
    counted = jnp.sum(hot, axis=-1, keepdims=True)
    hot_s[...] = hot.astype(BF16)
    few = jnp.minimum(counted, 256.0)
    lane_c = lax.broadcasted_iota(jnp.int32, (3 * rows, 128), 1)
    count_wide = jnp.where(lane_c < 64, few, counted - few)
    down = slice(rows - margin, rows)
    ahead = slice(2 * rows, 2 * rows + rim_rows)
    part_down[:, ct:] = count_wide[down].astype(BF16)
    part_up[:, ct:] = count_wide[ahead].astype(BF16)
    attend(inner)
    if rounds > 1:
        hear(0)
        tell(1)

    def with_low():
        rim_low()
        low_kv = mm(lo[...], waqkv[:, ca:])
        keys_s[:BEHIND, :] = low_kv[:, :ca]
        values_s[:BEHIND, :] = low_kv[:, ca:]
        attend(below)

    def with_high():
        rim_high()
        shifted[half : half + AHEAD, :] = up[...].astype(F32)
        moved = shifted[pl.ds(cap - live, span), :]
        row_ids = lax.broadcasted_iota(jnp.int32, (half, ca), 0) + first
        merged = jnp.where(row_ids < BEHIND + live, hs[half:cap, :], moved[:half])
        high_rows = jnp.concatenate([merged, moved[half:]], axis=0).astype(BF16)
        high_kv = mm(high_rows, waqkv[:, ca:])
        keys_s[first:, :] = high_kv[:, :ca]
        values_s[first:, :] = high_kv[:, ca:]
        for k in range(0, len(above), GROUP):
            attend(above[k : k + GROUP])

    pl.when(core == 0)(with_high)
    if rounds > 2:
        hear(1)
        tell(2)
    with_low()
    pl.when(core == 1)(with_high)
    finish_rim()
    atom_mid = mid[...] + mm(att_s[...], waout[...])
    mid[...] = atom_mid
    spread = jnp.maximum(mm(atom_mid.astype(BF16), wagg[...]), 0.0).astype(BF16)
    partial = mm(hot_s[...], spread)
    part_down[:, :ct] = partial[down].astype(BF16)
    part_up[:, :ct] = partial[ahead].astype(BF16)
    part_low, part_high, finish_part = exchange(1, part_up, from_low, part_down, from_high)

    need(tsingle)
    own_sum = partial[rows : 2 * rows]
    own_count = counted[rows : 2 * rows]
    middle = slice(margin, rows - margin)
    token_mid = tsingle[middle, :].astype(F32) + own_sum[middle] / jnp.maximum(own_count[middle], 1.0)
    early_all[pl.ds(me, 1)] = normalize(token_mid).astype(BF16)[None]

    messages = (early_all, late_all)

    def block(kind, src, peer, arrived, count=None):
        view = messages[kind].at[src if count is None else pl.ds(0, count)]
        return pltpu.make_async_remote_copy(
            src_ref=view,
            dst_ref=view,
            send_sem=local_sem.at[kind],
            recv_sem=arrived,
            device_id={"row": peer},
            device_id_type=pl.DeviceIdType.MESH,
        )

    def relay(kind, src):
        block(kind, src, across, cross_late.at[src // 4] if kind else cross_early.at[0]).start()
        block(kind, src, partner, pair_recv.at[0, kind]).start()

    def own_sends(kind):
        for there, peer in line[::-1] if kind else line:
            pl.when(there)(lambda peer=peer: block(kind, me, peer, line_recv.at[z, kind]).start())
        relay(kind, me)

    for step in range(max(min(rounds - 1, 2), 0), rounds):
        hear(step)
        if step + 1 < rounds:
            tell(step + 1)
    own_sends(0)

    need(pmask, tbias)
    pair = 2 * rows
    allowed = pmask[...] == 1
    front = lax.broadcasted_iota(jnp.int32, (1, 2 * pair), 1) < pair
    for h in range(TH):
        masked = jnp.where(allowed, tbias[h], masked_score)
        for k in range(depth // 2):
            one = masked[:, 4 * k * pair : (4 * k + 2) * pair]
            two = masked[:, (4 * k + 2) * pair : (4 * k + 4) * pair]
            here = slice(2 * k * pair, (2 * k + 2) * pair)
            bias_half[0, h, :, here] = jnp.where(front, one, pltpu.roll(two, pair, 1))
            bias_half[1, h, :, here] = jnp.where(front, pltpu.roll(one, pair, 1), two)
    mid_t = mid[...].T
    need(token_w, wpos)
    joint = mm(wtout[...], wback[...]).astype(BF16)
    part_low()
    part_high()
    low = from_low[...].astype(F32)
    high = from_high[...].astype(F32)

    def counts_in(sums):
        return sums[:, ct : ct + 1] + sums[:, ct + 64 : ct + 65]

    def edges(own, below, above):
        return jnp.concatenate(
            [own[:rim_rows] + below, own[rim_rows : rows - margin], own[rows - margin :] + above], axis=0
        )

    token_sum = edges(own_sum, low[:, :ct], high[:, :ct])
    token_count = edges(own_count, counts_in(low), counts_in(high))
    token_in = tsingle[...].astype(F32) + token_sum / jnp.maximum(token_count, 1.0)
    u_wide = normalize(token_in)
    u = u_wide.astype(BF16)
    chunks = ct // 128
    odd = [u_wide[margin : margin + 1, 128 * k : 128 * (k + 1)] for k in range(chunks)]
    odd.append(jnp.zeros((rim_rows - chunks, 128), F32))
    late = jnp.concatenate(
        [
            jnp.concatenate([u_wide[rows - margin :], u_wide[:margin]], axis=0),
            jnp.concatenate(odd, axis=0),
        ],
        axis=1,
    )
    late_all[pl.ds(me, 1)] = late.astype(BF16)[None]
    own_sends(1)

    direct = []
    for d in range(1, depth):
        direct.append((z >= d, z - d))
        direct.append((z + d < depth, z + d))

    def arrive(kind, some):
        for there, zz in some:
            src = index_of(zz, y, core)

            @pl.when(there)
            def _(src=src, zz=zz):
                block(kind, src, partner, line_recv.at[zz, kind]).wait_recv()
                relay(kind, src)

    def crossed_late(there, zz):
        src = index_of(zz, 1 - y, core)

        @pl.when(there)
        def _():
            block(1, src, partner, cross_late.at[zz]).wait_recv()
            block(1, src, partner, pair_recv.at[1, 1]).start()

    def crossed_early():
        block(0, 0, across, cross_early.at[0], depth).wait_recv()
        for zz in range(depth):
            block(0, index_of(zz, 1 - y, core), partner, pair_recv.at[1, 0]).start()

    def last_hops(side):
        for kind in range(2):
            block(kind, 0, partner, pair_recv.at[side, kind], depth).wait_recv()

    first_row = lax.broadcasted_iota(jnp.int32, (margin, ct), 0) == 0

    def assemble(side, column):
        for zz in range(depth):
            for cc in range(2):
                src = index_of(zz, column, cc)
                at = (2 * zz + cc) * rows
                early_rows = early_all[src]
                late_rows = late_all[src]
                u_half[side, at : at + margin, :] = late_rows[margin:, :ct]
                u_half[side, at + rows - margin : at + rows, :] = late_rows[:margin, :ct]
                extra = late_rows[:, ct:].astype(F32)
                row = jnp.concatenate([extra[k : k + 1] for k in range(chunks)], axis=1)
                tile = early_rows[:margin].astype(F32)
                u_half[side, at + margin : at + 2 * margin, :] = jnp.where(first_row, row, tile).astype(BF16)
                u_half[side, at + 2 * margin : at + rows - margin, :] = early_rows[margin:]

    arrive(0, direct[:2])
    tw = ct // TH
    tquery = (mm(u, wtqkv[:, :ct]) * (1.0 / tw**0.5)).astype(BF16)
    batches = []
    for first_head in range(0, TH, BATCH):
        heads = range(first_head, first_head + BATCH)
        left = first_head * tw // 128 * 128
        right = -(-(first_head + BATCH) * tw // 128) * 128
        lanes = [lanes_between(right - left, h * tw - left, (h + 1) * tw - left) for h in heads]
        q = tquery[:, left:right]
        wide = jnp.concatenate([q * m.astype(BF16) for m in lanes], axis=0)
        through = mm_t(wide, wtqkv[:, ct + left : ct + right]).astype(BF16)
        batches.append((first_head, left, right, lanes, through))
    gate = jax.nn.sigmoid(mm(u, wgate[...]))
    back_in = mm(token_in.astype(BF16), wback[...])
    arrive(0, direct[2:])
    arrive(1, direct)
    crossed_late(True, z)
    last_hops(0)
    assemble(0, y)

    def scored(features, column, some):
        bias = bias_half[column]
        scores = []
        for first_head, _, _, _, through in some:
            score = mm_t(through, features)
            scores.append(score + bias[first_head : first_head + BATCH].reshape(score.shape))
        return scores

    def valued(e, features, left, right):
        mixed = mm(e.astype(BF16), features).astype(BF16)
        return mm(mixed, wtqkv[:, 2 * ct + left : 2 * ct + right])

    features = u_half[0]
    own_max = []
    own_total = []
    own_out = []
    scores = scored(features, y, batches)
    for score in scores:
        own_max.append(jnp.max(score, axis=-1, keepdims=True))
    exps = [jnp.exp(score - m) for score, m in zip(scores, own_max)]
    for (_, left, right, _, _), e in zip(batches, exps):
        own_total.append(jnp.sum(e, axis=-1, keepdims=True))
        own_out.append(valued(e, features, left, right))
    for d in range(1, depth):
        crossed_late(z >= d, z - d)
        crossed_late(z + d < depth, z + d)
    crossed_early()
    last_hops(1)
    assemble(1, 1 - y)
    features = u_half[1]
    scores = scored(features, 1 - y, batches)
    all_max = [jnp.maximum(m, jnp.max(score, axis=-1, keepdims=True)) for score, m in zip(scores, own_max)]
    exps = [jnp.exp(score - m) for score, m in zip(scores, all_max)]
    outs = [valued(e, features, left, right) for e, (_, left, right, _, _) in zip(exps, batches)]
    blocks = [None] * chunks
    for k, (_, left, right, lanes, _) in enumerate(batches):
        scale = jnp.exp(own_max[k] - all_max[k])
        share = 1.0 / (own_total[k] * scale + jnp.sum(exps[k], axis=-1, keepdims=True))
        out = own_out[k] * (scale * share) + outs[k] * share
        total = out[:rows] * lanes[0]
        for h in range(1, BATCH):
            total = total + out[h * rows : (h + 1) * rows] * lanes[h]
        for c in range(left // 128, right // 128):
            part = total[:, 128 * c - left : 128 * (c + 1) - left]
            blocks[c] = part if blocks[c] is None else blocks[c] + part
    gated = (gate * jnp.concatenate(blocks, axis=1)).astype(BF16)
    near[rows : 2 * rows, :] = (back_in + mm(gated, joint)).astype(BF16)
    upper = near.at[2 * rows - margin : 2 * rows]
    lower = near.at[rows : rows + rim_rows]
    finish_part()
    back_low, back_high, finish_back = exchange(
        2, upper, near.at[rows - margin : rows], lower, near.at[2 * rows : 2 * rows + rim_rows]
    )
    tout_ref[...] = (token_in + mm(gated, wtout[...])).astype(BF16)
    for kind in range(2):
        block(kind, 0, partner, pair_recv.at[0, kind], n - 1).wait_send()
    back_low()
    back_high()
    back_t = lax.dot_general(near[...], hot_s[...], (((0,), (0,)), ((), ())), preferred_element_type=F32)
    atom_last = mid_t + back_t
    center = atom_last - jnp.mean(atom_last, axis=0, keepdims=True)
    width = jnp.mean(center * center, axis=0, keepdims=True)
    final = (center * lax.rsqrt(width + 1e-05)).astype(BF16)
    update = mm(wpos[...], final)
    den_ref[...] = jnp.where(living, skip_scale * noisy + output_scale * update, 0.0)
    finish_back()


def store(den, tout, den_h, tout_h, sem):
    copies = [pltpu.make_async_copy(den, den_h, sem.at[0]), pltpu.make_async_copy(tout, tout_h, sem.at[1])]
    for c in copies:
        c.start()
    for c in copies:
        c.wait()


def on_device(
    positions, noise, atom_single, atom_token, atom_counts, window_offsets, atom_bias,
    token_single, token_bias, pair_mask, w_coord, w_atom_qkv, w_atom_out, w_agg,
    w_tok_qkv, w_tok_gate, w_tok_out, w_back, w_pos,
):
    n = lax.axis_size("row")
    cap, ca = atom_single.shape
    rows, ct = token_single.shape
    big = (
        positions, noise, atom_single, atom_token, atom_bias, token_single,
        token_bias, pair_mask, w_coord, w_atom_qkv, w_atom_out, w_agg, w_tok_qkv, w_tok_gate,
        w_tok_out, w_back, w_pos,
    )
    margin = rows // 4
    send_up, send_down = (2 * margin, ct + 128), (margin, ct + 128)
    hbm = pl.BlockSpec(memory_space=pltpu.HBM)
    vmem = pl.BlockSpec(memory_space=pltpu.VMEM)
    out_shapes = (((positions.shape[0], cap), F32), ((rows, ct), BF16))
    results = pl.pallas_call(
        lambda *refs: kernel(n, *refs),
        out_shape=tuple(pltpu.VMEM(shape, kind) for shape, kind in out_shapes),
        in_specs=[pl.BlockSpec(memory_space=pltpu.SMEM)] + [hbm] * (1 + len(big)),
        out_specs=(vmem, vmem),
        scratch_shapes=[pltpu.SMEM(window_offsets.shape, jnp.int32)]
        + [pltpu.VMEM(a.shape, a.dtype) for a in big[:9]]
        + [pltpu.VMEM((ca, 4 * ca + ct), BF16), pltpu.VMEM((ct, 5 * ct + ca), BF16)]
        + [pltpu.VMEM(w_pos.shape, w_pos.dtype)]
        + [
            pltpu.VMEM((128, cap), F32),
            pltpu.VMEM((cap, ca), F32),
            pltpu.VMEM((BEHIND, ca), BF16),
            pltpu.VMEM((AHEAD, ca), BF16),
            pltpu.VMEM((BEHIND, ca), BF16),
            pltpu.VMEM((AHEAD, ca), BF16),
            pltpu.VMEM((cap + AHEAD, ca), F32),
            pltpu.VMEM((cap, ca), BF16),
            pltpu.VMEM((BEHIND + cap + AHEAD, ca), F32),
            pltpu.VMEM((BEHIND + cap + AHEAD, ca), F32),
            pltpu.VMEM((cap, ca), F32),
            pltpu.VMEM((cap, ca), BF16),
            pltpu.VMEM(send_down, BF16),
            pltpu.VMEM(send_up, BF16),
            pltpu.VMEM(send_up, BF16),
            pltpu.VMEM(send_down, BF16),
            pltpu.VMEM((n, rows - 2 * margin, ct), BF16),
            pltpu.VMEM((n, 2 * margin, ct + 128), BF16),
            pltpu.VMEM((2, n * rows // 2, ct), BF16),
            pltpu.VMEM((2, TH, rows, n * rows // 2), F32),
            pltpu.VMEM((3 * rows, cap), BF16),
            pltpu.VMEM((3 * rows, ca), BF16),
            pltpu.SemaphoreType.DMA((len(big) - 4,)),
            pltpu.SemaphoreType.DMA((4,)),
            pltpu.SemaphoreType.DMA((n // 4, 2)),
            pltpu.SemaphoreType.DMA((1,)),
            pltpu.SemaphoreType.DMA((n // 4,)),
            pltpu.SemaphoreType.DMA((2, 2)),
            pltpu.SemaphoreType.REGULAR((max(n // 4 - 2, 1),)),
        ],
        compiler_params=pltpu.CompilerParams(collective_id=0, has_side_effects=True, vmem_limit_bytes=VMEM_LIMIT),
    )(atom_counts, *(pltpu.with_memory_space_constraint(a, pltpu.HBM) for a in (window_offsets,) + big))
    results = tuple(pltpu.with_memory_space_constraint(a, pltpu.VMEM) for a in results)
    return pl.pallas_call(
        store,
        out_shape=tuple(jax.ShapeDtypeStruct(shape, kind) for shape, kind in out_shapes),
        in_specs=[vmem, vmem],
        out_specs=(hbm, hbm),
        scratch_shapes=[pltpu.SemaphoreType.DMA((2,))],
    )(*results)


def solution(mesh):
    placed = (
        P(None, ("grp", "row")),
        P(None, ("grp", "row")),
        P(("grp", "row"), None),
        P(("grp", "row")),
        P(("grp", "row")),
        P(("grp", "row")),
        P(None, ("grp", "row"), None),
        P(("grp", "row"), None),
        P(None, ("grp", "row"), None),
        P(("grp", "row"), None),
    ) + (P(),) * 9
    return jax.shard_map(
        on_device,
        mesh=mesh,
        in_specs=placed,
        out_specs=(P(None, ("grp", "row")), P(("grp", "row"), None)),
        check_vma=False,
    )
```
